32 devices in a mesh: mem: 4 (over y, core), sub: 8 (over z, x).
Axes of the slice: x: 2, y: 2, z: 4, core: 2. Of those that a mesh axis runs over, the one named last changes fastest.
Arguments:
- prior_sample_array: float32 [80, 8, 24, 512], P('mem', 'sub'), may hold values from -6 to 6
- courant_x: float32 [8, 512], P('sub'), may hold values from -0.3 to 0.3
- courant_y: float32 [8, 512], P('sub'), may hold values from -0.3 to 0.3
- diffusion: float32 [8, 512], P('sub'), may hold values from 0.02 to 0.09
- obs_cell: int32 [4, 128], replicated, may hold values from 0 to 4095
- obs_value: float32 [4, 128], replicated, may hold values from -6 to 6
- obs_error: float32 [4, 128], replicated, may hold values from 0.2 to 1
- obs_weight: float32 [4, 128, 24], replicated, may hold values from -1.25 to 1.25
- taper_radius: float32 [4, 128], replicated, may hold values from 64 to 256
Outputs:
- analysis: float32 [80, 8, 24, 512], P(None, 'sub', None, 'mem')
The draws below stay inside these ranges and needn't reach their ends.
All inputs are finite; a program needn't handle non-finite values.
Results may differ from the reference program's by a relative error of at most 0.0003.
Values sent between devices are 32-bit elements; how exact they have to be, the bound alone decides.
No kernel may reach another device: no remote copies, remote signals or barrier semaphores. Data moves between devices by JAX's collectives and lax.ppermute only.
A program may use at most 64 MiB of HBM per device.

```python
import math
import jax
import jax.numpy as jnp
from jax import lax

COMP = 24
MEMBERS = 80
NOBS = 128
BATCHES = 4
NY = 8
NX = 512


def place_ends(array, key, low, high):
    longest = array.shape.index(max(array.shape))
    spots = []
    for shift in (0, 1):
        where = [jax.random.randint(jax.random.fold_in(key, axis), (), 0, length) for axis, length in enumerate(array.shape)]
        where[longest] = (where[longest] + shift) % array.shape[longest]
        spots.append(tuple(where))
    return array.at[spots[0]].set(low).at[spots[1]].set(high)


def shard_levels(key, extent, pieces, least, top_value):
    def one(axis_at, parts):
        steps = jax.random.uniform(jax.random.fold_in(jax.random.fold_in(key, 6), axis_at), (parts,), jnp.float32, least / len(pieces), top_value / len(pieces))
        return jnp.repeat(jnp.exp(steps), extent[axis_at] // parts).reshape((-1,) + (1,) * (len(extent) - axis_at - 1))

    level = one(*pieces[0])
    for cut in pieces[1:]:
        level = level * one(*cut)
    return level


def normal_values(key, dims, spread, reach, pieces=(), kind=jnp.bfloat16):
    values = spread * jax.random.normal(key, dims, jnp.float32)
    if pieces:
        values = values * shard_levels(key, dims, pieces, -0.22, 0.18)
    return jnp.clip(values, -reach, reach).astype(kind)


def setup_inputs(seed: int = 0) -> dict:
    key_of = jax.random.split(jax.random.key(seed), 10)
    prior_sample_array = normal_values(key_of[0], (MEMBERS, NY, COMP, NX), 1.0, 6.0, ((0, 4), (1, 8)), jnp.float32)
    courant_x = jnp.clip(jax.random.uniform(key_of[1], (NY, NX), jnp.float32, -0.3, 0.3) * shard_levels(key_of[1], (NY, NX), ((0, 8),), -0.4, 0.0), -0.3, 0.3)
    courant_y = jnp.clip(jax.random.uniform(key_of[2], (NY, NX), jnp.float32, -0.3, 0.3) * shard_levels(key_of[2], (NY, NX), ((0, 8),), -0.4, 0.0), -0.3, 0.3)
    diffusion = jnp.clip(0.02 + 0.07000000402331352 * jax.random.uniform(key_of[3], (NY, NX), jnp.float32) ** shard_levels(key_of[3], (NY, NX), ((0, 8),), -0.2, 0.2), 0.02, 0.09)
    obs_cell = place_ends(jax.random.randint(key_of[4], (BATCHES, NOBS), 0, NY * NX), jax.random.fold_in(key_of[4], 1), 0, (NY * NX) - 1).astype(jnp.int32)
    obs_value = normal_values(key_of[5], (BATCHES, NOBS), 1.0, 6.0, (), jnp.float32)
    obs_error = jnp.clip(jnp.exp(jax.random.uniform(key_of[6], (BATCHES, NOBS), jnp.float32, math.log(0.2), math.log(1.0))), 0.2, 1.0)
    obs_weight = normal_values(key_of[7], (BATCHES, NOBS, COMP), COMP ** -0.5, 1.25, (), jnp.float32)
    taper_radius = jnp.clip(jnp.exp(jax.random.uniform(key_of[8], (BATCHES, NOBS), jnp.float32, math.log(64.0), math.log(256.0))), 64.0, 256.0)
    return dict(prior_sample_array=prior_sample_array, courant_x=courant_x, courant_y=courant_y, diffusion=diffusion, obs_cell=obs_cell, obs_value=obs_value, obs_error=obs_error, obs_weight=obs_weight, taper_radius=taper_radius)


highest = lax.Precision.HIGHEST

def gaspari(delta_row, delta_col, cutoff_radius, width):
    cyclic_shifted = (delta_col + width // 2) % width - width // 2
    row_dist = delta_row.astype(jnp.float32)
    col_dist = cyclic_shifted.astype(jnp.float32)
    ratio = jnp.sqrt(row_dist * row_dist + col_dist * col_dist) / cutoff_radius
    inner = (((-0.25 * ratio + 0.5) * ratio + 0.625) * ratio - 5.0 / 3.0) * ratio * ratio + 1.0
    bounded = jnp.maximum(ratio, 1.0)
    outer = ((((ratio / 12.0 - 0.5) * ratio + 0.625) * ratio + 5.0 / 3.0) * ratio - 5.0) * ratio + 4.0 - 2.0 / (3.0 * bounded)
    return jnp.where(ratio <= 1.0, inner, jnp.where(ratio < 2.0, outer, 0.0))

def carried_quantity(center, west_cells, east_cells, north_cells, southern_neighbours, flow_x, meridional_velocity, mixing):
    result = center - jnp.maximum(flow_x, 0.0) * (center - west_cells) - jnp.minimum(flow_x, 0.0) * (east_cells - center)
    result = result - jnp.maximum(meridional_velocity, 0.0) * (center - southern_neighbours) - jnp.minimum(meridional_velocity, 0.0) * (north_cells - center)
    return result + mixing * (east_cells + west_cells + north_cells + southern_neighbours - 4.0 * center)

def obs_factors(obs_prior, obs_value, obs_error):
    members = obs_prior.shape[1]
    average = lax.optimization_barrier(jnp.mean(obs_prior, axis=1))
    anomaly = obs_prior - average[:, None]
    covariance = jnp.dot(anomaly, anomaly.T, precision=highest) / (members - 1) + jnp.diag(obs_error)
    factor = jnp.linalg.cholesky(covariance)
    innovation = (obs_value - average)[:, None]
    midpoint_values = lax.linalg.triangular_solve(factor, innovation, left_side=True, lower=True)
    solved = lax.linalg.triangular_solve(factor, midpoint_values, left_side=True, lower=True, transpose_a=True)
    shifted = factor + jnp.diag(jnp.sqrt(obs_error))
    reduced = lax.linalg.triangular_solve(shifted, anomaly, left_side=True, lower=True)
    squared = lax.linalg.triangular_solve(factor, reduced, left_side=True, lower=True, transpose_a=True)
    return (anomaly, solved - squared)

def reference(prior_sample_array, courant_x, courant_y, diffusion, obs_cell, obs_value, obs_error, obs_weight, taper_radius):
    flow_x = courant_x[:, None, :]
    meridional_velocity = courant_y[:, None, :]
    mixing = diffusion[:, None, :]

    def realization_propagated(realization_grid):
        padded = jnp.pad(realization_grid, ((1, 1), (0, 0), (0, 0)))
        return carried_quantity(realization_grid, jnp.roll(realization_grid, 1, axis=2), jnp.roll(realization_grid, -1, axis=2), padded[2:], padded[:-2], flow_x, meridional_velocity, mixing)
    existing_grid_values = lax.map(realization_propagated, prior_sample_array)
    members = prior_sample_array.shape[0]
    columns = jnp.arange(NX, dtype=jnp.int32)
    for batch_index in range(BATCHES):
        obs_rows = obs_cell[batch_index] // NX
        obs_cols = obs_cell[batch_index] % NX
        picked = existing_grid_values[:, obs_rows, :, obs_cols]
        obs_prior = jnp.einsum('kmc,kc->km', picked, obs_weight[batch_index], precision=highest)
        obs_anomaly, coeffs = obs_factors(obs_prior, obs_value[batch_index], obs_error[batch_index])
        cutoff_radius = taper_radius[batch_index]

        def update_row(payload):
            row_state, row_index = payload
            average = lax.optimization_barrier(jnp.mean(row_state, axis=0))
            anomaly = row_state - average[None]
            cross_cov = jnp.einsum('mcx,km->cxk', anomaly, obs_anomaly, precision=highest) / (members - 1)
            weights = gaspari(row_index - obs_rows[None, :], columns[:, None] - obs_cols[None, :], cutoff_radius[None, :], NX)
            gain = cross_cov * weights[None]
            return row_state + jnp.einsum('cxk,km->mcx', gain, coeffs, precision=highest)
        updated = lax.map(update_row, (jnp.moveaxis(existing_grid_values, 1, 0), jnp.arange(NY, dtype=jnp.int32)))
        existing_grid_values = jnp.moveaxis(updated, 0, 1)
    return existing_grid_values
```

```python
import jax
import jax.numpy as jnp
from jax import lax
from jax.experimental import pallas as pl
from jax.experimental.pallas import tpu as pltpu
from jax.sharding import PartitionSpec as P

highest = lax.Precision.HIGHEST
f32 = jnp.float32
bf16 = jnp.bfloat16
TILE = (8, 128)


def dot(a, b, ca, cb, precision=highest):
    return lax.dot_general(
        a, b, (((ca,), (cb,)), ((), ())), precision=precision, preferred_element_type=f32
    )


def narrow(a, b, ca, cb):
    return dot(a, b, ca, cb, None)


def split2(x):
    hi = x.astype(bf16)
    return hi, (x - hi.astype(f32)).astype(bf16)


def split3(x):
    hi = x.astype(bf16)
    rest = x - hi.astype(f32)
    mid = rest.astype(bf16)
    return hi, mid, (rest - mid.astype(f32)).astype(bf16)


def call(kernel, out_shapes, name, operands, scalars=(), scratch=()):
    specs = [pl.BlockSpec(memory_space=pltpu.SMEM) for _ in scalars]
    specs += [pl.BlockSpec(memory_space=pltpu.VMEM) for _ in operands]
    return pl.pallas_call(
        kernel,
        in_specs=specs,
        out_specs=[pl.BlockSpec(memory_space=pltpu.VMEM) for _ in out_shapes],
        out_shape=[jax.ShapeDtypeStruct(s, f32) for s in out_shapes],
        scratch_shapes=list(scratch),
        compiler_params=pltpu.CompilerParams(vmem_limit_bytes=48 * 2**20),
        name=name,
    )(*scalars, *operands)


def rows_cols(cells, width):
    if width & (width - 1) == 0:
        shift = width.bit_length() - 1
        return cells >> shift, cells & (width - 1)
    return cells // width, cells % width


def to_columns(rows):
    n = rows.shape[0]
    return jnp.concatenate([rows, jnp.zeros((128 - n, 128), f32)], 0).T


def gaspari(delta_row, delta_col, cutoff_radius, width):
    half = width // 2
    folded = jnp.where(delta_col >= half, delta_col - width, delta_col)
    folded = jnp.where(delta_col < -half, delta_col + width, folded)
    ratio = jnp.sqrt(delta_row * delta_row + folded * folded) / cutoff_radius
    inner = (((-0.25 * ratio + 0.5) * ratio + 0.625) * ratio - 5.0 / 3.0) * ratio * ratio + 1.0
    bounded = jnp.maximum(ratio, 1.0)
    outer = (
        ((((ratio / 12.0 - 0.5) * ratio + 0.625) * ratio + 5.0 / 3.0) * ratio - 5.0) * ratio
        + 4.0
        - 2.0 / (3.0 * bounded)
    )
    return jnp.where(ratio <= 1.0, inner, jnp.where(ratio < 2.0, outer, 0.0))


def taper_kernel(width, batches, nobs, cols_dev):
    def kernel(place_ref, cell_ref, radius_ref, obs_taper_ref, cell_taper_ref):
        row_here = place_ref[0].astype(f32)
        col_here = place_ref[1] * cols_dev
        row_i, col_i = rows_cols(cell_ref[...], width)
        rows = row_i.astype(f32)
        cols = col_i.astype(f32)
        table = to_columns(jnp.concatenate([rows, cols, radius_ref[...]], 0))
        lane = lax.broadcasted_iota(jnp.int32, (1, cols_dev), 1)
        cell_cols = (lane + col_here).astype(f32)
        slot = 0
        for b in range(batches):
            row_j = table[:, b : b + 1]
            col_j = table[:, batches + b : batches + b + 1]
            radius = table[:, 2 * batches + b : 2 * batches + b + 1]
            cell_taper_ref[b] = gaspari(row_here - row_j, cell_cols - col_j, radius, width)
            for e in range(b + 1, batches):
                obs_taper_ref[slot] = gaspari(
                    rows[e : e + 1, :] - row_j, cols[e : e + 1, :] - col_j, radius, width
                )
                slot += 1

    return kernel


def observe_kernel(width, comps, batches, nobs, blocks, edge_rows):
    def kernel(q_ref, cx_ref, cy_ref, d_ref, cell_ref, weight_ref, own_ref, raw_ref, send_ref):
        q = q_ref[...]
        count = q.shape[0]
        cx, cy, d = cx_ref[...], cy_ref[...], d_ref[...]
        west = pltpu.roll(q, 1, 1)
        east = pltpu.roll(q, width - 1, 1)
        mine = q - jnp.maximum(cx, 0.0) * (q - west) - jnp.minimum(cx, 0.0) * (east - q)
        mine = mine - jnp.maximum(cy, 0.0) * q + jnp.minimum(cy, 0.0) * q
        mine = mine + d * (east + west - 4.0 * q)
        _, col = rows_cols(cell_ref[...], width)
        place = lax.broadcasted_iota(jnp.int32, (width, nobs), 0)
        pieces = split2(mine) + split2(q)
        stacked = jnp.concatenate(pieces, 0)
        for b in range(batches):
            pick = (place == col[b : b + 1, :]).astype(f32).astype(bf16)
            found = narrow(stacked, pick, 1, 0)
            w = jnp.concatenate(
                [weight_ref[b], jnp.zeros((nobs, 128 - comps), f32)], 1
            ).T[:comps]
            own = found[:count] + found[count : 2 * count]
            raw = found[2 * count : 3 * count] + found[3 * count :]
            at = slice(b * nobs, (b + 1) * nobs)
            own_ref[:, at] = jnp.sum(own.reshape(-1, comps, nobs) * w[None], axis=1)
            raw_ref[:, at] = jnp.sum(raw.reshape(-1, comps, nobs) * w[None], axis=1)
        cols_dev = width // blocks
        which = lax.broadcasted_iota(jnp.int32, (2 * blocks, width), 0)
        spot = lax.broadcasted_iota(jnp.int32, (2 * blocks, width), 1)
        start = (which >> 1) * cols_dev
        wanted = jnp.where(which & 1 == 0, start - 1, start + cols_dev)
        wanted = jnp.where(wanted < 0, wanted + width, wanted)
        wanted = jnp.where(wanted >= width, wanted - width, wanted)
        pick = (spot == wanted).astype(f32).astype(bf16)
        edges = sum(narrow(pick, part, 1, 1) for part in split3(q)[::-1])
        chunks = -(-count // 128)
        if chunks * 128 > count:
            edges = jnp.concatenate([edges, jnp.zeros((2 * blocks, chunks * 128 - count), f32)], 1)
        for i in range(blocks):
            at = slice(i * cols_dev, (i + 1) * cols_dev)
            send_ref[i, :count, :] = q[:, at]
            rows = [edges[2 * i : 2 * i + 2, j * 128 : (j + 1) * 128] for j in range(chunks)]
            if edge_rows > 2 * chunks:
                rows.append(jnp.zeros((edge_rows - 2 * chunks, 128), f32))
            send_ref[i, count:, :] = jnp.concatenate(rows, 0)

    return kernel


def join_kernel(width, batches, nobs):
    def kernel(place_ref, own_ref, raw_ref, above_ref, below_ref, cell_ref, out_ref):
        here = place_ref[0]
        row, col = rows_cols(cell_ref[...], width)
        place = lax.broadcasted_iota(jnp.int32, (width, nobs), 0)
        parts = split3(jnp.concatenate([above_ref[...], below_ref[...]], 0))
        stacked = jnp.concatenate([p.astype(f32) for p in parts] + [jnp.zeros((2, width), f32)], 0)
        stacked = stacked.astype(bf16)
        for b in range(batches):
            pick = (place == col[b : b + 1, :]).astype(f32).astype(bf16)
            found = narrow(stacked, pick, 1, 0)
            coef = found[0:2] + found[2:4] + found[4:6]
            r = row[b : b + 1, :]
            factor = jnp.where(r == here + 1, coef[0:1], jnp.where(r == here - 1, coef[1:2], 0.0))
            at = slice(b * nobs, (b + 1) * nobs)
            out_ref[:, at] = jnp.where(r == here, own_ref[:, at], factor * raw_ref[:, at])

    return kernel


def lane_spread(x, j):
    return jnp.take_along_axis(x, jnp.full(x.shape, j, jnp.int32), axis=1)


def row_spread(x, i):
    return jnp.broadcast_to(x[i : i + 1, :], x.shape)


def factored(cov, sides, error, members):
    tiles = cov.shape[0] // 8
    lane = lax.broadcasted_iota(jnp.int32, TILE, 1)
    sub = lax.broadcasted_iota(jnp.int32, TILE, 0)
    T = [cov[8 * q : 8 * q + 8, :] for q in range(tiles)]
    V = [sides[8 * q : 8 * q + 8, :] for q in range(tiles)]
    deviation = jnp.broadcast_to(jnp.sqrt(error), TILE)
    is_member = lane < members
    inverse, solved = [], []
    for p in range(tiles):
        block = (lane >= 8 * p) & (lane < 8 * p + 8)
        columns = [lane_spread(T[p], 8 * p + c) for c in range(8)]
        s = [[row_spread(columns[c], a) if a >= c else None for c in range(8)] for a in range(8)]
        joined = jnp.where(block, (lane - 8 * p == sub).astype(f32), T[p])
        R = [row_spread(joined, c) for c in range(8)]
        Z = [row_spread(V[p], c) for c in range(8)]
        rd, rs = [None] * 8, [None] * 8
        m = [[None] * 8 for _ in range(8)]
        for c in range(8):
            rd[c] = 1.0 / s[c][c]
            rs[c] = lax.rsqrt(s[c][c])
            root = s[c][c] * rs[c]
            spread = lane_spread(deviation, 8 * p + c)
            Z[c] = Z[c] * jnp.where(is_member, root / (root + spread), 1.0)
            for a in range(c + 1, 8):
                m[a][c] = s[a][c] * rd[c]
            for a in range(c + 1, 8):
                for e in range(c + 1, a + 1):
                    s[a][e] = s[a][e] - (s[a][c] * s[e][c]) * rd[c]
                R[a] = R[a] - m[a][c] * R[c]
                Z[a] = Z[a] - m[a][c] * Z[c]
        X, U = [None] * 8, [None] * 8
        for a in range(7, -1, -1):
            x, u = rd[a] * R[a], rd[a] * Z[a]
            for c in range(a + 1, 8):
                x = x - m[c][a] * X[c]
                u = u - m[c][a] * U[c]
            X[a], U[a] = x, u
        low, side = R[0] * rs[0], Z[0] * rs[0]
        for c in range(1, 8):
            low = jnp.where(sub == c, R[c] * rs[c], low)
            side = jnp.where(sub == c, Z[c] * rs[c], side)
        inverse.append(jnp.where(lane < 8 * p + 8, low, 0.0))
        solved.append(side)
        for q in range(p + 1, tiles):
            t, v = jnp.where(block, 0.0, T[q]), V[q]
            for c in range(8):
                column = lane_spread(T[q], 8 * p + c)
                t = t - column * X[c]
                v = v - column * U[c]
            T[q], V[q] = t, v
    return jnp.concatenate(inverse, 0), jnp.concatenate(solved, 0)


def coefficients(observed, value, error):
    members, nobs = observed.shape
    mean = jnp.sum(observed, axis=0, keepdims=True) / members
    anomaly = observed - mean
    row = lax.broadcasted_iota(jnp.int32, (nobs, nobs), 0)
    col = lax.broadcasted_iota(jnp.int32, (nobs, nobs), 1)
    cov = dot(anomaly, anomaly, 0, 0) / (members - 1) + jnp.where(row == col, error, 0.0)
    sides = jnp.concatenate(
        [anomaly, value - mean, jnp.zeros((nobs - members - 1, nobs), f32)], 0
    ).T
    inverse, solved = factored(cov, sides, error, members)
    back = dot(solved, inverse, 0, 0)
    return anomaly, back[members : members + 1] - back[:members]


def chain_kernel(batches, nobs):
    def kernel(y_ref, value_ref, error_ref, taper_ref, anomaly_ref, coeff_ref):
        members = y_ref.shape[0]
        Y = [y_ref[:, nobs * b : nobs * (b + 1)] for b in range(batches)]
        slot = 0
        for b in range(batches):
            anomaly, coeff = coefficients(Y[b], value_ref[b : b + 1, :], error_ref[b : b + 1, :])
            anomaly_ref[b] = anomaly
            coeff_ref[b] = coeff
            for e in range(b + 1, batches):
                spread = Y[e] - jnp.sum(Y[e], axis=0, keepdims=True) / members
                gain = dot(anomaly, spread, 0, 0) / (members - 1) * taper_ref[slot]
                Y[e] = Y[e] + dot(coeff, gain, 1, 0)
                slot += 1

    return kernel


def update_kernel(width, comps, batches, members, cols_dev, count, group):
    def kernel(
        place_ref, own_ref, north_ref, south_ref, cx_ref, cy_ref, d_ref,
        anomaly_ref, coeff_ref, taper_ref, out_ref, grid_ref,
    ):
        start = pl.multiple_of(place_ref[1] * cols_dev, cols_dev)
        cx = cx_ref[:, pl.ds(start, cols_dev)]
        cy = cy_ref[:, pl.ds(start, cols_dev)]
        d = d_ref[:, pl.ds(start, cols_dev)]
        lane = lax.broadcasted_iota(jnp.int32, (1, cols_dev), 1)
        for s in range(own_ref.shape[0]):
            outer = to_columns(own_ref[s, count:, :])
            for j in range(-(-count // 128)):
                size = min(128, count - 128 * j)
                at = slice(128 * j, 128 * j + size)
                q, north, south = own_ref[s, at, :], north_ref[s, at, :], south_ref[s, at, :]
                west = jnp.where(lane == 0, outer[:size, 2 * j : 2 * j + 1], pltpu.roll(q, 1, 1))
                east = jnp.where(
                    lane == cols_dev - 1,
                    outer[:size, 2 * j + 1 : 2 * j + 2],
                    pltpu.roll(q, cols_dev - 1, 1),
                )
                x = q - jnp.maximum(cx, 0.0) * (q - west) - jnp.minimum(cx, 0.0) * (east - q)
                x = x - jnp.maximum(cy, 0.0) * (q - south) - jnp.minimum(cy, 0.0) * (north - q)
                x = x + d * (east + west + north + south - 4.0 * q)
                grid_ref[pl.ds(s * count + 128 * j, size), :] = x
        left, right, tapers = [], [], []
        nobs = anomaly_ref.shape[2]
        fill = -3 * members % 128
        blank = jnp.zeros((fill, group * cols_dev), bf16)
        for b in range(batches):
            hi, lo = split2(anomaly_ref[b])
            left.append(jnp.concatenate([hi, lo, hi, jnp.zeros((fill, nobs), bf16)], 0))
            hi, lo = split2(coeff_ref[b])
            right.append(jnp.concatenate([hi, hi, lo], 1))
            tapers.append(jnp.tile(taper_ref[b] / (members - 1), (1, group)))
        for first in range(0, comps, group):
            x = jnp.concatenate(
                [grid_ref[pl.ds(first + i, members, comps), :] for i in range(group)], 1
            )
            for b in range(batches):
                spread = x - jnp.sum(x, axis=0, keepdims=True) / members
                hi, lo = split2(spread)
                gain = narrow(left[b], jnp.concatenate([hi, hi, lo, blank], 0), 0, 0) * tapers[b]
                hi, lo = split2(gain)
                x = x + narrow(right[b], jnp.concatenate([hi, lo, hi], 0), 1, 0)
            for i in range(group):
                out_ref[pl.ds(first + i, members, comps), :] = x[:, i * cols_dev : (i + 1) * cols_dev]

    return kernel


def summed(x, axis):
    size = lax.axis_size(axis)
    if size & (size - 1):
        return lax.psum(x, axis)
    step = 1
    while step < size:
        x = x + lax.ppermute(x, axis, [(i, i ^ step) for i in range(size)])
        step *= 2
    return x


def shards(
    prior_sample_array,
    courant_x,
    courant_y,
    diffusion,
    obs_cell,
    obs_value,
    obs_error,
    obs_weight,
    taper_radius,
):
    local, rows_dev, comps, width = prior_sample_array.shape
    blocks = lax.axis_size("mem")
    bands = lax.axis_size("sub")
    cols_dev = width // blocks
    members = local * blocks
    batches, nobs = obs_cell.shape
    count = local * comps
    edge_rows = -(-(2 * -(-count // 128)) // 8) * 8
    assert rows_dev == 1 and cols_dev == 128 and nobs == 128
    place = jnp.stack([lax.axis_index("sub"), lax.axis_index("mem")]).astype(jnp.int32)
    up = [(i, i + 1) for i in range(bands - 1)]
    down = [(i + 1, i) for i in range(bands - 1)]

    above = lax.ppermute(jnp.maximum(courant_y, 0.0) + diffusion, "sub", down)
    below = lax.ppermute(diffusion - jnp.minimum(courant_y, 0.0), "sub", up)
    own, raw, send = call(
        observe_kernel(width, comps, batches, nobs, blocks, edge_rows),
        [(local, batches * nobs)] * 2 + [(blocks, count + edge_rows, cols_dev)],
        "observe",
        (
            prior_sample_array.reshape(count, width),
            courant_x,
            courant_y,
            diffusion,
            obs_cell,
            obs_weight,
        ),
    )
    grid = lax.all_to_all(send, "mem", 0, 0)
    (partial,) = call(
        join_kernel(width, batches, nobs),
        [(local, batches * nobs)],
        "join",
        (own, raw, above, below, obs_cell),
        (place,),
    )
    observed = lax.all_gather(summed(partial, "sub"), "mem", tiled=True)
    north = lax.ppermute(grid, "sub", down)
    south = lax.ppermute(grid, "sub", up)
    obs_taper, cell_taper = call(
        taper_kernel(width, batches, nobs, cols_dev),
        [(batches * (batches - 1) // 2, nobs, nobs), (batches, nobs, cols_dev)],
        "tapers",
        (obs_cell, taper_radius),
        (place,),
    )
    anomaly, coeff = call(
        chain_kernel(batches, nobs),
        [(batches, members, nobs)] * 2,
        "chain",
        (observed, obs_value, obs_error, obs_taper),
    )
    (out,) = call(
        update_kernel(width, comps, batches, members, cols_dev, count, 4),
        [(members * comps, cols_dev)],
        "update",
        (grid, north, south, courant_x, courant_y, diffusion, anomaly, coeff, cell_taper),
        (place,),
        (pltpu.VMEM((members * comps, cols_dev), f32),),
    )
    return out.reshape(members, rows_dev, comps, cols_dev)


def solution(mesh):
    return jax.shard_map(
        shards,
        mesh=mesh,
        in_specs=(
            P("mem", "sub", None, None),
            P("sub", None),
            P("sub", None),
            P("sub", None),
            P(),
            P(),
            P(),
            P(),
            P(),
        ),
        out_specs=P(None, "sub", None, "mem"),
        check_vma=False,
    )
```

```python
import jax
import jax.numpy as jnp
from jax import lax
from jax.experimental import pallas as pl
from jax.experimental.pallas import tpu as pltpu
from jax.sharding import PartitionSpec as P

highest = lax.Precision.HIGHEST
f32 = jnp.float32
bf16 = jnp.bfloat16
TILE = (8, 128)


def dot(a, b, ca, cb, precision=highest):
    return lax.dot_general(
        a, b, (((ca,), (cb,)), ((), ())), precision=precision, preferred_element_type=f32
    )


def narrow(a, b, ca, cb):
    return dot(a, b, ca, cb, None)


def split2(x):
    hi = x.astype(bf16)
    return hi, (x - hi.astype(f32)).astype(bf16)


def split3(x):
    hi = x.astype(bf16)
    rest = x - hi.astype(f32)
    mid = rest.astype(bf16)
    return hi, mid, (rest - mid.astype(f32)).astype(bf16)


def call(kernel, out_shapes, name, operands, scalars=(), scratch=()):
    specs = [pl.BlockSpec(memory_space=pltpu.SMEM) for _ in scalars]
    specs += [pl.BlockSpec(memory_space=pltpu.VMEM) for _ in operands]
    return pl.pallas_call(
        kernel,
        in_specs=specs,
        out_specs=[pl.BlockSpec(memory_space=pltpu.VMEM) for _ in out_shapes],
        out_shape=[jax.ShapeDtypeStruct(s, f32) for s in out_shapes],
        scratch_shapes=list(scratch),
        compiler_params=pltpu.CompilerParams(vmem_limit_bytes=48 * 2**20),
        name=name,
    )(*scalars, *operands)


def rows_cols(cells, width):
    if width & (width - 1) == 0:
        shift = width.bit_length() - 1
        return cells >> shift, cells & (width - 1)
    return cells // width, cells % width


def to_columns(rows):
    n = rows.shape[0]
    return jnp.concatenate([rows, jnp.zeros((128 - n, 128), f32)], 0).T


def gaspari(delta_row, delta_col, cutoff_radius, width):
    half = width // 2
    folded = jnp.where(delta_col >= half, delta_col - width, delta_col)
    folded = jnp.where(delta_col < -half, delta_col + width, folded)
    ratio = jnp.sqrt(delta_row * delta_row + folded * folded) / cutoff_radius
    inner = (((-0.25 * ratio + 0.5) * ratio + 0.625) * ratio - 5.0 / 3.0) * ratio * ratio + 1.0
    bounded = jnp.maximum(ratio, 1.0)
    outer = (
        ((((ratio / 12.0 - 0.5) * ratio + 0.625) * ratio + 5.0 / 3.0) * ratio - 5.0) * ratio
        + 4.0
        - 2.0 / (3.0 * bounded)
    )
    return jnp.where(ratio <= 1.0, inner, jnp.where(ratio < 2.0, outer, 0.0))


def taper_kernel(width, batches, nobs, cols_dev):
    def kernel(place_ref, cell_ref, radius_ref, obs_taper_ref, cell_taper_ref):
        row_here = place_ref[0].astype(f32)
        col_here = place_ref[1] * cols_dev
        row_i, col_i = rows_cols(cell_ref[...], width)
        rows = row_i.astype(f32)
        cols = col_i.astype(f32)
        table = to_columns(jnp.concatenate([rows, cols, radius_ref[...]], 0))
        lane = lax.broadcasted_iota(jnp.int32, (1, cols_dev), 1)
        cell_cols = (lane + col_here).astype(f32)
        slot = 0
        for b in range(batches):
            row_j = table[:, b : b + 1]
            col_j = table[:, batches + b : batches + b + 1]
            radius = table[:, 2 * batches + b : 2 * batches + b + 1]
            cell_taper_ref[b] = gaspari(row_here - row_j, cell_cols - col_j, radius, width)
            for e in range(b + 1, batches):
                obs_taper_ref[slot] = gaspari(
                    rows[e : e + 1, :] - row_j, cols[e : e + 1, :] - col_j, radius, width
                )
                slot += 1

    return kernel


def observe_kernel(width, comps, batches, nobs, blocks, edge_rows):
    def kernel(q_ref, cx_ref, cy_ref, d_ref, cell_ref, weight_ref, own_ref, raw_ref, send_ref):
        q = q_ref[...]
        count = q.shape[0]
        cx, cy, d = cx_ref[...], cy_ref[...], d_ref[...]
        west = pltpu.roll(q, 1, 1)
        east = pltpu.roll(q, width - 1, 1)
        mine = q - jnp.maximum(cx, 0.0) * (q - west) - jnp.minimum(cx, 0.0) * (east - q)
        mine = mine - jnp.maximum(cy, 0.0) * q + jnp.minimum(cy, 0.0) * q
        mine = mine + d * (east + west - 4.0 * q)
        _, col = rows_cols(cell_ref[...], width)
        place = lax.broadcasted_iota(jnp.int32, (width, nobs), 0)
        pieces = split2(mine) + split2(q)
        stacked = jnp.concatenate(pieces, 0)
        for b in range(batches):
            pick = (place == col[b : b + 1, :]).astype(f32).astype(bf16)
            found = narrow(stacked, pick, 1, 0)
            w = jnp.concatenate(
                [weight_ref[b], jnp.zeros((nobs, 128 - comps), f32)], 1
            ).T[:comps]
            own = found[:count] + found[count : 2 * count]
            raw = found[2 * count : 3 * count] + found[3 * count :]
            at = slice(b * nobs, (b + 1) * nobs)
            own_ref[:, at] = jnp.sum(own.reshape(-1, comps, nobs) * w[None], axis=1)
            raw_ref[:, at] = jnp.sum(raw.reshape(-1, comps, nobs) * w[None], axis=1)
        cols_dev = width // blocks
        which = lax.broadcasted_iota(jnp.int32, (2 * blocks, width), 0)
        spot = lax.broadcasted_iota(jnp.int32, (2 * blocks, width), 1)
        start = (which >> 1) * cols_dev
        wanted = jnp.where(which & 1 == 0, start - 1, start + cols_dev)
        wanted = jnp.where(wanted < 0, wanted + width, wanted)
        wanted = jnp.where(wanted >= width, wanted - width, wanted)
        pick = (spot == wanted).astype(f32).astype(bf16)
        edges = sum(narrow(pick, part, 1, 1) for part in split3(q)[::-1])
        chunks = -(-count // 128)
        if chunks * 128 > count:
            edges = jnp.concatenate([edges, jnp.zeros((2 * blocks, chunks * 128 - count), f32)], 1)
        for i in range(blocks):
            at = slice(i * cols_dev, (i + 1) * cols_dev)
            send_ref[i, :count, :] = q[:, at]
            rows = [edges[2 * i : 2 * i + 2, j * 128 : (j + 1) * 128] for j in range(chunks)]
            if edge_rows > 2 * chunks:
                rows.append(jnp.zeros((edge_rows - 2 * chunks, 128), f32))
            send_ref[i, count:, :] = jnp.concatenate(rows, 0)

    return kernel


def join_kernel(width, batches, nobs):
    def kernel(place_ref, own_ref, raw_ref, above_ref, below_ref, cell_ref, out_ref):
        here = place_ref[0]
        row, col = rows_cols(cell_ref[...], width)
        place = lax.broadcasted_iota(jnp.int32, (width, nobs), 0)
        parts = split3(jnp.concatenate([above_ref[...], below_ref[...]], 0))
        stacked = jnp.concatenate([p.astype(f32) for p in parts] + [jnp.zeros((2, width), f32)], 0)
        stacked = stacked.astype(bf16)
        for b in range(batches):
            pick = (place == col[b : b + 1, :]).astype(f32).astype(bf16)
            found = narrow(stacked, pick, 1, 0)
            coef = found[0:2] + found[2:4] + found[4:6]
            r = row[b : b + 1, :]
            factor = jnp.where(r == here + 1, coef[0:1], jnp.where(r == here - 1, coef[1:2], 0.0))
            at = slice(b * nobs, (b + 1) * nobs)
            out_ref[:, at] = jnp.where(r == here, own_ref[:, at], factor * raw_ref[:, at])

    return kernel


def lane_spread(x, j):
    return jnp.take_along_axis(x, jnp.full(x.shape, j, jnp.int32), axis=1)


def row_spread(x, i):
    return jnp.broadcast_to(x[i : i + 1, :], x.shape)


def factored(cov, sides, error, members):
    tiles = cov.shape[0] // 8
    lane = lax.broadcasted_iota(jnp.int32, TILE, 1)
    sub = lax.broadcasted_iota(jnp.int32, TILE, 0)
    T = [cov[8 * q : 8 * q + 8, :] for q in range(tiles)]
    V = [sides[8 * q : 8 * q + 8, :] for q in range(tiles)]
    deviation = jnp.broadcast_to(jnp.sqrt(error), TILE)
    is_member = lane < members
    inverse, solved = [], []
    for p in range(tiles):
        block = (lane >= 8 * p) & (lane < 8 * p + 8)
        columns = [lane_spread(T[p], 8 * p + c) for c in range(8)]
        s = [[row_spread(columns[c], a) if a >= c else None for c in range(8)] for a in range(8)]
        joined = jnp.where(block, (lane - 8 * p == sub).astype(f32), T[p])
        R = [row_spread(joined, c) for c in range(8)]
        Z = [row_spread(V[p], c) for c in range(8)]
        rd, rs = [None] * 8, [None] * 8
        m = [[None] * 8 for _ in range(8)]
        for c in range(8):
            rd[c] = 1.0 / s[c][c]
            rs[c] = lax.rsqrt(s[c][c])
            root = s[c][c] * rs[c]
            spread = lane_spread(deviation, 8 * p + c)
            Z[c] = Z[c] * jnp.where(is_member, root / (root + spread), 1.0)
            for a in range(c + 1, 8):
                m[a][c] = s[a][c] * rd[c]
            for a in range(c + 1, 8):
                for e in range(c + 1, a + 1):
                    s[a][e] = s[a][e] - (s[a][c] * s[e][c]) * rd[c]
                R[a] = R[a] - m[a][c] * R[c]
                Z[a] = Z[a] - m[a][c] * Z[c]
        X, U = [None] * 8, [None] * 8
        for a in range(7, -1, -1):
            x, u = rd[a] * R[a], rd[a] * Z[a]
            for c in range(a + 1, 8):
                x = x - m[c][a] * X[c]
                u = u - m[c][a] * U[c]
            X[a], U[a] = x, u
        low, side = R[0] * rs[0], Z[0] * rs[0]
        for c in range(1, 8):
            low = jnp.where(sub == c, R[c] * rs[c], low)
            side = jnp.where(sub == c, Z[c] * rs[c], side)
        inverse.append(jnp.where(lane < 8 * p + 8, low, 0.0))
        solved.append(side)
        for q in range(p + 1, tiles):
            t, v = jnp.where(block, 0.0, T[q]), V[q]
            for c in range(8):
                column = lane_spread(T[q], 8 * p + c)
                t = t - column * X[c]
                v = v - column * U[c]
            T[q], V[q] = t, v
    return jnp.concatenate(inverse, 0), jnp.concatenate(solved, 0)


def coefficients(observed, value, error):
    members, nobs = observed.shape
    mean = jnp.sum(observed, axis=0, keepdims=True) / members
    anomaly = observed - mean
    row = lax.broadcasted_iota(jnp.int32, (nobs, nobs), 0)
    col = lax.broadcasted_iota(jnp.int32, (nobs, nobs), 1)
    cov = dot(anomaly, anomaly, 0, 0) / (members - 1) + jnp.where(row == col, error, 0.0)
    sides = jnp.concatenate(
        [anomaly, value - mean, jnp.zeros((nobs - members - 1, nobs), f32)], 0
    ).T
    inverse, solved = factored(cov, sides, error, members)
    back = dot(solved, inverse, 0, 0)
    return anomaly, back[members : members + 1] - back[:members]


def chain_kernel(part, batches, nobs):
    def kernel(y_ref, value_ref, error_ref, taper_ref, anomaly_ref, coeff_ref, *later_ref):
        if len(y_ref.shape) == 3:
            observed = jnp.concatenate([y_ref[i] for i in range(y_ref.shape[0])], 0)
        else:
            observed = y_ref[...]
        members = observed.shape[0]
        first = batches - observed.shape[1] // nobs
        Y = {b: observed[:, nobs * (b - first) : nobs * (b - first + 1)] for b in range(first, batches)}
        for b in part:
            anomaly, coeff = coefficients(Y[b], value_ref[b : b + 1, :], error_ref[b : b + 1, :])
            anomaly_ref[b - first] = anomaly
            coeff_ref[b - first] = coeff
            for e in range(b + 1, batches):
                slot = b * batches - b * (b + 1) // 2 + e - b - 1
                spread = Y[e] - jnp.sum(Y[e], axis=0, keepdims=True) / members
                gain = dot(anomaly, spread, 0, 0) / (members - 1) * taper_ref[slot]
                Y[e] = Y[e] + dot(coeff, gain, 1, 0)
        for e in range(part[-1] + 1, batches):
            at = e - part[-1] - 1
            later_ref[0][:, nobs * at : nobs * (at + 1)] = Y[e]

    return kernel


def update_kernel(width, comps, batches, members, cols_dev, count, group):
    def kernel(
        place_ref, own_ref, near_ref, far_ref, cx_ref, cy_ref, d_ref,
        taper_ref, *refs,
    ):
        *pair_refs, out_ref, grid_ref = refs
        pairs = [
            (pair_refs[i][k], pair_refs[i + 1][k])
            for i in range(0, len(pair_refs), 2)
            for k in range(pair_refs[i].shape[0])
        ]
        start = pl.multiple_of(place_ref[1] * cols_dev, cols_dev)
        cx = cx_ref[:, pl.ds(start, cols_dev)]
        cy = cy_ref[:, pl.ds(start, cols_dev)]
        d = d_ref[:, pl.ds(start, cols_dev)]
        lane = lax.broadcasted_iota(jnp.int32, (1, cols_dev), 1)
        even = jnp.full((1, cols_dev), place_ref[0] & 1, jnp.int32) == 0
        from_south, from_north = jnp.maximum(cy, 0.0), -jnp.minimum(cy, 0.0)
        from_near = jnp.where(even, from_north, from_south)
        from_far = jnp.where(even, from_south, from_north)
        from_west, from_east = jnp.maximum(cx, 0.0), -jnp.minimum(cx, 0.0)
        for s in range(own_ref.shape[0]):
            outer = to_columns(own_ref[s, count:, :])
            for j in range(-(-count // 128)):
                size = min(128, count - 128 * j)
                at = slice(128 * j, 128 * j + size)
                q, near, far = own_ref[s, at, :], near_ref[s, at, :], far_ref[s, at, :]
                west = jnp.where(lane == 0, outer[:size, 2 * j : 2 * j + 1], pltpu.roll(q, 1, 1))
                east = jnp.where(
                    lane == cols_dev - 1,
                    outer[:size, 2 * j + 1 : 2 * j + 2],
                    pltpu.roll(q, cols_dev - 1, 1),
                )
                x = q - from_west * (q - west) - from_east * (q - east)
                x = x - from_near * (q - near) - from_far * (q - far)
                x = x + d * (east + west + near + far - 4.0 * q)
                grid_ref[pl.ds(s * count + 128 * j, size), :] = x
        left, right, tapers = [], [], []
        nobs = taper_ref.shape[1]
        fill = -3 * members % 128
        blank = jnp.zeros((fill, group * cols_dev), bf16)
        for b in range(batches):
            hi, lo = split2(pairs[b][0])
            left.append(jnp.concatenate([hi, lo, hi, jnp.zeros((fill, nobs), bf16)], 0))
            hi, lo = split2(pairs[b][1])
            right.append(jnp.concatenate([hi, hi, lo], 1))
            tapers.append(jnp.tile(taper_ref[b] / (members - 1), (1, group)))
        for first in range(0, comps, group):
            x = jnp.concatenate(
                [grid_ref[pl.ds(first + i, members, comps), :] for i in range(group)], 1
            )
            for b in range(batches):
                spread = x - jnp.sum(x, axis=0, keepdims=True) / members
                hi, lo = split2(spread)
                gain = narrow(left[b], jnp.concatenate([hi, hi, lo, blank], 0), 0, 0) * tapers[b]
                hi, lo = split2(gain)
                x = x + narrow(right[b], jnp.concatenate([hi, lo, hi], 0), 1, 0)
            for i in range(group):
                out_ref[pl.ds(first + i, members, comps), :] = x[:, i * cols_dev : (i + 1) * cols_dev]

    return kernel


def summed(x, axis):
    size = lax.axis_size(axis)
    if size & (size - 1):
        return lax.psum(x, axis)
    step = 1
    while step < size:
        x = x + lax.ppermute(x, axis, [(i, i ^ step) for i in range(size)])
        step *= 2
    return x


def shards(
    prior_sample_array,
    courant_x,
    courant_y,
    diffusion,
    obs_cell,
    obs_value,
    obs_error,
    obs_weight,
    taper_radius,
):
    local, rows_dev, comps, width = prior_sample_array.shape
    blocks = lax.axis_size("mem")
    bands = lax.axis_size("sub")
    cols_dev = width // blocks
    members = local * blocks
    batches, nobs = obs_cell.shape
    count = local * comps
    edge_rows = -(-(2 * -(-count // 128)) // 8) * 8
    assert bands % 2 == 0 and rows_dev == 1 and cols_dev == 128 and nobs == 128
    place = jnp.stack([lax.axis_index("sub"), lax.axis_index("mem")]).astype(jnp.int32)
    up = [(i, i + 1) for i in range(bands - 1)]
    down = [(i + 1, i) for i in range(bands - 1)]

    above = lax.ppermute(jnp.maximum(courant_y, 0.0) + diffusion, "sub", down)
    below = lax.ppermute(diffusion - jnp.minimum(courant_y, 0.0), "sub", up)
    own, raw, send = call(
        observe_kernel(width, comps, batches, nobs, blocks, edge_rows),
        [(local, batches * nobs)] * 2 + [(blocks, count + edge_rows, cols_dev)],
        "observe",
        (
            prior_sample_array.reshape(count, width),
            courant_x,
            courant_y,
            diffusion,
            obs_cell,
            obs_weight,
        ),
    )
    grid = lax.all_to_all(send.reshape(blocks, 1, -1), "mem", 0, 0).reshape(send.shape)
    (partial,) = call(
        join_kernel(width, batches, nobs),
        [(local, batches * nobs)],
        "join",
        (own, raw, above, below, obs_cell),
        (place,),
    )
    obs_taper, cell_taper = call(
        taper_kernel(width, batches, nobs, cols_dev),
        [(batches * (batches - 1) // 2, nobs, nobs), (batches, nobs, cols_dev)],
        "tapers",
        (obs_cell, taper_radius),
        (place,),
    )
    reduced = summed(partial, "sub")
    reduced, grid = lax.optimization_barrier((reduced, grid))
    observed = lax.all_gather(reduced, "mem")
    near = lax.ppermute(grid, "sub", [(i, i ^ 1) for i in range(bands)])
    pairs = []
    half = batches // 2
    for part in (range(half), range(half, batches)):
        outs = call(
            chain_kernel(part, batches, nobs),
            [(len(part), members, nobs)] * 2
            + [(members, (batches - part[-1] - 1) * nobs)] * (part[-1] + 1 < batches),
            "chain",
            (observed, obs_value, obs_error, obs_taper),
        )
        pairs += outs[:2]
        if part[-1] + 1 < batches:
            observed, near = lax.optimization_barrier((outs[2], near))
    far = lax.ppermute(
        near,
        "sub",
        [(i, i + 2) for i in range(0, bands - 2, 2)] + [(i, i - 2) for i in range(3, bands, 2)],
    )
    (out,) = call(
        update_kernel(width, comps, batches, members, cols_dev, count, 4),
        [(members * comps, cols_dev)],
        "update",
        (grid, near, far, courant_x, courant_y, diffusion, cell_taper, *pairs),
        (place,),
        (pltpu.VMEM((members * comps, cols_dev), f32),),
    )
    return out.reshape(members, rows_dev, comps, cols_dev)


def solution(mesh):
    return jax.shard_map(
        shards,
        mesh=mesh,
        in_specs=(
            P("mem", "sub", None, None),
            P("sub", None),
            P("sub", None),
            P("sub", None),
            P(),
            P(),
            P(),
            P(),
            P(),
        ),
        out_specs=P(None, "sub", None, "mem"),
        check_vma=False,
    )
```

```python
import jax
import jax.numpy as jnp
from jax import lax
from jax.experimental import pallas as pl
from jax.experimental.pallas import tpu as pltpu
from jax.sharding import PartitionSpec as P

highest = lax.Precision.HIGHEST
f32 = jnp.float32
bf16 = jnp.bfloat16
TILE = (8, 128)


def dot(a, b, ca, cb, precision=highest):
    return lax.dot_general(
        a, b, (((ca,), (cb,)), ((), ())), precision=precision, preferred_element_type=f32
    )


def narrow(a, b, ca, cb):
    return dot(a, b, ca, cb, None)


def split2(x):
    hi = x.astype(bf16)
    return hi, (x - hi.astype(f32)).astype(bf16)


def split3(x):
    hi = x.astype(bf16)
    rest = x - hi.astype(f32)
    mid = rest.astype(bf16)
    return hi, mid, (rest - mid.astype(f32)).astype(bf16)


def call(kernel, out_shapes, name, operands, scalars=(), scratch=(), cost=None):
    specs = [pl.BlockSpec(memory_space=pltpu.SMEM) for _ in scalars]
    specs += [pl.BlockSpec(memory_space=pltpu.VMEM) for _ in operands]
    return pl.pallas_call(
        kernel,
        in_specs=specs,
        out_specs=[pl.BlockSpec(memory_space=pltpu.VMEM) for _ in out_shapes],
        out_shape=[jax.ShapeDtypeStruct(s, f32) for s in out_shapes],
        scratch_shapes=list(scratch),
        compiler_params=pltpu.CompilerParams(vmem_limit_bytes=48 * 2**20),
        cost_estimate=cost,
        name=name,
    )(*scalars, *operands)


def rows_cols(cells, width):
    if width & (width - 1) == 0:
        shift = width.bit_length() - 1
        return cells >> shift, cells & (width - 1)
    return cells // width, cells % width


def to_columns(rows):
    n = rows.shape[0]
    return jnp.concatenate([rows, jnp.zeros((128 - n, 128), f32)], 0).T


def gaspari(delta_row, delta_col, cutoff_radius, width):
    half = width // 2
    folded = jnp.where(delta_col >= half, delta_col - width, delta_col)
    folded = jnp.where(delta_col < -half, delta_col + width, folded)
    ratio = jnp.sqrt(delta_row * delta_row + folded * folded) / cutoff_radius
    inner = (((-0.25 * ratio + 0.5) * ratio + 0.625) * ratio - 5.0 / 3.0) * ratio * ratio + 1.0
    bounded = jnp.maximum(ratio, 1.0)
    outer = (
        ((((ratio / 12.0 - 0.5) * ratio + 0.625) * ratio + 5.0 / 3.0) * ratio - 5.0) * ratio
        + 4.0
        - 2.0 / (3.0 * bounded)
    )
    return jnp.where(ratio <= 1.0, inner, jnp.where(ratio < 2.0, outer, 0.0))


def taper_kernel(width, batches, nobs, cols_dev):
    def kernel(place_ref, cell_ref, radius_ref, obs_taper_ref, cell_taper_ref):
        row_here = place_ref[0].astype(f32)
        col_here = place_ref[1] * cols_dev
        row_i, col_i = rows_cols(cell_ref[...], width)
        rows = row_i.astype(f32)
        cols = col_i.astype(f32)
        table = to_columns(jnp.concatenate([rows, cols, radius_ref[...]], 0))
        lane = lax.broadcasted_iota(jnp.int32, (1, cols_dev), 1)
        cell_cols = (lane + col_here).astype(f32)
        slot = 0
        for b in range(batches):
            row_j = table[:, b : b + 1]
            col_j = table[:, batches + b : batches + b + 1]
            radius = table[:, 2 * batches + b : 2 * batches + b + 1]
            cell_taper_ref[b] = gaspari(row_here - row_j, cell_cols - col_j, radius, width)
            for e in range(b + 1, batches):
                obs_taper_ref[slot] = gaspari(
                    rows[e : e + 1, :] - row_j, cols[e : e + 1, :] - col_j, radius, width
                )
                slot += 1

    return kernel


def observe_kernel(width, comps, batches, nobs, blocks, edge_rows, local):
    def kernel(place_ref, q_ref, cx_ref, cy_ref, d_ref, cell_ref, weight_ref, share_ref, send_ref):
        here = place_ref[0]
        q = q_ref[...]
        count = q.shape[0]
        cx, cy, d = cx_ref[...], cy_ref[...], d_ref[...]
        west = pltpu.roll(q, 1, 1)
        east = pltpu.roll(q, width - 1, 1)
        mine = q - jnp.maximum(cx, 0.0) * (q - west) - jnp.minimum(cx, 0.0) * (east - q)
        mine = mine - jnp.maximum(cy, 0.0) * q + jnp.minimum(cy, 0.0) * q
        mine = mine + d * (east + west - 4.0 * q)
        from_south, from_north = jnp.maximum(cy, 0.0) + d, d - jnp.minimum(cy, 0.0)
        even = jnp.full((1, width), here & 1, jnp.int32) == 0
        near = jnp.where(even, from_north, from_south)
        far = jnp.where(even, from_south, from_north)
        scales = [part.astype(f32) for part in split3(jnp.concatenate([near, far], 0))]
        scales = jnp.concatenate(scales + [jnp.zeros((10, width), f32)], 0).astype(bf16)
        row, col = rows_cols(cell_ref[...], width)
        place = lax.broadcasted_iota(jnp.int32, (width, nobs), 0)
        stacked = jnp.concatenate(split2(mine) + split2(q) + (scales,), 0)
        for b in range(batches):
            pick = (place == col[b : b + 1, :]).astype(f32).astype(bf16)
            found = narrow(stacked, pick, 1, 0)
            own = found[:count] + found[count : 2 * count]
            raw = found[2 * count : 3 * count] + found[3 * count : 4 * count]
            scale = found[4 * count : 4 * count + 2]
            scale = scale + found[4 * count + 2 : 4 * count + 4]
            scale = scale + found[4 * count + 4 : 4 * count + 6]
            away = row[b : b + 1, :] - here
            owned, beside = away == 0, (away == 1) | (away == -1)
            value = jnp.where(owned, own, jnp.where(beside, raw, 0.0))
            value = jnp.sum(value.reshape(-1, comps, nobs) * weight_ref[b][None], axis=1)
            fill = share_ref.shape[0] - local - 2
            share = [value, jnp.where(owned, scale, 1.0)]
            if fill:
                share.append(jnp.zeros((fill, nobs), f32))
            share_ref[:, b * nobs : (b + 1) * nobs] = jnp.concatenate(share, 0)
        cols_dev = width // blocks
        which = lax.broadcasted_iota(jnp.int32, (2 * blocks, width), 0)
        spot = lax.broadcasted_iota(jnp.int32, (2 * blocks, width), 1)
        start = (which >> 1) * cols_dev
        wanted = jnp.where(which & 1 == 0, start - 1, start + cols_dev)
        wanted = jnp.where(wanted < 0, wanted + width, wanted)
        wanted = jnp.where(wanted >= width, wanted - width, wanted)
        pick = (spot == wanted).astype(f32).astype(bf16)
        edges = sum(narrow(pick, part, 1, 1) for part in split3(q)[::-1])
        chunks = -(-count // 128)
        if chunks * 128 > count:
            edges = jnp.concatenate([edges, jnp.zeros((2 * blocks, chunks * 128 - count), f32)], 1)
        for i in range(blocks):
            at = slice(i * cols_dev, (i + 1) * cols_dev)
            send_ref[i, :count, :] = q[:, at]
            rows = [edges[2 * i : 2 * i + 2, j * 128 : (j + 1) * 128] for j in range(chunks)]
            if edge_rows > 2 * chunks:
                rows.append(jnp.zeros((edge_rows - 2 * chunks, 128), f32))
            send_ref[i, count:, :] = jnp.concatenate(rows, 0)

    return kernel


def join_kernel(local, first, last):
    def kernel(mine_ref, other_ref, out_ref):
        mine, other = mine_ref[...], other_ref[...]
        at = local
        value = mine[:local] * other[at : at + 1] + other[:local] * mine[at : at + 1]
        if last:
            out_ref[...] = value
        else:
            at = local + 1 if first else local
            scale = mine[at : at + 1] * other[at : at + 1]
            blank = jnp.zeros((out_ref.shape[0] - local - 1, value.shape[1]), f32)
            out_ref[...] = jnp.concatenate([value, scale, blank], 0)

    return kernel


def lane_spread(x, j):
    return jnp.take_along_axis(x, jnp.full(x.shape, j, jnp.int32), axis=1)


def row_spread(x, i):
    return jnp.broadcast_to(x[i : i + 1, :], x.shape)


def factored(cov, sides, error, members):
    tiles = cov.shape[0] // 8
    lane = lax.broadcasted_iota(jnp.int32, TILE, 1)
    sub = lax.broadcasted_iota(jnp.int32, TILE, 0)
    T = [cov[8 * q : 8 * q + 8, :] for q in range(tiles)]
    V = [sides[8 * q : 8 * q + 8, :] for q in range(tiles)]
    deviation = jnp.broadcast_to(jnp.sqrt(error), TILE)
    is_member = lane < members
    inverse, solved = [], []
    for p in range(tiles):
        block = (lane >= 8 * p) & (lane < 8 * p + 8)
        columns = [lane_spread(T[p], 8 * p + c) for c in range(8)]
        s = [[row_spread(columns[c], a) if a >= c else None for c in range(8)] for a in range(8)]
        joined = jnp.where(block, (lane - 8 * p == sub).astype(f32), T[p])
        R = [row_spread(joined, c) for c in range(8)]
        Z = [row_spread(V[p], c) for c in range(8)]
        rd, rs = [None] * 8, [None] * 8
        m = [[None] * 8 for _ in range(8)]
        for c in range(8):
            rd[c] = 1.0 / s[c][c]
            rs[c] = lax.rsqrt(s[c][c])
            root = s[c][c] * rs[c]
            spread = lane_spread(deviation, 8 * p + c)
            Z[c] = Z[c] * jnp.where(is_member, root / (root + spread), 1.0)
            for a in range(c + 1, 8):
                m[a][c] = s[a][c] * rd[c]
            for a in range(c + 1, 8):
                for e in range(c + 1, a + 1):
                    s[a][e] = s[a][e] - (s[a][c] * s[e][c]) * rd[c]
                R[a] = R[a] - m[a][c] * R[c]
                Z[a] = Z[a] - m[a][c] * Z[c]
        X, U = [None] * 8, [None] * 8
        for a in range(7, -1, -1):
            x, u = rd[a] * R[a], rd[a] * Z[a]
            for c in range(a + 1, 8):
                x = x - m[c][a] * X[c]
                u = u - m[c][a] * U[c]
            X[a], U[a] = x, u
        low, side = R[0] * rs[0], Z[0] * rs[0]
        for c in range(1, 8):
            low = jnp.where(sub == c, R[c] * rs[c], low)
            side = jnp.where(sub == c, Z[c] * rs[c], side)
        inverse.append(jnp.where(lane < 8 * p + 8, low, 0.0))
        solved.append(side)
        for q in range(p + 1, tiles):
            t, v = jnp.where(block, 0.0, T[q]), V[q]
            for c in range(8):
                column = lane_spread(T[q], 8 * p + c)
                t = t - column * X[c]
                v = v - column * U[c]
            T[q], V[q] = t, v
    return jnp.concatenate(inverse, 0), jnp.concatenate(solved, 0)


def coefficients(observed, value, error):
    members, nobs = observed.shape
    mean = jnp.sum(observed, axis=0, keepdims=True) / members
    anomaly = observed - mean
    row = lax.broadcasted_iota(jnp.int32, (nobs, nobs), 0)
    col = lax.broadcasted_iota(jnp.int32, (nobs, nobs), 1)
    cov = dot(anomaly, anomaly, 0, 0) / (members - 1) + jnp.where(row == col, error, 0.0)
    sides = jnp.concatenate(
        [anomaly, value - mean, jnp.zeros((nobs - members - 1, nobs), f32)], 0
    ).T
    inverse, solved = factored(cov, sides, error, members)
    back = dot(solved, inverse, 0, 0)
    return anomaly, back[members : members + 1] - back[:members]


def chain_kernel(part, batches, nobs):
    def kernel(y_ref, value_ref, error_ref, taper_ref, anomaly_ref, coeff_ref, *later_ref):
        if len(y_ref.shape) == 3:
            observed = jnp.concatenate([y_ref[i] for i in range(y_ref.shape[0])], 0)
        else:
            observed = y_ref[...]
        members = observed.shape[0]
        first = batches - observed.shape[1] // nobs
        Y = {b: observed[:, nobs * (b - first) : nobs * (b - first + 1)] for b in range(first, batches)}
        for b in part:
            anomaly, coeff = coefficients(Y[b], value_ref[b : b + 1, :], error_ref[b : b + 1, :])
            anomaly_ref[b - first] = anomaly
            coeff_ref[b - first] = coeff
            for e in range(b + 1, batches):
                slot = b * batches - b * (b + 1) // 2 + e - b - 1
                spread = Y[e] - jnp.sum(Y[e], axis=0, keepdims=True) / members
                gain = dot(anomaly, spread, 0, 0) / (members - 1) * taper_ref[slot]
                Y[e] = Y[e] + dot(coeff, gain, 1, 0)
        for e in range(part[-1] + 1, batches):
            at = e - part[-1] - 1
            later_ref[0][:, nobs * at : nobs * (at + 1)] = Y[e]

    return kernel


def update_kernel(width, comps, batches, members, cols_dev, count, group):
    def kernel(
        place_ref, own_ref, near_a, near_b, far_a, far_b, cx_ref, cy_ref, d_ref,
        taper_ref, *refs,
    ):
        *pair_refs, out_ref, grid_ref = refs
        pairs = [
            (pair_refs[i][k], pair_refs[i + 1][k])
            for i in range(0, len(pair_refs), 2)
            for k in range(pair_refs[i].shape[0])
        ]
        start = pl.multiple_of(place_ref[1] * cols_dev, cols_dev)
        cx = cx_ref[:, pl.ds(start, cols_dev)]
        cy = cy_ref[:, pl.ds(start, cols_dev)]
        d = d_ref[:, pl.ds(start, cols_dev)]
        lane = lax.broadcasted_iota(jnp.int32, (1, cols_dev), 1)
        even = jnp.full((1, cols_dev), place_ref[0] & 1, jnp.int32) == 0
        from_south, from_north = jnp.maximum(cy, 0.0), -jnp.minimum(cy, 0.0)
        from_near = jnp.where(even, from_north, from_south)
        from_far = jnp.where(even, from_south, from_north)
        from_west, from_east = jnp.maximum(cx, 0.0), -jnp.minimum(cx, 0.0)
        for s in range(own_ref.shape[0]):
            middle = near_a.shape[0]
            near_ref, far_ref = (near_a, far_a) if s < middle else (near_b, far_b)
            outer = to_columns(own_ref[s, count:, :])
            for j in range(-(-count // 128)):
                size = min(128, count - 128 * j)
                at = slice(128 * j, 128 * j + size)
                q, near, far = own_ref[s, at, :], near_ref[s % middle, at, :], far_ref[s % middle, at, :]
                west = jnp.where(lane == 0, outer[:size, 2 * j : 2 * j + 1], pltpu.roll(q, 1, 1))
                east = jnp.where(
                    lane == cols_dev - 1,
                    outer[:size, 2 * j + 1 : 2 * j + 2],
                    pltpu.roll(q, cols_dev - 1, 1),
                )
                x = q - from_west * (q - west) - from_east * (q - east)
                x = x - from_near * (q - near) - from_far * (q - far)
                x = x + d * (east + west + near + far - 4.0 * q)
                grid_ref[pl.ds(s * count + 128 * j, size), :] = x
        left, right, tapers = [], [], []
        nobs = taper_ref.shape[1]
        fill = -3 * members % 128
        blank = jnp.zeros((fill, group * cols_dev), bf16)
        for b in range(batches):
            hi, lo = split2(pairs[b][0])
            left.append(jnp.concatenate([hi, lo, hi, jnp.zeros((fill, nobs), bf16)], 0))
            hi, lo = split2(pairs[b][1])
            right.append(jnp.concatenate([hi, hi, lo], 1))
            tapers.append(jnp.tile(taper_ref[b] / (members - 1), (1, group)))
        for first in range(0, comps, group):
            x = jnp.concatenate(
                [grid_ref[pl.ds(first + i, members, comps), :] for i in range(group)], 1
            )
            for b in range(batches):
                spread = x - jnp.sum(x, axis=0, keepdims=True) / members
                hi, lo = split2(spread)
                gain = narrow(left[b], jnp.concatenate([hi, hi, lo, blank], 0), 0, 0) * tapers[b]
                hi, lo = split2(gain)
                x = x + narrow(right[b], jnp.concatenate([hi, lo, hi], 0), 1, 0)
            for i in range(group):
                out_ref[pl.ds(first + i, members, comps), :] = x[:, i * cols_dev : (i + 1) * cols_dev]

    return kernel


def shards(
    prior_sample_array,
    courant_x,
    courant_y,
    diffusion,
    obs_cell,
    obs_value,
    obs_error,
    obs_weight,
    taper_radius,
):
    local, rows_dev, comps, width = prior_sample_array.shape
    blocks = lax.axis_size("mem")
    bands = lax.axis_size("sub")
    cols_dev = width // blocks
    members = local * blocks
    batches, nobs = obs_cell.shape
    count = local * comps
    edge_rows = -(-(2 * -(-count // 128)) // 8) * 8
    assert bands & (bands - 1) == 0 and bands > 1 and rows_dev == 1 and batches > 2 and cols_dev == 128 and nobs == 128
    place = jnp.stack([lax.axis_index("sub"), lax.axis_index("mem")]).astype(jnp.int32)

    share_rows = -(-(local + 2) // 8) * 8
    share, send = call(
        observe_kernel(width, comps, batches, nobs, blocks, edge_rows, local),
        [(share_rows, batches * nobs), (blocks, count + edge_rows, cols_dev)],
        "observe",
        (
            prior_sample_array.reshape(count, width),
            courant_x,
            courant_y,
            diffusion,
            obs_cell,
            obs_weight.transpose(0, 2, 1),
        ),
        (place,),
    )
    grid = lax.all_to_all(send.reshape(blocks, 1, -1), "mem", 0, 0).reshape(send.shape)
    obs_taper, cell_taper = call(
        taper_kernel(width, batches, nobs, cols_dev),
        [(batches * (batches - 1) // 2, nobs, nobs), (batches, nobs, cols_dev)],
        "tapers",
        (obs_cell, taper_radius),
        (place,),
    )
    step = 1
    while step < bands:
        other = lax.ppermute(share, "sub", [(i, i ^ step) for i in range(bands)])
        if step == 1:
            other, obs_taper, cell_taper = lax.optimization_barrier((other, obs_taper, cell_taper))
        last = 2 * step == bands
        (share,) = call(
            join_kernel(local, step == 1, last),
            [(local if last else share_rows, batches * nobs)],
            "join",
            (share, other),
        )
        step *= 2
    share, grid = lax.optimization_barrier((share, grid))
    swap = [(i, i ^ 1) for i in range(bands)]
    onward = [(i, i + 2) for i in range(0, bands - 2, 2)] + [(i, i - 2) for i in range(3, bands, 2)]
    middle = blocks // 2
    near = [lax.ppermute(part, "sub", swap) for part in (grid[:middle], grid[middle:])]
    observed = lax.all_gather(share, "mem")
    pairs, far = [], []
    for i, part in enumerate((range(1), range(1, 2), range(2, batches))):
        if i != 1:
            at = i // 2
            observed, near[at] = lax.optimization_barrier((observed, near[at]))
            if at:
                observed, far[0] = lax.optimization_barrier((observed, far[0]))
            far.append(lax.ppermute(near[at], "sub", onward))
        outs = call(
            chain_kernel(part, batches, nobs),
            [(len(part), members, nobs)] * 2
            + [(members, (batches - part[-1] - 1) * nobs)] * (part[-1] + 1 < batches),
            "chain",
            (observed, obs_value, obs_error, obs_taper),
            cost=pl.CostEstimate(flops=1000, bytes_accessed=1000, transcendentals=0),
        )
        pairs += outs[:2]
        observed = outs[-1]
    (out,) = call(
        update_kernel(width, comps, batches, members, cols_dev, count, 4),
        [(members * comps, cols_dev)],
        "update",
        (grid, *near, *far, courant_x, courant_y, diffusion, cell_taper, *pairs),
        (place,),
        (pltpu.VMEM((members * comps, cols_dev), f32),),
    )
    return out.reshape(members, rows_dev, comps, cols_dev)


def solution(mesh):
    return jax.shard_map(
        shards,
        mesh=mesh,
        in_specs=(
            P("mem", "sub", None, None),
            P("sub", None),
            P("sub", None),
            P("sub", None),
            P(),
            P(),
            P(),
            P(),
            P(),
        ),
        out_specs=P(None, "sub", None, "mem"),
        check_vma=False,
    )
```

```python
import jax
import jax.numpy as jnp
from jax import lax
from jax.experimental import pallas as pl
from jax.experimental.pallas import tpu as pltpu
from jax.sharding import PartitionSpec as P

highest = lax.Precision.HIGHEST
f32 = jnp.float32
bf16 = jnp.bfloat16
TILE = (8, 128)


def dot(a, b, ca, cb, precision=highest):
    return lax.dot_general(
        a, b, (((ca,), (cb,)), ((), ())), precision=precision, preferred_element_type=f32
    )


def narrow(a, b, ca, cb):
    return dot(a, b, ca, cb, None)


def split2(x):
    hi = x.astype(bf16)
    return hi, (x - hi.astype(f32)).astype(bf16)


def split3(x):
    hi = x.astype(bf16)
    rest = x - hi.astype(f32)
    mid = rest.astype(bf16)
    return hi, mid, (rest - mid.astype(f32)).astype(bf16)


def call(kernel, out_shapes, name, operands, scalars=(), scratch=(), cost=None):
    specs = [pl.BlockSpec(memory_space=pltpu.SMEM) for _ in scalars]
    specs += [pl.BlockSpec(memory_space=pltpu.VMEM) for _ in operands]
    return pl.pallas_call(
        kernel,
        in_specs=specs,
        out_specs=[pl.BlockSpec(memory_space=pltpu.VMEM) for _ in out_shapes],
        out_shape=[jax.ShapeDtypeStruct(s, f32) for s in out_shapes],
        scratch_shapes=list(scratch),
        compiler_params=pltpu.CompilerParams(vmem_limit_bytes=48 * 2**20),
        cost_estimate=cost,
        name=name,
    )(*scalars, *operands)


def rows_cols(cells, width):
    if width & (width - 1) == 0:
        shift = width.bit_length() - 1
        return cells >> shift, cells & (width - 1)
    return cells // width, cells % width


def to_columns(rows):
    n = rows.shape[0]
    return jnp.concatenate([rows, jnp.zeros((128 - n, 128), f32)], 0).T


def gaspari(delta_row, delta_col, cutoff_radius, width):
    half = width // 2
    folded = jnp.where(delta_col >= half, delta_col - width, delta_col)
    folded = jnp.where(delta_col < -half, delta_col + width, folded)
    ratio = jnp.sqrt(delta_row * delta_row + folded * folded) / cutoff_radius
    inner = (((-0.25 * ratio + 0.5) * ratio + 0.625) * ratio - 5.0 / 3.0) * ratio * ratio + 1.0
    bounded = jnp.maximum(ratio, 1.0)
    outer = (
        ((((ratio / 12.0 - 0.5) * ratio + 0.625) * ratio + 5.0 / 3.0) * ratio - 5.0) * ratio
        + 4.0
        - 2.0 / (3.0 * bounded)
    )
    return jnp.where(ratio <= 1.0, inner, jnp.where(ratio < 2.0, outer, 0.0))


def taper_kernel(width, batches, nobs, cols_dev):
    def kernel(place_ref, cell_ref, radius_ref, obs_taper_ref, cell_taper_ref):
        row_here = place_ref[0].astype(f32)
        col_here = place_ref[1] * cols_dev
        row_i, col_i = rows_cols(cell_ref[...], width)
        rows = row_i.astype(f32)
        cols = col_i.astype(f32)
        table = to_columns(jnp.concatenate([rows, cols, radius_ref[...]], 0))
        lane = lax.broadcasted_iota(jnp.int32, (1, cols_dev), 1)
        cell_cols = (lane + col_here).astype(f32)
        slot = 0
        for b in range(batches):
            row_j = table[:, b : b + 1]
            col_j = table[:, batches + b : batches + b + 1]
            radius = table[:, 2 * batches + b : 2 * batches + b + 1]
            cell_taper_ref[b] = gaspari(row_here - row_j, cell_cols - col_j, radius, width)
            for e in range(b + 1, batches):
                obs_taper_ref[slot] = gaspari(
                    rows[e : e + 1, :] - row_j, cols[e : e + 1, :] - col_j, radius, width
                )
                slot += 1

    return kernel


def observe_kernel(width, comps, batches, nobs, blocks, edge_rows, local):
    def kernel(place_ref, q_ref, cx_ref, cy_ref, d_ref, cell_ref, weight_ref, share_ref, send_ref):
        here = place_ref[0]
        q = q_ref[...]
        count = q.shape[0]
        cx, cy, d = cx_ref[...], cy_ref[...], d_ref[...]
        west = pltpu.roll(q, 1, 1)
        east = pltpu.roll(q, width - 1, 1)
        mine = q - jnp.maximum(cx, 0.0) * (q - west) - jnp.minimum(cx, 0.0) * (east - q)
        mine = mine - jnp.maximum(cy, 0.0) * q + jnp.minimum(cy, 0.0) * q
        mine = mine + d * (east + west - 4.0 * q)
        from_south, from_north = jnp.maximum(cy, 0.0) + d, d - jnp.minimum(cy, 0.0)
        even = jnp.full((1, width), here & 1, jnp.int32) == 0
        near = jnp.where(even, from_north, from_south)
        far = jnp.where(even, from_south, from_north)
        scales = [part.astype(f32) for part in split3(jnp.concatenate([near, far], 0))]
        scales = jnp.concatenate(scales + [jnp.zeros((10, width), f32)], 0).astype(bf16)
        row, col = rows_cols(cell_ref[...], width)
        row = jnp.concatenate([row[b : b + 1] for b in range(batches)], 1)
        col = jnp.concatenate([col[b : b + 1] for b in range(batches)], 1)
        away = row - here
        owned, beside = away == 0, (away == 1) | (away == -1)
        place = lax.broadcasted_iota(jnp.int32, (width, batches * nobs), 0)
        own_pick = (place == jnp.where(owned, col, -1)).astype(f32).astype(bf16)
        raw_pick = (place == jnp.where(beside, col, -1)).astype(f32).astype(bf16)
        q_parts = split3(q)
        value = narrow(
            jnp.concatenate(split2(mine) + q_parts[:2], 1),
            jnp.concatenate([own_pick, own_pick, raw_pick, raw_pick], 0),
            1,
            0,
        )
        weight = jnp.concatenate([weight_ref[b] for b in range(batches)], 1)
        value = jnp.sum(value.reshape(-1, comps, batches * nobs) * weight[None], axis=1)
        scale = narrow(scales, own_pick, 1, 0)
        scale = scale[0:2] + scale[2:4] + scale[4:6]
        share = [value, jnp.where(owned, scale, 1.0)]
        fill = share_ref.shape[0] - local - 2
        if fill:
            share.append(jnp.zeros((fill, batches * nobs), f32))
        share_ref[...] = jnp.concatenate(share, 0)
        cols_dev = width // blocks
        lanes = -(-2 * blocks // 128) * 128
        which = lax.broadcasted_iota(jnp.int32, (width, lanes), 1)
        spot = lax.broadcasted_iota(jnp.int32, (width, lanes), 0)
        start = (which >> 1) * cols_dev
        wanted = jnp.where(which & 1 == 0, start - 1, start + cols_dev)
        wanted = jnp.where(wanted < 0, wanted + width, wanted)
        wanted = jnp.where(wanted == width, 0, wanted)
        pick = (spot == wanted).astype(f32).astype(bf16)
        edges = narrow(
            jnp.concatenate(q_parts, 1), jnp.concatenate([pick, pick, pick], 0), 1, 0
        )
        room = -count % 128
        if room:
            edges = jnp.concatenate([edges, jnp.zeros((room, lanes), f32)], 0)
        edges = edges.T
        chunks = -(-count // 128)
        for i in range(blocks):
            at = slice(i * cols_dev, (i + 1) * cols_dev)
            send_ref[i, :count, :] = q[:, at]
            rows = [edges[2 * i : 2 * i + 2, j * 128 : (j + 1) * 128] for j in range(chunks)]
            if edge_rows > 2 * chunks:
                rows.append(jnp.zeros((edge_rows - 2 * chunks, 128), f32))
            send_ref[i, count:, :] = jnp.concatenate(rows, 0)

    return kernel


def join_kernel(local, first, last):
    def kernel(mine_ref, other_ref, out_ref):
        mine, other = mine_ref[...], other_ref[...]
        at = local
        value = mine[:local] * other[at : at + 1] + other[:local] * mine[at : at + 1]
        if last:
            out_ref[...] = value
        else:
            at = local + 1 if first else local
            scale = mine[at : at + 1] * other[at : at + 1]
            blank = jnp.zeros((out_ref.shape[0] - local - 1, value.shape[1]), f32)
            out_ref[...] = jnp.concatenate([value, scale, blank], 0)

    return kernel


def lane_spread(x, j):
    return jnp.take_along_axis(x, jnp.full(x.shape, j, jnp.int32), axis=1)


def row_spread(x, i):
    return jnp.broadcast_to(x[i : i + 1, :], x.shape)


def factored(cov, sides, error, members, span=4):
    tiles = cov.shape[0] // 8
    lane = lax.broadcasted_iota(jnp.int32, TILE, 1)
    sub = lax.broadcasted_iota(jnp.int32, TILE, 0)
    T = [cov[8 * q : 8 * q + 8, :] for q in range(tiles)]
    V = [sides[8 * q : 8 * q + 8, :] for q in range(tiles)]
    deviation = jnp.broadcast_to(jnp.sqrt(error), TILE)
    is_member = lane < members
    inverse, solved, finished = [], [], []
    for p in range(tiles):
        block = (lane >= 8 * p) & (lane < 8 * p + 8)
        columns = [lane_spread(T[p], 8 * p + c) for c in range(8)]
        s = [[row_spread(columns[c], a) if a >= c else None for c in range(8)] for a in range(8)]
        joined = jnp.where(block, (lane - 8 * p == sub).astype(f32), T[p])
        R = [row_spread(joined, c) for c in range(8)]
        Z = [row_spread(V[p], c) for c in range(8)]
        rd, rs = [None] * 8, [None] * 8
        m = [[None] * 8 for _ in range(8)]
        for c in range(8):
            rd[c] = 1.0 / s[c][c]
            rs[c] = lax.rsqrt(s[c][c])
            root = s[c][c] * rs[c]
            spread = lane_spread(deviation, 8 * p + c)
            Z[c] = Z[c] * jnp.where(is_member, root / (root + spread), 1.0)
            for a in range(c + 1, 8):
                m[a][c] = s[a][c] * rd[c]
            for a in range(c + 1, 8):
                for e in range(c + 1, a + 1):
                    s[a][e] = s[a][e] - (s[a][c] * s[e][c]) * rd[c]
                R[a] = R[a] - m[a][c] * R[c]
                Z[a] = Z[a] - m[a][c] * Z[c]
        X, U = [None] * 8, [None] * 8
        for a in range(7, -1, -1):
            x, u = rd[a] * R[a], rd[a] * Z[a]
            for c in range(a + 1, 8):
                x = x - m[c][a] * X[c]
                u = u - m[c][a] * U[c]
            X[a], U[a] = x, u
        low, side = R[0] * rs[0], Z[0] * rs[0]
        for c in range(1, 8):
            low = jnp.where(sub == c, R[c] * rs[c], low)
            side = jnp.where(sub == c, Z[c] * rs[c], side)
        inverse.append(jnp.where(lane < 8 * p + 8, low, 0.0))
        solved.append(side)
        finished.append((low, side))
        edge = (p // span + 1) * span
        for q in range(p + 1, edge):
            t, v = jnp.where(block, 0.0, T[q]), V[q]
            for c in range(8):
                column = lane_spread(T[q], 8 * p + c)
                t = t - column * X[c]
                v = v - column * U[c]
            T[q], V[q] = t, v
        if p + 1 == edge and edge < tiles:
            rows = finished[edge - span : edge]
            upper = jnp.concatenate([low for low, _ in rows], 0)
            keep = [
                jnp.where((lane < 8 * (edge - span + i + 1)) | (lane >= 8 * edge), low, 0.0)
                for i, (low, _) in enumerate(rows)
            ]
            side_rows = jnp.concatenate([side for _, side in rows], 0)
            taken = products(upper, jnp.concatenate([jnp.concatenate(keep, 0), side_rows], 1))
            inside = (lane >= 8 * (edge - span)) & (lane < 8 * edge)
            for q in range(edge, tiles):
                at = slice(8 * q, 8 * q + 8)
                T[q] = jnp.where(inside, 0.0, T[q]) - taken[at, :128]
                V[q] = V[q] - taken[at, 128:]
    return jnp.concatenate(inverse, 0), jnp.concatenate(solved, 0)


def products(a, b):
    ah, am, al = split3(a)
    bh, bm, bl = split3(b)
    return narrow(
        jnp.concatenate([al, am, ah, am, ah, ah], 0),
        jnp.concatenate([bh, bm, bl, bh, bm, bh], 0),
        0,
        0,
    )


def coefficients(observed, value, error):
    members, nobs = observed.shape
    mean = jnp.sum(observed, axis=0, keepdims=True) / members
    anomaly = observed - mean
    row = lax.broadcasted_iota(jnp.int32, (nobs, nobs), 0)
    col = lax.broadcasted_iota(jnp.int32, (nobs, nobs), 1)
    cov = products(anomaly, anomaly) / (members - 1) + jnp.where(row == col, error, 0.0)
    sides = jnp.concatenate(
        [anomaly, value - mean, jnp.zeros((nobs - members - 1, nobs), f32)], 0
    ).T
    inverse, solved = factored(cov, sides, error, members)
    back = products(solved, inverse)
    return anomaly, back[members : members + 1] - back[:members]


def chain_kernel(part, batches, nobs):
    def kernel(y_ref, value_ref, error_ref, taper_ref, anomaly_ref, coeff_ref, *later_ref):
        if len(y_ref.shape) == 3:
            observed = jnp.concatenate([y_ref[i] for i in range(y_ref.shape[0])], 0)
        else:
            observed = y_ref[...]
        members = observed.shape[0]
        first = batches - observed.shape[1] // nobs
        Y = {b: observed[:, nobs * (b - first) : nobs * (b - first + 1)] for b in range(first, batches)}
        for b in part:
            anomaly, coeff = coefficients(Y[b], value_ref[b : b + 1, :], error_ref[b : b + 1, :])
            anomaly_ref[b - first] = anomaly
            coeff_ref[b - first] = coeff
            after = range(b + 1, batches)
            if after:
                slot = b * batches - b * (b + 1) // 2
                later = jnp.concatenate([Y[e] for e in after], 1)
                spread = later - jnp.sum(later, axis=0, keepdims=True) / members
                taper = jnp.concatenate([taper_ref[slot + i] for i in range(len(after))], 1)
                hi, lo = split2(anomaly)
                fill = -3 * members % 128
                left = jnp.concatenate([hi, lo, hi, jnp.zeros((fill, nobs), bf16)], 0)
                hi, lo = split2(spread)
                blank = jnp.zeros((fill, later.shape[1]), bf16)
                gain = narrow(left, jnp.concatenate([hi, hi, lo, blank], 0), 0, 0)
                gain = gain / (members - 1) * taper
                coeff_hi, coeff_lo = split2(coeff)
                hi, lo = split2(gain)
                left = jnp.concatenate([coeff_hi, coeff_hi, coeff_lo], 1)
                later = later + narrow(left, jnp.concatenate([hi, lo, hi], 0), 1, 0)
                for i, e in enumerate(after):
                    Y[e] = later[:, nobs * i : nobs * (i + 1)]
        for e in range(part[-1] + 1, batches):
            at = e - part[-1] - 1
            later_ref[0][:, nobs * at : nobs * (at + 1)] = Y[e]

    return kernel


def update_kernel(width, comps, batches, members, cols_dev, count, group):
    def kernel(
        place_ref, own_ref, near_a, near_b, far_a, far_b, cx_ref, cy_ref, d_ref,
        taper_ref, *refs,
    ):
        *pair_refs, out_ref, grid_ref = refs
        pairs = [
            (pair_refs[i][k], pair_refs[i + 1][k])
            for i in range(0, len(pair_refs), 2)
            for k in range(pair_refs[i].shape[0])
        ]
        start = pl.multiple_of(place_ref[1] * cols_dev, cols_dev)
        cx = cx_ref[:, pl.ds(start, cols_dev)]
        cy = cy_ref[:, pl.ds(start, cols_dev)]
        d = d_ref[:, pl.ds(start, cols_dev)]
        lane = lax.broadcasted_iota(jnp.int32, (1, cols_dev), 1)
        even = jnp.full((1, cols_dev), place_ref[0] & 1, jnp.int32) == 0
        from_south, from_north = jnp.maximum(cy, 0.0), -jnp.minimum(cy, 0.0)
        from_near = jnp.where(even, from_north, from_south)
        from_far = jnp.where(even, from_south, from_north)
        from_west, from_east = jnp.maximum(cx, 0.0), -jnp.minimum(cx, 0.0)
        for s in range(own_ref.shape[0]):
            middle = near_a.shape[0]
            near_ref, far_ref = (near_a, far_a) if s < middle else (near_b, far_b)
            outer = to_columns(own_ref[s, count:, :])
            for j in range(-(-count // 128)):
                size = min(128, count - 128 * j)
                at = slice(128 * j, 128 * j + size)
                q, near, far = own_ref[s, at, :], near_ref[s % middle, at, :], far_ref[s % middle, at, :]
                west = jnp.where(lane == 0, outer[:size, 2 * j : 2 * j + 1], pltpu.roll(q, 1, 1))
                east = jnp.where(
                    lane == cols_dev - 1,
                    outer[:size, 2 * j + 1 : 2 * j + 2],
                    pltpu.roll(q, cols_dev - 1, 1),
                )
                x = q - from_west * (q - west) - from_east * (q - east)
                x = x - from_near * (q - near) - from_far * (q - far)
                x = x + d * (east + west + near + far - 4.0 * q)
                grid_ref[pl.ds(s * count + 128 * j, size), :] = x
        left, right, tapers = [], [], []
        nobs = taper_ref.shape[1]
        fill = -3 * members % 128
        blank = jnp.zeros((fill, group * cols_dev), bf16)
        for b in range(batches):
            hi, lo = split2(pairs[b][0])
            left.append(jnp.concatenate([hi, lo, hi, jnp.zeros((fill, nobs), bf16)], 0))
            hi, lo = split2(pairs[b][1])
            right.append(jnp.concatenate([hi, hi, lo], 1))
            tapers.append(jnp.tile(taper_ref[b] / (members - 1), (1, group)))
        for first in range(0, comps, group):
            x = jnp.concatenate(
                [grid_ref[pl.ds(first + i, members, comps), :] for i in range(group)], 1
            )
            for b in range(batches):
                spread = x - jnp.sum(x, axis=0, keepdims=True) / members
                hi, lo = split2(spread)
                gain = narrow(left[b], jnp.concatenate([hi, hi, lo, blank], 0), 0, 0) * tapers[b]
                hi, lo = split2(gain)
                x = x + narrow(right[b], jnp.concatenate([hi, lo, hi], 0), 1, 0)
            for i in range(group):
                out_ref[pl.ds(first + i, members, comps), :] = x[:, i * cols_dev : (i + 1) * cols_dev]

    return kernel


def shards(
    prior_sample_array,
    courant_x,
    courant_y,
    diffusion,
    obs_cell,
    obs_value,
    obs_error,
    obs_weight,
    taper_radius,
):
    local, rows_dev, comps, width = prior_sample_array.shape
    blocks = lax.axis_size("mem")
    bands = lax.axis_size("sub")
    cols_dev = width // blocks
    members = local * blocks
    batches, nobs = obs_cell.shape
    count = local * comps
    edge_rows = -(-(2 * -(-count // 128)) // 8) * 8
    assert bands & (bands - 1) == 0 and bands > 1 and rows_dev == 1 and batches == 4 and cols_dev == 128 and nobs == 128
    place = jnp.stack([lax.axis_index("sub"), lax.axis_index("mem")]).astype(jnp.int32)

    share_rows = -(-(local + 2) // 8) * 8
    share, send = call(
        observe_kernel(width, comps, batches, nobs, blocks, edge_rows, local),
        [(share_rows, batches * nobs), (blocks, count + edge_rows, cols_dev)],
        "observe",
        (
            prior_sample_array.reshape(count, width),
            courant_x,
            courant_y,
            diffusion,
            obs_cell,
            obs_weight.transpose(0, 2, 1),
        ),
        (place,),
    )
    grid = lax.all_to_all(send.reshape(blocks, 1, -1), "mem", 0, 0).reshape(send.shape)
    obs_taper, cell_taper = call(
        taper_kernel(width, batches, nobs, cols_dev),
        [(batches * (batches - 1) // 2, nobs, nobs), (batches, nobs, cols_dev)],
        "tapers",
        (obs_cell, taper_radius),
        (place,),
    )
    step = 1
    while step < bands:
        other = lax.ppermute(share, "sub", [(i, i ^ step) for i in range(bands)])
        if step == 1:
            other, obs_taper, cell_taper = lax.optimization_barrier((other, obs_taper, cell_taper))
        last = 2 * step == bands
        (share,) = call(
            join_kernel(local, step == 1, last),
            [(local if last else share_rows, batches * nobs)],
            "join",
            (share, other),
        )
        step *= 2
    share, grid = lax.optimization_barrier((share, grid))
    swap = [(i, i ^ 1) for i in range(bands)]
    onward = [(i, i + 2) for i in range(0, bands - 2, 2)] + [(i, i - 2) for i in range(3, bands, 2)]
    middle = blocks // 2
    near = [lax.ppermute(part, "sub", swap) for part in (grid[:middle], grid[middle:])]
    observed = lax.all_gather(share, "mem")
    pairs, far = [], []
    for b in range(batches):
        part = range(b, b + 1)
        if b == 3:
            observed, far[0] = lax.optimization_barrier((observed, far[0]))
        if b in (1, 2):
            observed, near[b - 1] = lax.optimization_barrier((observed, near[b - 1]))
            far.append(lax.ppermute(near[b - 1], "sub", onward))
        outs = call(
            chain_kernel(part, batches, nobs),
            [(len(part), members, nobs)] * 2
            + [(members, (batches - part[-1] - 1) * nobs)] * (part[-1] + 1 < batches),
            "chain",
            (observed, obs_value, obs_error, obs_taper),
            cost=pl.CostEstimate(flops=1000, bytes_accessed=1000, transcendentals=0),
        )
        pairs += outs[:2]
        observed = outs[-1]
    (out,) = call(
        update_kernel(width, comps, batches, members, cols_dev, count, comps),
        [(members * comps, cols_dev)],
        "update",
        (grid, *near, *far, courant_x, courant_y, diffusion, cell_taper, *pairs),
        (place,),
        (pltpu.VMEM((members * comps, cols_dev), f32),),
    )
    return out.reshape(members, rows_dev, comps, cols_dev)


def solution(mesh):
    return jax.shard_map(
        shards,
        mesh=mesh,
        in_specs=(
            P("mem", "sub", None, None),
            P("sub", None),
            P("sub", None),
            P("sub", None),
            P(),
            P(),
            P(),
            P(),
            P(),
        ),
        out_specs=P(None, "sub", None, "mem"),
        check_vma=False,
    )
```

```python
import jax
import jax.numpy as jnp
from jax import lax
from jax.experimental import pallas as pl
from jax.experimental.pallas import tpu as pltpu
from jax.sharding import PartitionSpec as P

highest = lax.Precision.HIGHEST
f32 = jnp.float32
bf16 = jnp.bfloat16
TILE = (8, 128)


def dot(a, b, ca, cb, precision=highest):
    return lax.dot_general(
        a, b, (((ca,), (cb,)), ((), ())), precision=precision, preferred_element_type=f32
    )


def narrow(a, b, ca, cb):
    return dot(a, b, ca, cb, None)


def split2(x):
    hi = x.astype(bf16)
    return hi, (x - hi.astype(f32)).astype(bf16)


def split3(x):
    hi = x.astype(bf16)
    rest = x - hi.astype(f32)
    mid = rest.astype(bf16)
    return hi, mid, (rest - mid.astype(f32)).astype(bf16)


def call(kernel, out_shapes, name, operands, scalars=(), scratch=(), space=pltpu.VMEM):
    specs = [pl.BlockSpec(memory_space=pltpu.SMEM) for _ in scalars]
    specs += [pl.BlockSpec(memory_space=space) for _ in operands]
    return pl.pallas_call(
        kernel,
        in_specs=specs,
        out_specs=[pl.BlockSpec(memory_space=pltpu.VMEM) for _ in out_shapes],
        out_shape=[jax.ShapeDtypeStruct(s, f32) for s in out_shapes],
        scratch_shapes=list(scratch),
        compiler_params=pltpu.CompilerParams(vmem_limit_bytes=48 * 2**20),
        name=name,
    )(*scalars, *operands)


def rows_cols(cells, width):
    if width & (width - 1) == 0:
        shift = width.bit_length() - 1
        return cells >> shift, cells & (width - 1)
    return cells // width, cells % width


def to_columns(rows):
    n = rows.shape[0]
    return jnp.concatenate([rows, jnp.zeros((128 - n, 128), f32)], 0).T


def gaspari(delta_row, delta_col, cutoff_radius, width):
    half = width // 2
    folded = jnp.where(delta_col >= half, delta_col - width, delta_col)
    folded = jnp.where(delta_col < -half, delta_col + width, folded)
    ratio = jnp.sqrt(delta_row * delta_row + folded * folded) / cutoff_radius
    inner = (((-0.25 * ratio + 0.5) * ratio + 0.625) * ratio - 5.0 / 3.0) * ratio * ratio + 1.0
    bounded = jnp.maximum(ratio, 1.0)
    outer = (
        ((((ratio / 12.0 - 0.5) * ratio + 0.625) * ratio + 5.0 / 3.0) * ratio - 5.0) * ratio
        + 4.0
        - 2.0 / (3.0 * bounded)
    )
    return jnp.where(ratio <= 1.0, inner, jnp.where(ratio < 2.0, outer, 0.0))


def taper_kernel(width, batches, nobs, cols_dev):
    def kernel(place_ref, cell_ref, radius_ref, obs_taper_ref, cell_taper_ref):
        row_here = place_ref[0].astype(f32)
        col_here = place_ref[1] * cols_dev
        row_i, col_i = rows_cols(cell_ref[...], width)
        rows = row_i.astype(f32)
        cols = col_i.astype(f32)
        table = to_columns(jnp.concatenate([rows, cols, radius_ref[...]], 0))
        lane = lax.broadcasted_iota(jnp.int32, (1, cols_dev), 1)
        cell_cols = (lane + col_here).astype(f32)
        slot = 0
        for b in range(batches):
            row_j = table[:, b : b + 1]
            col_j = table[:, batches + b : batches + b + 1]
            radius = table[:, 2 * batches + b : 2 * batches + b + 1]
            cell_taper_ref[b] = gaspari(row_here - row_j, cell_cols - col_j, radius, width)
            for e in range(b + 1, batches):
                obs_taper_ref[slot] = gaspari(
                    rows[e : e + 1, :] - row_j, cols[e : e + 1, :] - col_j, radius, width
                )
                slot += 1

    return kernel


def share_kernel(width, comps, batches, nobs, local):
    def kernel(place_ref, *refs):
        sources, (share_ref, *fetched, arrived) = refs[:6], refs[6:]
        q_ref, cx_ref, cy_ref, d_ref, cell_ref, weight_ref = fetched
        copies = [
            pltpu.make_async_copy(source, target, arrived.at[i])
            for i, (source, target) in enumerate(zip(sources, fetched))
        ]
        for copy in copies:
            copy.start()
        here = place_ref[0]
        for copy in copies[1:]:
            copy.wait()
        cx, cy, d = cx_ref[...], cy_ref[...], d_ref[...]
        from_south, from_north = jnp.maximum(cy, 0.0) + d, d - jnp.minimum(cy, 0.0)
        even = jnp.full((1, width), here & 1, jnp.int32) == 0
        near = jnp.where(even, from_north, from_south)
        far = jnp.where(even, from_south, from_north)
        scales = [part.astype(f32) for part in split3(jnp.concatenate([near, far], 0))]
        scales = jnp.concatenate(scales + [jnp.zeros((10, width), f32)], 0).astype(bf16)
        row, col = rows_cols(cell_ref[...], width)
        row = jnp.concatenate([row[b : b + 1] for b in range(batches)], 1)
        col = jnp.concatenate([col[b : b + 1] for b in range(batches)], 1)
        away = row - here
        owned, beside = away == 0, (away == 1) | (away == -1)
        place = lax.broadcasted_iota(jnp.int32, (width, batches * nobs), 0)
        own_pick = (place == jnp.where(owned, col, -1)).astype(f32).astype(bf16)
        raw_pick = (place == jnp.where(beside, col, -1)).astype(f32).astype(bf16)
        copies[0].wait()
        q = q_ref[...]
        west = pltpu.roll(q, 1, 1)
        east = pltpu.roll(q, width - 1, 1)
        mine = q - jnp.maximum(cx, 0.0) * (q - west) - jnp.minimum(cx, 0.0) * (east - q)
        mine = mine - jnp.maximum(cy, 0.0) * q + jnp.minimum(cy, 0.0) * q
        mine = mine + d * (east + west - 4.0 * q)
        value = narrow(
            jnp.concatenate(split2(mine) + split2(q), 1),
            jnp.concatenate([own_pick, own_pick, raw_pick, raw_pick], 0),
            1,
            0,
        )
        weight = jnp.concatenate([weight_ref[b] for b in range(batches)], 1)
        value = jnp.sum(value.reshape(-1, comps, batches * nobs) * weight[None], axis=1)
        scale = narrow(scales, own_pick, 1, 0)
        scale = scale[0:2] + scale[2:4] + scale[4:6]
        share = [value, jnp.where(owned, scale, 1.0)]
        fill = share_ref.shape[0] - local - 2
        if fill:
            share.append(jnp.zeros((fill, batches * nobs), f32))
        share_ref[...] = jnp.concatenate(share, 0)

    return kernel


def send_kernel(width, blocks, edge_rows):
    def kernel(q_ref, send_ref):
        q = q_ref[...]
        count = q.shape[0]
        q_parts = split3(q)
        cols_dev = width // blocks
        lanes = -(-2 * blocks // 128) * 128
        which = lax.broadcasted_iota(jnp.int32, (width, lanes), 1)
        spot = lax.broadcasted_iota(jnp.int32, (width, lanes), 0)
        start = (which >> 1) * cols_dev
        wanted = jnp.where(which & 1 == 0, start - 1, start + cols_dev)
        wanted = jnp.where(wanted < 0, wanted + width, wanted)
        wanted = jnp.where(wanted == width, 0, wanted)
        pick = (spot == wanted).astype(f32).astype(bf16)
        edges = narrow(
            jnp.concatenate(q_parts, 1), jnp.concatenate([pick, pick, pick], 0), 1, 0
        )
        room = -count % 128
        if room:
            edges = jnp.concatenate([edges, jnp.zeros((room, lanes), f32)], 0)
        edges = edges.T
        chunks = -(-count // 128)
        for i in range(blocks):
            at = slice(i * cols_dev, (i + 1) * cols_dev)
            send_ref[i, :count, :] = q[:, at]
            rows = [edges[2 * i : 2 * i + 2, j * 128 : (j + 1) * 128] for j in range(chunks)]
            if edge_rows > 2 * chunks:
                rows.append(jnp.zeros((edge_rows - 2 * chunks, 128), f32))
            send_ref[i, count:, :] = jnp.concatenate(rows, 0)

    return kernel


def join_kernel(local, first, last):
    def kernel(mine_ref, other_ref, out_ref):
        mine, other = mine_ref[...], other_ref[...]
        at = local
        value = mine[:local] * other[at : at + 1] + other[:local] * mine[at : at + 1]
        if last:
            out_ref[...] = value
        else:
            at = local + 1 if first else local
            scale = mine[at : at + 1] * other[at : at + 1]
            blank = jnp.zeros((out_ref.shape[0] - local - 1, value.shape[1]), f32)
            out_ref[...] = jnp.concatenate([value, scale, blank], 0)

    return kernel


def lane_spread(x, j):
    return jnp.take_along_axis(x, jnp.full(x.shape, j, jnp.int32), axis=1)


def row_spread(x, i):
    return jnp.broadcast_to(x[i : i + 1, :], x.shape)


def factored(cov, sides, error, members, span=4):
    tiles = cov.shape[0] // 8
    lane = lax.broadcasted_iota(jnp.int32, TILE, 1)
    sub = lax.broadcasted_iota(jnp.int32, TILE, 0)
    T = [cov[8 * q : 8 * q + 8, :] for q in range(tiles)]
    V = [sides[8 * q : 8 * q + 8, :] for q in range(tiles)]
    deviation = jnp.broadcast_to(jnp.sqrt(error), TILE)
    is_member = lane < members
    inverse, solved, finished = [], [], []
    for p in range(tiles):
        block = (lane >= 8 * p) & (lane < 8 * p + 8)
        columns = [lane_spread(T[p], 8 * p + c) for c in range(8)]
        s = [[row_spread(columns[c], a) if a >= c else None for c in range(8)] for a in range(8)]
        joined = jnp.where(block, (lane - 8 * p == sub).astype(f32), T[p])
        R = [row_spread(joined, c) for c in range(8)]
        Z = [row_spread(V[p], c) for c in range(8)]
        rd, rs = [None] * 8, [None] * 8
        m = [[None] * 8 for _ in range(8)]
        for c in range(8):
            rd[c] = 1.0 / s[c][c]
            rs[c] = lax.rsqrt(s[c][c])
            root = s[c][c] * rs[c]
            spread = lane_spread(deviation, 8 * p + c)
            Z[c] = Z[c] * jnp.where(is_member, root / (root + spread), 1.0)
            for a in range(c + 1, 8):
                m[a][c] = s[a][c] * rd[c]
            for a in range(c + 1, 8):
                for e in range(c + 1, a + 1):
                    s[a][e] = s[a][e] - (s[a][c] * s[e][c]) * rd[c]
                R[a] = R[a] - m[a][c] * R[c]
                Z[a] = Z[a] - m[a][c] * Z[c]
        X, U = [None] * 8, [None] * 8
        for a in range(7, -1, -1):
            x, u = rd[a] * R[a], rd[a] * Z[a]
            for c in range(a + 1, 8):
                x = x - m[c][a] * X[c]
                u = u - m[c][a] * U[c]
            X[a], U[a] = x, u
        low, side = R[0] * rs[0], Z[0] * rs[0]
        for c in range(1, 8):
            low = jnp.where(sub == c, R[c] * rs[c], low)
            side = jnp.where(sub == c, Z[c] * rs[c], side)
        inverse.append(jnp.where(lane < 8 * p + 8, low, 0.0))
        solved.append(side)
        finished.append((low, side))
        edge = (p // span + 1) * span
        for q in range(p + 1, edge):
            t, v = jnp.where(block, 0.0, T[q]), V[q]
            for c in range(8):
                column = lane_spread(T[q], 8 * p + c)
                t = t - column * X[c]
                v = v - column * U[c]
            T[q], V[q] = t, v
        if p + 1 == edge and edge < tiles:
            rows = finished[edge - span : edge]
            upper = jnp.concatenate([low for low, _ in rows], 0)
            keep = [
                jnp.where((lane < 8 * (edge - span + i + 1)) | (lane >= 8 * edge), low, 0.0)
                for i, (low, _) in enumerate(rows)
            ]
            side_rows = jnp.concatenate([side for _, side in rows], 0)
            taken = products(upper, jnp.concatenate([jnp.concatenate(keep, 0), side_rows], 1))
            inside = (lane >= 8 * (edge - span)) & (lane < 8 * edge)
            for q in range(edge, tiles):
                at = slice(8 * q, 8 * q + 8)
                T[q] = jnp.where(inside, 0.0, T[q]) - taken[at, :128]
                V[q] = V[q] - taken[at, 128:]
    return jnp.concatenate(inverse, 0), jnp.concatenate(solved, 0)


def products(a, b):
    ah, am, al = split3(a)
    bh, bm, bl = split3(b)
    return narrow(
        jnp.concatenate([al, am, ah, am, ah, ah], 0),
        jnp.concatenate([bh, bm, bl, bh, bm, bh], 0),
        0,
        0,
    )


def coefficients(observed, value, error):
    members, nobs = observed.shape
    mean = jnp.sum(observed, axis=0, keepdims=True) / members
    anomaly = observed - mean
    row = lax.broadcasted_iota(jnp.int32, (nobs, nobs), 0)
    col = lax.broadcasted_iota(jnp.int32, (nobs, nobs), 1)
    cov = products(anomaly, anomaly) / (members - 1) + jnp.where(row == col, error, 0.0)
    sides = jnp.concatenate(
        [anomaly, value - mean, jnp.zeros((nobs - members - 1, nobs), f32)], 0
    ).T
    inverse, solved = factored(cov, sides, error, members)
    back = products(solved, inverse)
    return anomaly, back[members : members + 1] - back[:members]


def chain_kernel(part, batches, nobs, pieces):
    def kernel(place_ref, *refs):
        y_refs, refs = refs[:pieces], refs[pieces:]
        value_ref, error_ref, taper_ref, anomaly_ref, coeff_ref, *later_ref = refs
        blocks = [ref[...] for ref in y_refs]
        step = 1
        while step < pieces:
            odd = jnp.full(blocks[0].shape, place_ref[1] & step, jnp.int32) != 0
            blocks = [jnp.where(odd, blocks[k ^ step], blocks[k]) for k in range(pieces)]
            step *= 2
        observed = jnp.concatenate(blocks, 0) if pieces > 1 else blocks[0]
        members = observed.shape[0]
        first = batches - observed.shape[1] // nobs
        Y = {b: observed[:, nobs * (b - first) : nobs * (b - first + 1)] for b in range(first, batches)}
        for b in part:
            anomaly, coeff = coefficients(Y[b], value_ref[b : b + 1, :], error_ref[b : b + 1, :])
            anomaly_ref[b - first] = anomaly
            coeff_ref[b - first] = coeff
            after = range(b + 1, batches)
            if after:
                slot = b * batches - b * (b + 1) // 2
                later = jnp.concatenate([Y[e] for e in after], 1)
                spread = later - jnp.sum(later, axis=0, keepdims=True) / members
                taper = jnp.concatenate([taper_ref[slot + i] for i in range(len(after))], 1)
                hi, lo = split2(anomaly)
                fill = -3 * members % 128
                left = jnp.concatenate([hi, lo, hi, jnp.zeros((fill, nobs), bf16)], 0)
                hi, lo = split2(spread)
                blank = jnp.zeros((fill, later.shape[1]), bf16)
                gain = narrow(left, jnp.concatenate([hi, hi, lo, blank], 0), 0, 0)
                gain = gain / (members - 1) * taper
                coeff_hi, coeff_lo = split2(coeff)
                hi, lo = split2(gain)
                left = jnp.concatenate([coeff_hi, coeff_hi, coeff_lo], 1)
                later = later + narrow(left, jnp.concatenate([hi, lo, hi], 0), 1, 0)
                for i, e in enumerate(after):
                    Y[e] = later[:, nobs * i : nobs * (i + 1)]
        for e in range(part[-1] + 1, batches):
            at = e - part[-1] - 1
            later_ref[0][:, nobs * at : nobs * (at + 1)] = Y[e]

    return kernel


def update_kernel(width, comps, batches, members, cols_dev, count, group):
    def kernel(
        place_ref, own_ref, near_a, near_b, far_a, far_b, cx_ref, cy_ref, d_ref,
        taper_ref, *refs,
    ):
        *pair_refs, out_ref, grid_ref = refs
        pairs = [
            (pair_refs[i][k], pair_refs[i + 1][k])
            for i in range(0, len(pair_refs), 2)
            for k in range(pair_refs[i].shape[0])
        ]
        start = pl.multiple_of(place_ref[1] * cols_dev, cols_dev)
        cx = cx_ref[:, pl.ds(start, cols_dev)]
        cy = cy_ref[:, pl.ds(start, cols_dev)]
        d = d_ref[:, pl.ds(start, cols_dev)]
        lane = lax.broadcasted_iota(jnp.int32, (1, cols_dev), 1)
        even = jnp.full((1, cols_dev), place_ref[0] & 1, jnp.int32) == 0
        from_south, from_north = jnp.maximum(cy, 0.0), -jnp.minimum(cy, 0.0)
        from_near = jnp.where(even, from_north, from_south)
        from_far = jnp.where(even, from_south, from_north)
        from_west, from_east = jnp.maximum(cx, 0.0), -jnp.minimum(cx, 0.0)
        for s in range(own_ref.shape[0]):
            middle = near_a.shape[0]
            near_ref, far_ref = (near_a, far_a) if s < middle else (near_b, far_b)
            outer = to_columns(own_ref[s, count:, :])
            for j in range(-(-count // 128)):
                size = min(128, count - 128 * j)
                at = slice(128 * j, 128 * j + size)
                q, near, far = own_ref[s, at, :], near_ref[s % middle, at, :], far_ref[s % middle, at, :]
                west = jnp.where(lane == 0, outer[:size, 2 * j : 2 * j + 1], pltpu.roll(q, 1, 1))
                east = jnp.where(
                    lane == cols_dev - 1,
                    outer[:size, 2 * j + 1 : 2 * j + 2],
                    pltpu.roll(q, cols_dev - 1, 1),
                )
                x = q - from_west * (q - west) - from_east * (q - east)
                x = x - from_near * (q - near) - from_far * (q - far)
                x = x + d * (east + west + near + far - 4.0 * q)
                grid_ref[pl.ds(s * count + 128 * j, size), :] = x
        left, right, tapers = [], [], []
        nobs = taper_ref.shape[1]
        fill = -3 * members % 128
        blank = jnp.zeros((fill, group * cols_dev), bf16)
        for b in range(batches):
            hi, lo = split2(pairs[b][0])
            left.append(jnp.concatenate([hi, lo, hi, jnp.zeros((fill, nobs), bf16)], 0))
            hi, lo = split2(pairs[b][1])
            right.append(jnp.concatenate([hi, hi, lo], 1))
            tapers.append(jnp.tile(taper_ref[b] / (members - 1), (1, group)))
        for first in range(0, comps, group):
            x = jnp.concatenate(
                [grid_ref[pl.ds(first + i, members, comps), :] for i in range(group)], 1
            )
            for b in range(batches):
                spread = x - jnp.sum(x, axis=0, keepdims=True) / members
                hi, lo = split2(spread)
                gain = narrow(left[b], jnp.concatenate([hi, hi, lo, blank], 0), 0, 0) * tapers[b]
                hi, lo = split2(gain)
                x = x + narrow(right[b], jnp.concatenate([hi, lo, hi], 0), 1, 0)
            for i in range(group):
                out_ref[pl.ds(first + i, members, comps), :] = x[:, i * cols_dev : (i + 1) * cols_dev]

    return kernel


def shards(
    prior_sample_array,
    courant_x,
    courant_y,
    diffusion,
    obs_cell,
    obs_value,
    obs_error,
    obs_weight,
    taper_radius,
):
    local, rows_dev, comps, width = prior_sample_array.shape
    blocks = lax.axis_size("mem")
    bands = lax.axis_size("sub")
    cols_dev = width // blocks
    members = local * blocks
    batches, nobs = obs_cell.shape
    count = local * comps
    edge_rows = -(-(2 * -(-count // 128)) // 8) * 8
    assert bands & (bands - 1) == 0 and bands > 2 and blocks & (blocks - 1) == 0 and rows_dev == 1 and batches == 4 and cols_dev == 128 and nobs == 128
    place = jnp.stack([lax.axis_index("sub"), lax.axis_index("mem")]).astype(jnp.int32)

    share_rows = -(-(local + 2) // 8) * 8
    prior = prior_sample_array.reshape(count, width)
    (send,) = call(
        send_kernel(width, blocks, edge_rows),
        [(blocks, count + edge_rows, cols_dev)],
        "send",
        (prior,),
    )
    grid = lax.all_to_all(send.reshape(blocks, 1, -1), "mem", 0, 0).reshape(send.shape)
    sources = (prior, courant_x, courant_y, diffusion, obs_cell, obs_weight.transpose(0, 2, 1))
    (place, send) = lax.optimization_barrier((place, send))
    (share,) = call(
        share_kernel(width, comps, batches, nobs, local),
        [(share_rows, batches * nobs)],
        "share",
        sources,
        (place,),
        [pltpu.VMEM(x.shape, x.dtype) for x in sources] + [pltpu.SemaphoreType.DMA((6,))],
        pl.ANY,
    )
    obs_taper, cell_taper = call(
        taper_kernel(width, batches, nobs, cols_dev),
        [(batches * (batches - 1) // 2, nobs, nobs), (batches, nobs, cols_dev)],
        "tapers",
        (obs_cell, taper_radius),
        (place,),
    )
    step = 1
    while step < bands:
        other = lax.ppermute(share, "sub", [(i, i ^ step) for i in range(bands)])
        if step == 1:
            other, obs_taper, cell_taper = lax.optimization_barrier((other, obs_taper, cell_taper))
        last = 2 * step == bands
        (share,) = call(
            join_kernel(local, step == 1, last),
            [(local if last else share_rows, batches * nobs)],
            "join",
            (share, other),
        )
        if 4 * step == bands:
            share, grid = lax.optimization_barrier((share, grid))
        step *= 2
    swap = [(i, i ^ 1) for i in range(bands)]
    onward = [(i, i + 2) for i in range(0, bands - 2, 2)] + [(i, i - 2) for i in range(3, bands, 2)]
    middle = blocks // 2
    near = [lax.ppermute(part, "sub", swap) for part in (grid[:middle], grid[middle:])]
    observed = {0: share}
    step = blocks // 2
    while step:
        to = [(i, i ^ step) for i in range(blocks)]
        observed.update({k ^ step: lax.ppermute(x, "mem", to) for k, x in observed.items()})
        step //= 2
    observed = [observed[k] for k in range(blocks)]
    pairs, far = [], []
    for b in range(batches):
        part = range(b, b + 1)
        if b == 2:
            *observed, far[0] = lax.optimization_barrier((*observed, far[0]))
        if b < 2:
            *observed, near[b] = lax.optimization_barrier((*observed, near[b]))
            far.append(lax.ppermute(near[b], "sub", onward))
        outs = call(
            chain_kernel(part, batches, nobs, len(observed)),
            [(len(part), members, nobs)] * 2
            + [(members, (batches - part[-1] - 1) * nobs)] * (part[-1] + 1 < batches),
            "chain",
            (*observed, obs_value, obs_error, obs_taper),
            (place,),
        )
        pairs += outs[:2]
        observed = outs[2:]
    (out,) = call(
        update_kernel(width, comps, batches, members, cols_dev, count, comps),
        [(members * comps, cols_dev)],
        "update",
        (grid, *near, *far, courant_x, courant_y, diffusion, cell_taper, *pairs),
        (place,),
        (pltpu.VMEM((members * comps, cols_dev), f32),),
    )
    return out.reshape(members, rows_dev, comps, cols_dev)


def solution(mesh):
    return jax.shard_map(
        shards,
        mesh=mesh,
        in_specs=(
            P("mem", "sub", None, None),
            P("sub", None),
            P("sub", None),
            P("sub", None),
            P(),
            P(),
            P(),
            P(),
            P(),
        ),
        out_specs=P(None, "sub", None, "mem"),
        check_vma=False,
    )
```

```python
import jax
import jax.numpy as jnp
from jax import lax
from jax.experimental import pallas as pl
from jax.experimental.pallas import tpu as pltpu
from jax.sharding import PartitionSpec as P

highest = lax.Precision.HIGHEST
f32 = jnp.float32
bf16 = jnp.bfloat16
TILE = (8, 128)


def dot(a, b, ca, cb, precision=highest):
    return lax.dot_general(
        a, b, (((ca,), (cb,)), ((), ())), precision=precision, preferred_element_type=f32
    )


def narrow(a, b, ca, cb):
    return dot(a, b, ca, cb, None)


def split2(x):
    hi = x.astype(bf16)
    return hi, (x - hi.astype(f32)).astype(bf16)


def split3(x):
    hi = x.astype(bf16)
    rest = x - hi.astype(f32)
    mid = rest.astype(bf16)
    return hi, mid, (rest - mid.astype(f32)).astype(bf16)


def call(kernel, out_shapes, name, operands, scratch=(), space=pltpu.VMEM):
    specs = [pl.BlockSpec(memory_space=space) for _ in operands]
    return pl.pallas_call(
        kernel,
        in_specs=specs,
        out_specs=[pl.BlockSpec(memory_space=pltpu.VMEM) for _ in out_shapes],
        out_shape=[jax.ShapeDtypeStruct(s, f32) for s in out_shapes],
        scratch_shapes=list(scratch),
        compiler_params=pltpu.CompilerParams(vmem_limit_bytes=48 * 2**20),
        name=name,
    )(*operands)


def rows_cols(cells, width):
    if width & (width - 1) == 0:
        shift = width.bit_length() - 1
        return cells >> shift, cells & (width - 1)
    return cells // width, cells % width


def to_columns(rows):
    n = rows.shape[0]
    return jnp.concatenate([rows, jnp.zeros((128 - n, 128), f32)], 0).T


def gaspari(delta_row, delta_col, cutoff_radius, width):
    half = width // 2
    folded = jnp.where(delta_col >= half, delta_col - width, delta_col)
    folded = jnp.where(delta_col < -half, delta_col + width, folded)
    ratio = jnp.sqrt(delta_row * delta_row + folded * folded) / cutoff_radius
    inner = (((-0.25 * ratio + 0.5) * ratio + 0.625) * ratio - 5.0 / 3.0) * ratio * ratio + 1.0
    bounded = jnp.maximum(ratio, 1.0)
    outer = (
        ((((ratio / 12.0 - 0.5) * ratio + 0.625) * ratio + 5.0 / 3.0) * ratio - 5.0) * ratio
        + 4.0
        - 2.0 / (3.0 * bounded)
    )
    return jnp.where(ratio <= 1.0, inner, jnp.where(ratio < 2.0, outer, 0.0))


def taper_kernel(width, batches, nobs, cols_dev):
    def kernel(cell_ref, radius_ref, obs_taper_ref, cell_taper_ref):
        row_here = lax.axis_index("sub").astype(f32)
        col_here = lax.axis_index("mem") * cols_dev
        row_i, col_i = rows_cols(cell_ref[...], width)
        rows = row_i.astype(f32)
        cols = col_i.astype(f32)
        table = to_columns(jnp.concatenate([rows, cols, radius_ref[...]], 0))
        lane = lax.broadcasted_iota(jnp.int32, (1, cols_dev), 1)
        cell_cols = (lane + col_here).astype(f32)
        slot = 0
        for b in range(batches):
            row_j = table[:, b : b + 1]
            col_j = table[:, batches + b : batches + b + 1]
            radius = table[:, 2 * batches + b : 2 * batches + b + 1]
            cell_taper_ref[b] = gaspari(row_here - row_j, cell_cols - col_j, radius, width)
            for e in range(b + 1, batches):
                obs_taper_ref[slot] = gaspari(
                    rows[e : e + 1, :] - row_j, cols[e : e + 1, :] - col_j, radius, width
                )
                slot += 1

    return kernel


def share_kernel(width, comps, batches, nobs, local):
    def kernel(*refs):
        sources, (share_ref, *fetched, arrived) = refs[:6], refs[6:]
        q_ref, cx_ref, cy_ref, d_ref, cell_ref, weight_ref = fetched
        copies = [
            pltpu.make_async_copy(source, target, arrived.at[i])
            for i, (source, target) in enumerate(zip(sources, fetched))
        ]
        for copy in copies:
            copy.start()
        here = lax.axis_index("sub")
        for copy in copies[1:]:
            copy.wait()
        cx, cy, d = cx_ref[...], cy_ref[...], d_ref[...]
        from_south, from_north = jnp.maximum(cy, 0.0) + d, d - jnp.minimum(cy, 0.0)
        even = jnp.full((1, width), here & 1, jnp.int32) == 0
        near = jnp.where(even, from_north, from_south)
        far = jnp.where(even, from_south, from_north)
        scales = [part.astype(f32) for part in split3(jnp.concatenate([near, far], 0))]
        scales = jnp.concatenate(scales + [jnp.zeros((10, width), f32)], 0).astype(bf16)
        row, col = rows_cols(cell_ref[...], width)
        row = jnp.concatenate([row[b : b + 1] for b in range(batches)], 1)
        col = jnp.concatenate([col[b : b + 1] for b in range(batches)], 1)
        away = row - here
        owned, beside = away == 0, (away == 1) | (away == -1)
        place = lax.broadcasted_iota(jnp.int32, (width, batches * nobs), 0)
        own_pick = (place == jnp.where(owned, col, -1)).astype(f32).astype(bf16)
        raw_pick = (place == jnp.where(beside, col, -1)).astype(f32).astype(bf16)
        copies[0].wait()
        q = q_ref[...]
        west = pltpu.roll(q, 1, 1)
        east = pltpu.roll(q, width - 1, 1)
        mine = q - jnp.maximum(cx, 0.0) * (q - west) - jnp.minimum(cx, 0.0) * (east - q)
        mine = mine - jnp.maximum(cy, 0.0) * q + jnp.minimum(cy, 0.0) * q
        mine = mine + d * (east + west - 4.0 * q)
        value = narrow(
            jnp.concatenate(split2(mine) + split2(q), 1),
            jnp.concatenate([own_pick, own_pick, raw_pick, raw_pick], 0),
            1,
            0,
        )
        weight = jnp.concatenate([weight_ref[b] for b in range(batches)], 1)
        value = jnp.sum(value.reshape(-1, comps, batches * nobs) * weight[None], axis=1)
        scale = narrow(scales, own_pick, 1, 0)
        scale = scale[0:2] + scale[2:4] + scale[4:6]
        share = [value, jnp.where(owned, scale, 1.0)]
        fill = share_ref.shape[0] - local - 2
        if fill:
            share.append(jnp.zeros((fill, batches * nobs), f32))
        share_ref[...] = jnp.concatenate(share, 0)

    return kernel


def send_kernel(width, blocks, edge_rows):
    def kernel(q_ref, send_ref):
        q = q_ref[...]
        count = q.shape[0]
        q_parts = split3(q)
        cols_dev = width // blocks
        lanes = -(-2 * blocks // 128) * 128
        which = lax.broadcasted_iota(jnp.int32, (width, lanes), 1)
        spot = lax.broadcasted_iota(jnp.int32, (width, lanes), 0)
        start = (which >> 1) * cols_dev
        wanted = jnp.where(which & 1 == 0, start - 1, start + cols_dev)
        wanted = jnp.where(wanted < 0, wanted + width, wanted)
        wanted = jnp.where(wanted == width, 0, wanted)
        pick = (spot == wanted).astype(f32).astype(bf16)
        edges = narrow(
            jnp.concatenate(q_parts, 1), jnp.concatenate([pick, pick, pick], 0), 1, 0
        )
        room = -count % 128
        if room:
            edges = jnp.concatenate([edges, jnp.zeros((room, lanes), f32)], 0)
        edges = edges.T
        chunks = -(-count // 128)
        for i in range(blocks):
            at = slice(i * cols_dev, (i + 1) * cols_dev)
            send_ref[i, :count, :] = q[:, at]
            rows = [edges[2 * i : 2 * i + 2, j * 128 : (j + 1) * 128] for j in range(chunks)]
            if edge_rows > 2 * chunks:
                rows.append(jnp.zeros((edge_rows - 2 * chunks, 128), f32))
            send_ref[i, count:, :] = jnp.concatenate(rows, 0)

    return kernel


def join_kernel(local, first, last):
    def kernel(mine_ref, other_ref, out_ref):
        mine, other = mine_ref[...], other_ref[...]
        at = local
        value = mine[:local] * other[at : at + 1] + other[:local] * mine[at : at + 1]
        if last:
            out_ref[...] = value
        else:
            at = local + 1 if first else local
            scale = mine[at : at + 1] * other[at : at + 1]
            blank = jnp.zeros((out_ref.shape[0] - local - 1, value.shape[1]), f32)
            out_ref[...] = jnp.concatenate([value, scale, blank], 0)

    return kernel


def lane_spread(x, j):
    return jnp.take_along_axis(x, jnp.full(x.shape, j, jnp.int32), axis=1)


def row_spread(x, i):
    return jnp.broadcast_to(x[i : i + 1, :], x.shape)


def factored(cov, sides, error, members, span=4):
    tiles = cov.shape[0] // 8
    lane = lax.broadcasted_iota(jnp.int32, TILE, 1)
    sub = lax.broadcasted_iota(jnp.int32, TILE, 0)
    T = [cov[8 * q : 8 * q + 8, :] for q in range(tiles)]
    V = [sides[8 * q : 8 * q + 8, :] for q in range(tiles)]
    deviation = jnp.broadcast_to(jnp.sqrt(error), TILE)
    is_member = lane < members
    inverse, solved, finished = [], [], []
    for p in range(tiles):
        block = (lane >= 8 * p) & (lane < 8 * p + 8)
        columns = [lane_spread(T[p], 8 * p + c) for c in range(8)]
        s = [[row_spread(columns[c], a) if a >= c else None for c in range(8)] for a in range(8)]
        joined = jnp.where(block, (lane - 8 * p == sub).astype(f32), T[p])
        R = [row_spread(joined, c) for c in range(8)]
        Z = [row_spread(V[p], c) for c in range(8)]
        rd, rs = [None] * 8, [None] * 8
        m = [[None] * 8 for _ in range(8)]
        for c in range(8):
            rd[c] = 1.0 / s[c][c]
            rs[c] = lax.rsqrt(s[c][c])
            root = s[c][c] * rs[c]
            spread = lane_spread(deviation, 8 * p + c)
            Z[c] = Z[c] * jnp.where(is_member, root / (root + spread), 1.0)
            for a in range(c + 1, 8):
                m[a][c] = s[a][c] * rd[c]
            for a in range(c + 1, 8):
                for e in range(c + 1, a + 1):
                    s[a][e] = s[a][e] - (s[a][c] * s[e][c]) * rd[c]
                R[a] = R[a] - m[a][c] * R[c]
                Z[a] = Z[a] - m[a][c] * Z[c]
        X, U = [None] * 8, [None] * 8
        for a in range(7, -1, -1):
            x, u = rd[a] * R[a], rd[a] * Z[a]
            for c in range(a + 1, 8):
                x = x - m[c][a] * X[c]
                u = u - m[c][a] * U[c]
            X[a], U[a] = x, u
        low, side = R[0] * rs[0], Z[0] * rs[0]
        for c in range(1, 8):
            low = jnp.where(sub == c, R[c] * rs[c], low)
            side = jnp.where(sub == c, Z[c] * rs[c], side)
        inverse.append(jnp.where(lane < 8 * p + 8, low, 0.0))
        solved.append(side)
        finished.append((low, side))
        edge = (p // span + 1) * span
        for q in range(p + 1, edge):
            column = [lane_spread(T[q], 8 * p + c) for c in range(8)]
            left, right = X, U
            if q == p + 1:
                for c in range(8):
                    for a in range(c):
                        column[c] = column[c] - m[c][a] * column[a]
                column = [column[c] * rd[c] for c in range(8)]
                left, right = R, Z
            t, v = jnp.where(block, 0.0, T[q]), V[q]
            for c in range(8):
                t = t - column[c] * left[c]
                v = v - column[c] * right[c]
            T[q], V[q] = t, v
        if p + 1 == edge and edge < tiles:
            rows = finished[edge - span : edge]
            upper = jnp.concatenate([low for low, _ in rows], 0)
            keep = [
                jnp.where((lane < 8 * (edge - span + i + 1)) | (lane >= 8 * edge), low, 0.0)
                for i, (low, _) in enumerate(rows)
            ]
            side_rows = jnp.concatenate([side for _, side in rows], 0)
            taken = products(upper, jnp.concatenate([jnp.concatenate(keep, 0), side_rows], 1))
            inside = (lane >= 8 * (edge - span)) & (lane < 8 * edge)
            for q in range(edge, tiles):
                at = slice(8 * q, 8 * q + 8)
                T[q] = jnp.where(inside, 0.0, T[q]) - taken[at, :128]
                V[q] = V[q] - taken[at, 128:]
    return jnp.concatenate(inverse, 0), jnp.concatenate(solved, 0)


def products(a, b):
    ah, am, al = split3(a)
    bh, bm, bl = split3(b)
    return narrow(
        jnp.concatenate([al, am, ah, am, ah, ah], 0),
        jnp.concatenate([bh, bm, bl, bh, bm, bh], 0),
        0,
        0,
    )


def coefficients(observed, value, error):
    members, nobs = observed.shape
    mean = jnp.sum(observed, axis=0, keepdims=True) / members
    anomaly = observed - mean
    row = lax.broadcasted_iota(jnp.int32, (nobs, nobs), 0)
    col = lax.broadcasted_iota(jnp.int32, (nobs, nobs), 1)
    cov = products(anomaly, anomaly) / (members - 1) + jnp.where(row == col, error, 0.0)
    sides = jnp.concatenate(
        [anomaly, value - mean, jnp.zeros((nobs - members - 1, nobs), f32)], 0
    ).T
    inverse, solved = factored(cov, sides, error, members)
    back = products(solved, inverse)
    return anomaly, back[members : members + 1] - back[:members]


def chain_kernel(part, batches, nobs, pieces):
    def kernel(*refs):
        y_refs, refs = refs[:pieces], refs[pieces:]
        value_ref, error_ref, taper_ref, anomaly_ref, coeff_ref, *later_ref = refs
        blocks = [ref[...] for ref in y_refs]
        step = 1
        while step < pieces:
            odd = jnp.full(blocks[0].shape, lax.axis_index("mem") & step, jnp.int32) != 0
            blocks = [jnp.where(odd, blocks[k ^ step], blocks[k]) for k in range(pieces)]
            step *= 2
        observed = jnp.concatenate(blocks, 0) if pieces > 1 else blocks[0]
        members = observed.shape[0]
        first = batches - observed.shape[1] // nobs
        Y = {b: observed[:, nobs * (b - first) : nobs * (b - first + 1)] for b in range(first, batches)}
        for b in part:
            anomaly, coeff = coefficients(Y[b], value_ref[b : b + 1, :], error_ref[b : b + 1, :])
            anomaly_ref[b - first] = anomaly
            coeff_ref[b - first] = coeff
            after = range(b + 1, batches)
            if after:
                slot = b * batches - b * (b + 1) // 2
                later = jnp.concatenate([Y[e] for e in after], 1)
                spread = later - jnp.sum(later, axis=0, keepdims=True) / members
                taper = jnp.concatenate([taper_ref[slot + i] for i in range(len(after))], 1)
                hi, lo = split2(anomaly)
                fill = -3 * members % 128
                left = jnp.concatenate([hi, lo, hi, jnp.zeros((fill, nobs), bf16)], 0)
                hi, lo = split2(spread)
                blank = jnp.zeros((fill, later.shape[1]), bf16)
                gain = narrow(left, jnp.concatenate([hi, hi, lo, blank], 0), 0, 0)
                gain = gain / (members - 1) * taper
                coeff_hi, coeff_lo = split2(coeff)
                hi, lo = split2(gain)
                left = jnp.concatenate([coeff_hi, coeff_hi, coeff_lo], 1)
                later = later + narrow(left, jnp.concatenate([hi, lo, hi], 0), 1, 0)
                for i, e in enumerate(after):
                    Y[e] = later[:, nobs * i : nobs * (i + 1)]
        for e in range(part[-1] + 1, batches):
            at = e - part[-1] - 1
            later_ref[0][:, nobs * at : nobs * (at + 1)] = Y[e]

    return kernel


def update_kernel(width, comps, batches, members, cols_dev, count, group):
    def kernel(
        own_ref, near_a, near_b, far_a, far_b, cx_ref, cy_ref, d_ref,
        taper_ref, *refs,
    ):
        *pair_refs, out_ref, grid_ref = refs
        pairs = [
            (pair_refs[i][k], pair_refs[i + 1][k])
            for i in range(0, len(pair_refs), 2)
            for k in range(pair_refs[i].shape[0])
        ]
        start = pl.multiple_of(lax.axis_index("mem") * cols_dev, cols_dev)
        cx = cx_ref[:, pl.ds(start, cols_dev)]
        cy = cy_ref[:, pl.ds(start, cols_dev)]
        d = d_ref[:, pl.ds(start, cols_dev)]
        lane = lax.broadcasted_iota(jnp.int32, (1, cols_dev), 1)
        even = jnp.full((1, cols_dev), lax.axis_index("sub") & 1, jnp.int32) == 0
        from_south, from_north = jnp.maximum(cy, 0.0), -jnp.minimum(cy, 0.0)
        from_near = jnp.where(even, from_north, from_south)
        from_far = jnp.where(even, from_south, from_north)
        from_west, from_east = jnp.maximum(cx, 0.0), -jnp.minimum(cx, 0.0)
        for s in range(own_ref.shape[0]):
            middle = near_a.shape[0]
            near_ref, far_ref = (near_a, far_a) if s < middle else (near_b, far_b)
            outer = to_columns(own_ref[s, count:, :])
            for j in range(-(-count // 128)):
                size = min(128, count - 128 * j)
                at = slice(128 * j, 128 * j + size)
                q, near, far = own_ref[s, at, :], near_ref[s % middle, at, :], far_ref[s % middle, at, :]
                west = jnp.where(lane == 0, outer[:size, 2 * j : 2 * j + 1], pltpu.roll(q, 1, 1))
                east = jnp.where(
                    lane == cols_dev - 1,
                    outer[:size, 2 * j + 1 : 2 * j + 2],
                    pltpu.roll(q, cols_dev - 1, 1),
                )
                x = q - from_west * (q - west) - from_east * (q - east)
                x = x - from_near * (q - near) - from_far * (q - far)
                x = x + d * (east + west + near + far - 4.0 * q)
                grid_ref[pl.ds(s * count + 128 * j, size), :] = x
        left, right, tapers = [], [], []
        nobs = taper_ref.shape[1]
        fill = -3 * members % 128
        blank = jnp.zeros((fill, group * cols_dev), bf16)
        for b in range(batches):
            hi, lo = split2(pairs[b][0])
            left.append(jnp.concatenate([hi, lo, hi, jnp.zeros((fill, nobs), bf16)], 0))
            hi, lo = split2(pairs[b][1])
            right.append(jnp.concatenate([hi, hi, lo], 1))
            tapers.append(jnp.tile(taper_ref[b] / (members - 1), (1, group)))
        for first in range(0, comps, group):
            x = jnp.concatenate(
                [grid_ref[pl.ds(first + i, members, comps), :] for i in range(group)], 1
            )
            for b in range(batches):
                spread = x - jnp.sum(x, axis=0, keepdims=True) / members
                hi, lo = split2(spread)
                gain = narrow(left[b], jnp.concatenate([hi, hi, lo, blank], 0), 0, 0) * tapers[b]
                hi, lo = split2(gain)
                x = x + narrow(right[b], jnp.concatenate([hi, lo, hi], 0), 1, 0)
            for i in range(group):
                out_ref[pl.ds(first + i, members, comps), :] = x[:, i * cols_dev : (i + 1) * cols_dev]

    return kernel


def shards(
    prior_sample_array,
    courant_x,
    courant_y,
    diffusion,
    obs_cell,
    obs_value,
    obs_error,
    obs_weight,
    taper_radius,
):
    local, rows_dev, comps, width = prior_sample_array.shape
    blocks = lax.axis_size("mem")
    bands = lax.axis_size("sub")
    cols_dev = width // blocks
    members = local * blocks
    batches, nobs = obs_cell.shape
    count = local * comps
    edge_rows = -(-(2 * -(-count // 128)) // 8) * 8
    assert bands & (bands - 1) == 0 and bands > 2 and blocks & (blocks - 1) == 0 and rows_dev == 1 and batches == 4 and cols_dev == 128 and nobs == 128

    share_rows = -(-(local + 2) // 8) * 8
    prior = prior_sample_array.reshape(count, width)
    (send,) = call(
        send_kernel(width, blocks, edge_rows),
        [(blocks, count + edge_rows, cols_dev)],
        "send",
        (prior,),
    )
    grid = lax.all_to_all(send.reshape(blocks, 1, -1), "mem", 0, 0).reshape(send.shape)
    held_x, send = lax.optimization_barrier((courant_x, send))
    sources = (prior, held_x, courant_y, diffusion, obs_cell, obs_weight.transpose(0, 2, 1))
    (share,) = call(
        share_kernel(width, comps, batches, nobs, local),
        [(share_rows, batches * nobs)],
        "share",
        sources,
        [pltpu.VMEM(x.shape, x.dtype) for x in sources] + [pltpu.SemaphoreType.DMA((6,))],
        pl.ANY,
    )
    obs_taper, cell_taper = call(
        taper_kernel(width, batches, nobs, cols_dev),
        [(batches * (batches - 1) // 2, nobs, nobs), (batches, nobs, cols_dev)],
        "tapers",
        (obs_cell, taper_radius),
    )
    step = 1
    while step < bands:
        other = lax.ppermute(share, "sub", [(i, i ^ step) for i in range(bands)])
        if step == 1:
            other, obs_taper, cell_taper = lax.optimization_barrier((other, obs_taper, cell_taper))
        last = 2 * step == bands
        (share,) = call(
            join_kernel(local, step == 1, last),
            [(local if last else share_rows, batches * nobs)],
            "join",
            (share, other),
        )
        if 4 * step == bands:
            share, grid = lax.optimization_barrier((share, grid))
        step *= 2
    swap = [(i, i ^ 1) for i in range(bands)]
    onward = [(i, i + 2) for i in range(0, bands - 2, 2)] + [(i, i - 2) for i in range(3, bands, 2)]
    middle = blocks // 2
    near = [lax.ppermute(part, "sub", swap) for part in (grid[:middle], grid[middle:])]
    observed = {0: share}
    step = blocks // 2
    while step:
        to = [(i, i ^ step) for i in range(blocks)]
        observed.update({k ^ step: lax.ppermute(x, "mem", to) for k, x in observed.items()})
        step //= 2
    observed = [observed[k] for k in range(blocks)]
    pairs, far = [], []
    for b in range(batches):
        part = range(b, b + 1)
        if b == 2:
            *observed, far[0] = lax.optimization_barrier((*observed, far[0]))
        if b < 2:
            *observed, near[b] = lax.optimization_barrier((*observed, near[b]))
            far.append(lax.ppermute(near[b], "sub", onward))
        outs = call(
            chain_kernel(part, batches, nobs, len(observed)),
            [(len(part), members, nobs)] * 2
            + [(members, (batches - part[-1] - 1) * nobs)] * (part[-1] + 1 < batches),
            "chain",
            (*observed, obs_value, obs_error, obs_taper),
        )
        pairs += outs[:2]
        observed = outs[2:]
    (out,) = call(
        update_kernel(width, comps, batches, members, cols_dev, count, comps),
        [(members * comps, cols_dev)],
        "update",
        (grid, *near, *far, courant_x, courant_y, diffusion, cell_taper, *pairs),
        (pltpu.VMEM((members * comps, cols_dev), f32),),
    )
    return out.reshape(members, rows_dev, comps, cols_dev)


def solution(mesh):
    return jax.shard_map(
        shards,
        mesh=mesh,
        in_specs=(
            P("mem", "sub", None, None),
            P("sub", None),
            P("sub", None),
            P("sub", None),
            P(),
            P(),
            P(),
            P(),
            P(),
        ),
        out_specs=P(None, "sub", None, "mem"),
        check_vma=False,
    )
```

```python
import jax
import jax.numpy as jnp
from jax import lax
from jax.experimental import pallas as pl
from jax.experimental.pallas import tpu as pltpu
from jax.sharding import PartitionSpec as P

highest = lax.Precision.HIGHEST
f32 = jnp.float32
bf16 = jnp.bfloat16
TILE = (8, 128)


def dot(a, b, ca, cb, precision=highest):
    return lax.dot_general(
        a, b, (((ca,), (cb,)), ((), ())), precision=precision, preferred_element_type=f32
    )


def narrow(a, b, ca, cb):
    return dot(a, b, ca, cb, None)


def split2(x):
    hi = x.astype(bf16)
    return hi, (x - hi.astype(f32)).astype(bf16)


def split3(x):
    hi = x.astype(bf16)
    rest = x - hi.astype(f32)
    mid = rest.astype(bf16)
    return hi, mid, (rest - mid.astype(f32)).astype(bf16)


def call(kernel, out_shapes, name, operands, scratch=(), space=pltpu.VMEM):
    specs = [pl.BlockSpec(memory_space=space) for _ in operands]
    return pl.pallas_call(
        kernel,
        in_specs=specs,
        out_specs=[pl.BlockSpec(memory_space=pltpu.VMEM) for _ in out_shapes],
        out_shape=[jax.ShapeDtypeStruct(s, f32) for s in out_shapes],
        scratch_shapes=list(scratch),
        compiler_params=pltpu.CompilerParams(vmem_limit_bytes=48 * 2**20),
        name=name,
    )(*operands)


def rows_cols(cells, width):
    if width & (width - 1) == 0:
        shift = width.bit_length() - 1
        return cells >> shift, cells & (width - 1)
    return cells // width, cells % width


def to_columns(rows):
    n = rows.shape[0]
    return jnp.concatenate([rows, jnp.zeros((128 - n, 128), f32)], 0).T


def gaspari(delta_row, delta_col, cutoff_radius, width):
    half = width // 2
    folded = jnp.where(delta_col >= half, delta_col - width, delta_col)
    folded = jnp.where(delta_col < -half, delta_col + width, folded)
    ratio = jnp.sqrt(delta_row * delta_row + folded * folded) / cutoff_radius
    inner = (((-0.25 * ratio + 0.5) * ratio + 0.625) * ratio - 5.0 / 3.0) * ratio * ratio + 1.0
    bounded = jnp.maximum(ratio, 1.0)
    outer = (
        ((((ratio / 12.0 - 0.5) * ratio + 0.625) * ratio + 5.0 / 3.0) * ratio - 5.0) * ratio
        + 4.0
        - 2.0 / (3.0 * bounded)
    )
    return jnp.where(ratio <= 1.0, inner, jnp.where(ratio < 2.0, outer, 0.0))


def taper_kernel(width, batches, nobs, cols_dev):
    def kernel(cell_ref, radius_ref, obs_taper_ref, cell_taper_ref):
        row_here = lax.axis_index("sub").astype(f32)
        col_here = lax.axis_index("mem") * cols_dev
        row_i, col_i = rows_cols(cell_ref[...], width)
        rows = row_i.astype(f32)
        cols = col_i.astype(f32)
        table = to_columns(jnp.concatenate([rows, cols, radius_ref[...]], 0))
        lane = lax.broadcasted_iota(jnp.int32, (1, cols_dev), 1)
        cell_cols = (lane + col_here).astype(f32)
        slot = 0
        for b in range(batches):
            row_j = table[:, b : b + 1]
            col_j = table[:, batches + b : batches + b + 1]
            radius = table[:, 2 * batches + b : 2 * batches + b + 1]
            cell_taper_ref[b] = gaspari(row_here - row_j, cell_cols - col_j, radius, width)
            for e in range(b + 1, batches):
                obs_taper_ref[slot] = gaspari(
                    rows[e : e + 1, :] - row_j, cols[e : e + 1, :] - col_j, radius, width
                )
                slot += 1

    return kernel


def share_kernel(width, comps, batches, nobs, local):
    def kernel(*refs):
        sources, (share_ref, *fetched, arrived) = refs[:6], refs[6:]
        q_ref, cx_ref, cy_ref, d_ref, cell_ref, weight_ref = fetched
        copies = [
            pltpu.make_async_copy(source, target, arrived.at[i])
            for i, (source, target) in enumerate(zip(sources, fetched))
        ]
        for copy in copies:
            copy.start()
        here = lax.axis_index("sub")
        for copy in copies[1:]:
            copy.wait()
        cx, cy, d = cx_ref[...], cy_ref[...], d_ref[...]
        from_south, from_north = jnp.maximum(cy, 0.0) + d, d - jnp.minimum(cy, 0.0)
        even = jnp.full((1, width), here & 1, jnp.int32) == 0
        near = jnp.where(even, from_north, from_south)
        far = jnp.where(even, from_south, from_north)
        scales = [part.astype(f32) for part in split3(jnp.concatenate([near, far], 0))]
        scales = jnp.concatenate(scales + [jnp.zeros((10, width), f32)], 0).astype(bf16)
        row, col = rows_cols(cell_ref[...], width)
        row = jnp.concatenate([row[b : b + 1] for b in range(batches)], 1)
        col = jnp.concatenate([col[b : b + 1] for b in range(batches)], 1)
        away = row - here
        owned, beside = away == 0, (away == 1) | (away == -1)
        place = lax.broadcasted_iota(jnp.int32, (width, batches * nobs), 0)
        own_pick = (place == jnp.where(owned, col, -1)).astype(f32).astype(bf16)
        raw_pick = (place == jnp.where(beside, col, -1)).astype(f32).astype(bf16)
        copies[0].wait()
        q = q_ref[...]
        west = pltpu.roll(q, 1, 1)
        east = pltpu.roll(q, width - 1, 1)
        mine = q - jnp.maximum(cx, 0.0) * (q - west) - jnp.minimum(cx, 0.0) * (east - q)
        mine = mine - jnp.maximum(cy, 0.0) * q + jnp.minimum(cy, 0.0) * q
        mine = mine + d * (east + west - 4.0 * q)
        value = narrow(
            jnp.concatenate(split2(mine) + split2(q), 1),
            jnp.concatenate([own_pick, own_pick, raw_pick, raw_pick], 0),
            1,
            0,
        )
        weight = jnp.concatenate([weight_ref[b] for b in range(batches)], 1)
        value = jnp.sum(value.reshape(-1, comps, batches * nobs) * weight[None], axis=1)
        scale = narrow(scales, own_pick, 1, 0)
        scale = scale[0:2] + scale[2:4] + scale[4:6]
        share = [value, jnp.where(owned, scale, 1.0)]
        fill = share_ref.shape[0] - local - 2
        if fill:
            share.append(jnp.zeros((fill, batches * nobs), f32))
        share_ref[...] = jnp.concatenate(share, 0)

    return kernel


def send_kernel(width, blocks, edge_rows):
    def kernel(q_ref, *send_refs):
        here = lax.axis_index("mem")
        q = q_ref[...]
        count = q.shape[0]
        q_parts = split3(q)
        cols_dev = width // blocks
        lanes = -(-2 * blocks // 128) * 128
        which = lax.broadcasted_iota(jnp.int32, (width, lanes), 1)
        spot = lax.broadcasted_iota(jnp.int32, (width, lanes), 0)
        start = ((which >> 1) ^ here) * cols_dev
        wanted = jnp.where(which & 1 == 0, start - 1, start + cols_dev)
        wanted = jnp.where(wanted < 0, wanted + width, wanted)
        wanted = jnp.where(wanted == width, 0, wanted)
        pick = (spot == wanted).astype(f32).astype(bf16)
        edges = narrow(
            jnp.concatenate(q_parts, 1), jnp.concatenate([pick, pick, pick], 0), 1, 0
        )
        room = -count % 128
        if room:
            edges = jnp.concatenate([edges, jnp.zeros((room, lanes), f32)], 0)
        edges = edges.T
        chunks = -(-count // 128)
        for i, send_ref in enumerate(send_refs):
            first = pl.multiple_of((here ^ i) * cols_dev, cols_dev)
            send_ref[:count, :] = q_ref[:, pl.ds(first, cols_dev)]
            rows = [edges[2 * i : 2 * i + 2, j * 128 : (j + 1) * 128] for j in range(chunks)]
            if edge_rows > 2 * chunks:
                rows.append(jnp.zeros((edge_rows - 2 * chunks, 128), f32))
            send_ref[count:, :] = jnp.concatenate(rows, 0)

    return kernel


def join_kernel(local, first, last):
    def kernel(mine_ref, other_ref, out_ref):
        mine, other = mine_ref[...], other_ref[...]
        at = local
        value = mine[:local] * other[at : at + 1] + other[:local] * mine[at : at + 1]
        if last:
            out_ref[...] = value
        else:
            at = local + 1 if first else local
            scale = mine[at : at + 1] * other[at : at + 1]
            blank = jnp.zeros((out_ref.shape[0] - local - 1, value.shape[1]), f32)
            out_ref[...] = jnp.concatenate([value, scale, blank], 0)

    return kernel


def lane_spread(x, j):
    return jnp.take_along_axis(x, jnp.full(x.shape, j, jnp.int32), axis=1)


def row_spread(x, i):
    return jnp.broadcast_to(x[i : i + 1, :], x.shape)


def factored(cov, sides, error, members, span=4):
    tiles = cov.shape[0] // 8
    lane = lax.broadcasted_iota(jnp.int32, TILE, 1)
    sub = lax.broadcasted_iota(jnp.int32, TILE, 0)
    T = [cov[8 * q : 8 * q + 8, :] for q in range(tiles)]
    V = [sides[8 * q : 8 * q + 8, :] for q in range(tiles)]
    deviation = jnp.broadcast_to(jnp.sqrt(error), TILE)
    is_member = lane < members
    inverse, solved, finished = [], [], []
    for p in range(tiles):
        block = (lane >= 8 * p) & (lane < 8 * p + 8)
        columns = [lane_spread(T[p], 8 * p + c) for c in range(8)]
        s = [[row_spread(columns[c], a) if a >= c else None for c in range(8)] for a in range(8)]
        joined = jnp.where(block, (lane - 8 * p == sub).astype(f32), T[p])
        R = [row_spread(joined, c) for c in range(8)]
        Z = [row_spread(V[p], c) for c in range(8)]
        rd, rs = [None] * 8, [None] * 8
        m = [[None] * 8 for _ in range(8)]
        for c in range(8):
            rd[c] = 1.0 / s[c][c]
            rs[c] = lax.rsqrt(s[c][c])
            root = s[c][c] * rs[c]
            spread = lane_spread(deviation, 8 * p + c)
            Z[c] = Z[c] * jnp.where(is_member, root / (root + spread), 1.0)
            for a in range(c + 1, 8):
                m[a][c] = s[a][c] * rd[c]
            for a in range(c + 1, 8):
                for e in range(c + 1, a + 1):
                    s[a][e] = s[a][e] - (s[a][c] * s[e][c]) * rd[c]
                R[a] = R[a] - m[a][c] * R[c]
                Z[a] = Z[a] - m[a][c] * Z[c]
        X, U = [None] * 8, [None] * 8
        for a in range(7, -1, -1):
            x, u = rd[a] * R[a], rd[a] * Z[a]
            for c in range(a + 1, 8):
                x = x - m[c][a] * X[c]
                u = u - m[c][a] * U[c]
            X[a], U[a] = x, u
        low, side = R[0] * rs[0], Z[0] * rs[0]
        for c in range(1, 8):
            low = jnp.where(sub == c, R[c] * rs[c], low)
            side = jnp.where(sub == c, Z[c] * rs[c], side)
        inverse.append(jnp.where(lane < 8 * p + 8, low, 0.0))
        solved.append(side)
        finished.append((low, side))
        edge = (p // span + 1) * span
        for q in range(p + 1, edge):
            column = [lane_spread(T[q], 8 * p + c) for c in range(8)]
            left, right = X, U
            if q == p + 1:
                for c in range(8):
                    for a in range(c):
                        column[c] = column[c] - m[c][a] * column[a]
                column = [column[c] * rd[c] for c in range(8)]
                left, right = R, Z
            t, v = jnp.where(block, 0.0, T[q]), V[q]
            for c in range(8):
                t = t - column[c] * left[c]
                v = v - column[c] * right[c]
            T[q], V[q] = t, v
        if p + 1 == edge and edge < tiles:
            rows = finished[edge - span : edge]
            upper = jnp.concatenate([low for low, _ in rows], 0)
            keep = [
                jnp.where((lane < 8 * (edge - span + i + 1)) | (lane >= 8 * edge), low, 0.0)
                for i, (low, _) in enumerate(rows)
            ]
            side_rows = jnp.concatenate([side for _, side in rows], 0)
            taken = products(upper, jnp.concatenate([jnp.concatenate(keep, 0), side_rows], 1))
            inside = (lane >= 8 * (edge - span)) & (lane < 8 * edge)
            for q in range(edge, tiles):
                at = slice(8 * q, 8 * q + 8)
                T[q] = jnp.where(inside, 0.0, T[q]) - taken[at, :128]
                V[q] = V[q] - taken[at, 128:]
    return jnp.concatenate(inverse, 0), jnp.concatenate(solved, 0)


def products(a, b):
    ah, am, al = split3(a)
    bh, bm, bl = split3(b)
    return narrow(
        jnp.concatenate([al, am, ah, am, ah, ah], 0),
        jnp.concatenate([bh, bm, bl, bh, bm, bh], 0),
        0,
        0,
    )


def coefficients(observed, value, error):
    members, nobs = observed.shape
    mean = jnp.sum(observed, axis=0, keepdims=True) / members
    anomaly = observed - mean
    row = lax.broadcasted_iota(jnp.int32, (nobs, nobs), 0)
    col = lax.broadcasted_iota(jnp.int32, (nobs, nobs), 1)
    cov = products(anomaly, anomaly) / (members - 1) + jnp.where(row == col, error, 0.0)
    sides = jnp.concatenate(
        [anomaly, value - mean, jnp.zeros((nobs - members - 1, nobs), f32)], 0
    ).T
    inverse, solved = factored(cov, sides, error, members)
    back = products(solved, inverse)
    return anomaly, back[members : members + 1] - back[:members]


def chain_kernel(part, batches, nobs, pieces):
    def kernel(*refs):
        y_refs, refs = refs[:pieces], refs[pieces:]
        value_ref, error_ref, taper_ref, anomaly_ref, coeff_ref, *later_ref = refs
        blocks = [ref[...] for ref in y_refs]
        step = 1
        while step < pieces:
            odd = jnp.full(blocks[0].shape, lax.axis_index("mem") & step, jnp.int32) != 0
            blocks = [jnp.where(odd, blocks[k ^ step], blocks[k]) for k in range(pieces)]
            step *= 2
        observed = jnp.concatenate(blocks, 0) if pieces > 1 else blocks[0]
        members = observed.shape[0]
        first = batches - observed.shape[1] // nobs
        Y = {b: observed[:, nobs * (b - first) : nobs * (b - first + 1)] for b in range(first, batches)}
        for b in part:
            anomaly, coeff = coefficients(Y[b], value_ref[b : b + 1, :], error_ref[b : b + 1, :])
            anomaly_ref[b - first] = anomaly
            coeff_ref[b - first] = coeff
            after = range(b + 1, batches)
            if after:
                slot = b * batches - b * (b + 1) // 2
                later = jnp.concatenate([Y[e] for e in after], 1)
                spread = later - jnp.sum(later, axis=0, keepdims=True) / members
                taper = jnp.concatenate([taper_ref[slot + i] for i in range(len(after))], 1)
                hi, lo = split2(anomaly)
                fill = -3 * members % 128
                left = jnp.concatenate([hi, lo, hi, jnp.zeros((fill, nobs), bf16)], 0)
                hi, lo = split2(spread)
                blank = jnp.zeros((fill, later.shape[1]), bf16)
                gain = narrow(left, jnp.concatenate([hi, hi, lo, blank], 0), 0, 0)
                gain = gain / (members - 1) * taper
                coeff_hi, coeff_lo = split2(coeff)
                hi, lo = split2(gain)
                left = jnp.concatenate([coeff_hi, coeff_hi, coeff_lo], 1)
                later = later + narrow(left, jnp.concatenate([hi, lo, hi], 0), 1, 0)
                for i, e in enumerate(after):
                    Y[e] = later[:, nobs * i : nobs * (i + 1)]
        for e in range(part[-1] + 1, batches):
            at = e - part[-1] - 1
            later_ref[0][:, nobs * at : nobs * (at + 1)] = Y[e]

    return kernel


def update_kernel(width, comps, batches, members, cols_dev, count, blocks, group):
    def kernel(
        *refs,
    ):
        own_refs, near_refs, far_refs = (refs[i * blocks : (i + 1) * blocks] for i in range(3))
        cx_ref, cy_ref, d_ref, taper_ref, *pair_refs, out_ref, grid_ref = refs[3 * blocks :]
        pairs = [
            (pair_refs[i][k], pair_refs[i + 1][k])
            for i in range(0, len(pair_refs), 2)
            for k in range(pair_refs[i].shape[0])
        ]
        start = pl.multiple_of(lax.axis_index("mem") * cols_dev, cols_dev)
        cx = cx_ref[:, pl.ds(start, cols_dev)]
        cy = cy_ref[:, pl.ds(start, cols_dev)]
        d = d_ref[:, pl.ds(start, cols_dev)]
        lane = lax.broadcasted_iota(jnp.int32, (1, cols_dev), 1)
        even = jnp.full((1, cols_dev), lax.axis_index("sub") & 1, jnp.int32) == 0
        from_south, from_north = jnp.maximum(cy, 0.0), -jnp.minimum(cy, 0.0)
        from_near = jnp.where(even, from_north, from_south)
        from_far = jnp.where(even, from_south, from_north)
        from_west, from_east = jnp.maximum(cx, 0.0), -jnp.minimum(cx, 0.0)
        for s, (own_ref, near_ref, far_ref) in enumerate(zip(own_refs, near_refs, far_refs)):
            base = pl.multiple_of((lax.axis_index("mem") ^ s) * count, 8)
            outer = to_columns(own_ref[count:, :])
            for j in range(-(-count // 128)):
                size = min(128, count - 128 * j)
                at = slice(128 * j, 128 * j + size)
                q, near, far = own_ref[at, :], near_ref[at, :], far_ref[at, :]
                west = jnp.where(lane == 0, outer[:size, 2 * j : 2 * j + 1], pltpu.roll(q, 1, 1))
                east = jnp.where(
                    lane == cols_dev - 1,
                    outer[:size, 2 * j + 1 : 2 * j + 2],
                    pltpu.roll(q, cols_dev - 1, 1),
                )
                x = q - from_west * (q - west) - from_east * (q - east)
                x = x - from_near * (q - near) - from_far * (q - far)
                x = x + d * (east + west + near + far - 4.0 * q)
                grid_ref[pl.ds(base + 128 * j, size), :] = x
        left, right, tapers = [], [], []
        nobs = taper_ref.shape[1]
        fill = -3 * members % 128
        blank = jnp.zeros((fill, group * cols_dev), bf16)
        for b in range(batches):
            hi, lo = split2(pairs[b][0])
            left.append(jnp.concatenate([hi, lo, hi, jnp.zeros((fill, nobs), bf16)], 0))
            hi, lo = split2(pairs[b][1])
            right.append(jnp.concatenate([hi, hi, lo], 1))
            tapers.append(jnp.tile(taper_ref[b] / (members - 1), (1, group)))
        for first in range(0, comps, group):
            x = jnp.concatenate(
                [grid_ref[pl.ds(first + i, members, comps), :] for i in range(group)], 1
            )
            for b in range(batches):
                spread = x - jnp.sum(x, axis=0, keepdims=True) / members
                hi, lo = split2(spread)
                gain = narrow(left[b], jnp.concatenate([hi, hi, lo, blank], 0), 0, 0) * tapers[b]
                hi, lo = split2(gain)
                x = x + narrow(right[b], jnp.concatenate([hi, lo, hi], 0), 1, 0)
            for i in range(group):
                out_ref[pl.ds(first + i, members, comps), :] = x[:, i * cols_dev : (i + 1) * cols_dev]

    return kernel


def shards(
    prior_sample_array,
    courant_x,
    courant_y,
    diffusion,
    obs_cell,
    obs_value,
    obs_error,
    obs_weight,
    taper_radius,
):
    local, rows_dev, comps, width = prior_sample_array.shape
    blocks = lax.axis_size("mem")
    bands = lax.axis_size("sub")
    cols_dev = width // blocks
    members = local * blocks
    batches, nobs = obs_cell.shape
    count = local * comps
    edge_rows = -(-(2 * -(-count // 128)) // 8) * 8
    assert bands & (bands - 1) == 0 and bands > 2 and blocks & (blocks - 1) == 0 and rows_dev == 1 and batches == 4 and cols_dev == 128 and nobs == 128

    share_rows = -(-(local + 2) // 8) * 8
    prior = prior_sample_array.reshape(count, width)
    sends = call(
        send_kernel(width, blocks, edge_rows),
        [(count + edge_rows, cols_dev)] * blocks,
        "send",
        (prior,),
    )
    grid = [sends[0]] + [
        lax.ppermute(sends[k], "mem", [(i, i ^ k) for i in range(blocks)]) for k in range(1, blocks)
    ]
    held_x, *sends = lax.optimization_barrier((courant_x, *sends))
    sources = (prior, held_x, courant_y, diffusion, obs_cell, obs_weight.transpose(0, 2, 1))
    (share,) = call(
        share_kernel(width, comps, batches, nobs, local),
        [(share_rows, batches * nobs)],
        "share",
        sources,
        [pltpu.VMEM(x.shape, x.dtype) for x in sources] + [pltpu.SemaphoreType.DMA((6,))],
        pl.ANY,
    )
    obs_taper, cell_taper = call(
        taper_kernel(width, batches, nobs, cols_dev),
        [(batches * (batches - 1) // 2, nobs, nobs), (batches, nobs, cols_dev)],
        "tapers",
        (obs_cell, taper_radius),
    )
    swap = [(i, i ^ 1) for i in range(bands)]
    onward = [(i, i + 2) for i in range(0, bands - 2, 2)] + [(i, i - 2) for i in range(3, bands, 2)]
    middle = blocks // 2
    parts = (slice(0, middle), slice(middle, blocks))
    near, far = [], []
    step = 1
    while step < bands:
        other = lax.ppermute(share, "sub", [(i, i ^ step) for i in range(bands)])
        if step == 1:
            other, obs_taper, cell_taper = lax.optimization_barrier((other, obs_taper, cell_taper))
        last = 2 * step == bands
        (share,) = call(
            join_kernel(local, step == 1, last),
            [(local if last else share_rows, batches * nobs)],
            "join",
            (share, other),
        )
        if step in (1, 2):
            part = parts[step // 2]
            share, *grid[part] = lax.optimization_barrier((share, *grid[part]))
            near += [lax.ppermute(x, "sub", swap) for x in grid[part]]
        step *= 2
    share, *near[:middle] = lax.optimization_barrier((share, *near[:middle]))
    far += [lax.ppermute(x, "sub", onward) for x in near[:middle]]
    observed = {0: share}
    step = blocks // 2
    while step:
        to = [(i, i ^ step) for i in range(blocks)]
        observed.update({k ^ step: lax.ppermute(x, "mem", to) for k, x in observed.items()})
        step //= 2
    observed = [observed[k] for k in range(blocks)]
    pairs = []
    for b in range(batches):
        part = range(b, b + 1)
        if b == 0:
            held = lax.optimization_barrier((*observed, *near[middle:]))
            observed, near[middle:] = held[: len(observed)], held[len(observed) :]
            far += [lax.ppermute(x, "sub", onward) for x in near[middle:]]
        if b == 2:
            held = lax.optimization_barrier((*observed, *far[:middle]))
            observed, far[:middle] = held[: len(observed)], held[len(observed) :]
        outs = call(
            chain_kernel(part, batches, nobs, len(observed)),
            [(len(part), members, nobs)] * 2
            + [(members, (batches - part[-1] - 1) * nobs)] * (part[-1] + 1 < batches),
            "chain",
            (*observed, obs_value, obs_error, obs_taper),
        )
        pairs += outs[:2]
        observed = outs[2:]
    (out,) = call(
        update_kernel(width, comps, batches, members, cols_dev, count, blocks, comps),
        [(members * comps, cols_dev)],
        "update",
        (*grid, *near, *far, courant_x, courant_y, diffusion, cell_taper, *pairs),
        (pltpu.VMEM((members * comps, cols_dev), f32),),
    )
    return out.reshape(members, rows_dev, comps, cols_dev)


def solution(mesh):
    return jax.shard_map(
        shards,
        mesh=mesh,
        in_specs=(
            P("mem", "sub", None, None),
            P("sub", None),
            P("sub", None),
            P("sub", None),
            P(),
            P(),
            P(),
            P(),
            P(),
        ),
        out_specs=P(None, "sub", None, "mem"),
        check_vma=False,
    )
```

```python
import jax
import jax.numpy as jnp
from jax import lax
from jax.experimental import pallas as pl
from jax.experimental.pallas import tpu as pltpu
from jax.sharding import PartitionSpec as P

highest = lax.Precision.HIGHEST
f32 = jnp.float32
bf16 = jnp.bfloat16
TILE = (8, 128)


def dot(a, b, ca, cb, precision=highest):
    return lax.dot_general(
        a, b, (((ca,), (cb,)), ((), ())), precision=precision, preferred_element_type=f32
    )


def narrow(a, b, ca, cb):
    return dot(a, b, ca, cb, None)


def split2(x):
    hi = x.astype(bf16)
    return hi, (x - hi.astype(f32)).astype(bf16)


def split3(x):
    hi = x.astype(bf16)
    rest = x - hi.astype(f32)
    mid = rest.astype(bf16)
    return hi, mid, (rest - mid.astype(f32)).astype(bf16)


def call(kernel, out_shapes, name, operands, scratch=(), space=pltpu.VMEM):
    specs = [pl.BlockSpec(memory_space=space) for _ in operands]
    return pl.pallas_call(
        kernel,
        in_specs=specs,
        out_specs=[pl.BlockSpec(memory_space=pltpu.VMEM) for _ in out_shapes],
        out_shape=[jax.ShapeDtypeStruct(s, f32) for s in out_shapes],
        scratch_shapes=list(scratch),
        compiler_params=pltpu.CompilerParams(vmem_limit_bytes=48 * 2**20),
        name=name,
    )(*operands)


def rows_cols(cells, width):
    if width & (width - 1) == 0:
        shift = width.bit_length() - 1
        return cells >> shift, cells & (width - 1)
    return cells // width, cells % width


def to_columns(rows):
    n = rows.shape[0]
    return jnp.concatenate([rows, jnp.zeros((128 - n, 128), f32)], 0).T


def gaspari(delta_row, delta_col, cutoff_radius, width):
    half = width // 2
    folded = jnp.where(delta_col >= half, delta_col - width, delta_col)
    folded = jnp.where(delta_col < -half, delta_col + width, folded)
    ratio = jnp.sqrt(delta_row * delta_row + folded * folded) / cutoff_radius
    inner = (((-0.25 * ratio + 0.5) * ratio + 0.625) * ratio - 5.0 / 3.0) * ratio * ratio + 1.0
    bounded = jnp.maximum(ratio, 1.0)
    outer = (
        ((((ratio / 12.0 - 0.5) * ratio + 0.625) * ratio + 5.0 / 3.0) * ratio - 5.0) * ratio
        + 4.0
        - 2.0 / (3.0 * bounded)
    )
    return jnp.where(ratio <= 1.0, inner, jnp.where(ratio < 2.0, outer, 0.0))


def taper_kernel(width, batches, nobs, cols_dev):
    def kernel(cell_ref, radius_ref, obs_taper_ref, cell_taper_ref):
        row_here = lax.axis_index("sub").astype(f32)
        col_here = lax.axis_index("mem") * cols_dev
        row_i, col_i = rows_cols(cell_ref[...], width)
        rows = row_i.astype(f32)
        cols = col_i.astype(f32)
        table = to_columns(jnp.concatenate([rows, cols, radius_ref[...]], 0))
        lane = lax.broadcasted_iota(jnp.int32, (1, cols_dev), 1)
        cell_cols = (lane + col_here).astype(f32)
        slot = 0
        for b in range(batches):
            row_j = table[:, b : b + 1]
            col_j = table[:, batches + b : batches + b + 1]
            radius = table[:, 2 * batches + b : 2 * batches + b + 1]
            cell_taper_ref[b] = gaspari(row_here - row_j, cell_cols - col_j, radius, width)
            for e in range(b + 1, batches):
                obs_taper_ref[slot] = gaspari(
                    rows[e : e + 1, :] - row_j, cols[e : e + 1, :] - col_j, radius, width
                )
                slot += 1

    return kernel


def share_kernel(width, comps, batches, nobs, local):
    def kernel(*refs):
        sources, (share_ref, *fetched, arrived) = refs[:6], refs[6:]
        q_ref, cx_ref, cy_ref, d_ref, cell_ref, weight_ref = fetched
        copies = [
            pltpu.make_async_copy(source, target, arrived.at[i])
            for i, (source, target) in enumerate(zip(sources, fetched))
        ]
        for copy in copies:
            copy.start()
        here = lax.axis_index("sub")
        for copy in copies[1:]:
            copy.wait()
        cx, cy, d = cx_ref[...], cy_ref[...], d_ref[...]
        from_south, from_north = jnp.maximum(cy, 0.0) + d, d - jnp.minimum(cy, 0.0)
        even = jnp.full((1, width), here & 1, jnp.int32) == 0
        near = jnp.where(even, from_north, from_south)
        far = jnp.where(even, from_south, from_north)
        scales = [part.astype(f32) for part in split3(jnp.concatenate([near, far], 0))]
        scales = jnp.concatenate(scales + [jnp.zeros((10, width), f32)], 0).astype(bf16)
        row, col = rows_cols(cell_ref[...], width)
        row = jnp.concatenate([row[b : b + 1] for b in range(batches)], 1)
        col = jnp.concatenate([col[b : b + 1] for b in range(batches)], 1)
        away = row - here
        owned, beside = away == 0, (away == 1) | (away == -1)
        place = lax.broadcasted_iota(jnp.int32, (width, batches * nobs), 0)
        own_pick = (place == jnp.where(owned, col, -1)).astype(f32).astype(bf16)
        raw_pick = (place == jnp.where(beside, col, -1)).astype(f32).astype(bf16)
        copies[0].wait()
        q = q_ref[...]
        west = pltpu.roll(q, 1, 1)
        east = pltpu.roll(q, width - 1, 1)
        mine = q - jnp.maximum(cx, 0.0) * (q - west) - jnp.minimum(cx, 0.0) * (east - q)
        mine = mine - jnp.maximum(cy, 0.0) * q + jnp.minimum(cy, 0.0) * q
        mine = mine + d * (east + west - 4.0 * q)
        value = narrow(
            jnp.concatenate(split2(mine) + split2(q), 1),
            jnp.concatenate([own_pick, own_pick, raw_pick, raw_pick], 0),
            1,
            0,
        )
        weight = jnp.concatenate([weight_ref[b] for b in range(batches)], 1)
        value = jnp.sum(value.reshape(-1, comps, batches * nobs) * weight[None], axis=1)
        scale = narrow(scales, own_pick, 1, 0)
        scale = scale[0:2] + scale[2:4] + scale[4:6]
        share = [value, jnp.where(owned, scale, 1.0)]
        fill = share_ref.shape[0] - local - 2
        if fill:
            share.append(jnp.zeros((fill, batches * nobs), f32))
        share_ref[...] = jnp.concatenate(share, 0)

    return kernel


def send_kernel(width, blocks, edge_rows):
    def kernel(q_ref, *send_refs):
        here = lax.axis_index("mem")
        q = q_ref[...]
        count = q.shape[0]
        q_parts = split3(q)
        cols_dev = width // blocks
        lanes = -(-2 * blocks // 128) * 128
        which = lax.broadcasted_iota(jnp.int32, (width, lanes), 1)
        spot = lax.broadcasted_iota(jnp.int32, (width, lanes), 0)
        start = ((which >> 1) ^ here) * cols_dev
        wanted = jnp.where(which & 1 == 0, start - 1, start + cols_dev)
        wanted = jnp.where(wanted < 0, wanted + width, wanted)
        wanted = jnp.where(wanted == width, 0, wanted)
        pick = (spot == wanted).astype(f32).astype(bf16)
        edges = narrow(
            jnp.concatenate(q_parts, 1), jnp.concatenate([pick, pick, pick], 0), 1, 0
        )
        room = -count % 128
        if room:
            edges = jnp.concatenate([edges, jnp.zeros((room, lanes), f32)], 0)
        edges = edges.T
        chunks = -(-count // 128)
        for i, send_ref in enumerate(send_refs):
            first = pl.multiple_of((here ^ i) * cols_dev, cols_dev)
            send_ref[:count, :] = q_ref[:, pl.ds(first, cols_dev)]
            rows = [edges[2 * i : 2 * i + 2, j * 128 : (j + 1) * 128] for j in range(chunks)]
            if edge_rows > 2 * chunks:
                rows.append(jnp.zeros((edge_rows - 2 * chunks, 128), f32))
            send_ref[count:, :] = jnp.concatenate(rows, 0)

    return kernel


def join_kernel(local, first, last):
    def kernel(mine_ref, other_ref, out_ref):
        mine, other = mine_ref[...], other_ref[...]
        at = local
        value = mine[:local] * other[at : at + 1] + other[:local] * mine[at : at + 1]
        if last:
            out_ref[...] = value
        else:
            at = local + 1 if first else local
            scale = mine[at : at + 1] * other[at : at + 1]
            blank = jnp.zeros((out_ref.shape[0] - local - 1, value.shape[1]), f32)
            out_ref[...] = jnp.concatenate([value, scale, blank], 0)

    return kernel


def lane_spread(x, j):
    return jnp.take_along_axis(x, jnp.full(x.shape, j, jnp.int32), axis=1)


def row_spread(x, i):
    return jnp.broadcast_to(x[i : i + 1, :], x.shape)


def factored(cov, sides, error, members, span=4):
    tiles = cov.shape[0] // 8
    lane = lax.broadcasted_iota(jnp.int32, TILE, 1)
    sub = lax.broadcasted_iota(jnp.int32, TILE, 0)
    T = [cov[8 * q : 8 * q + 8, :] for q in range(tiles)]
    V = [sides[8 * q : 8 * q + 8, :] for q in range(tiles)]
    deviation = jnp.broadcast_to(jnp.sqrt(error), TILE)
    is_member = lane < members
    inverse, solved, finished = [], [], []
    for p in range(tiles):
        block = (lane >= 8 * p) & (lane < 8 * p + 8)
        columns = [lane_spread(T[p], 8 * p + c) for c in range(8)]
        s = [[row_spread(columns[c], a) if a >= c else None for c in range(8)] for a in range(8)]
        joined = jnp.where(block, (lane - 8 * p == sub).astype(f32), T[p])
        R = [row_spread(joined, c) for c in range(8)]
        Z = [row_spread(V[p], c) for c in range(8)]
        rd, rs = [None] * 8, [None] * 8
        m = [[None] * 8 for _ in range(8)]
        for c in range(8):
            rd[c] = 1.0 / s[c][c]
            rs[c] = lax.rsqrt(s[c][c])
            root = s[c][c] * rs[c]
            spread = lane_spread(deviation, 8 * p + c)
            Z[c] = Z[c] * jnp.where(is_member, root / (root + spread), 1.0)
            for a in range(c + 1, 8):
                m[a][c] = s[a][c] * rd[c]
            for a in range(c + 1, 8):
                for e in range(c + 1, a + 1):
                    s[a][e] = s[a][e] - (s[a][c] * s[e][c]) * rd[c]
                R[a] = R[a] - m[a][c] * R[c]
                Z[a] = Z[a] - m[a][c] * Z[c]
        X, U = [None] * 8, [None] * 8
        for a in range(7, -1, -1):
            x, u = rd[a] * R[a], rd[a] * Z[a]
            for c in range(a + 1, 8):
                x = x - m[c][a] * X[c]
                u = u - m[c][a] * U[c]
            X[a], U[a] = x, u
        low, side = R[0] * rs[0], Z[0] * rs[0]
        for c in range(1, 8):
            low = jnp.where(sub == c, R[c] * rs[c], low)
            side = jnp.where(sub == c, Z[c] * rs[c], side)
        inverse.append(jnp.where(lane < 8 * p + 8, low, 0.0))
        solved.append(side)
        finished.append((low, side))
        edge = (p // span + 1) * span
        for q in range(p + 1, edge):
            column = [lane_spread(T[q], 8 * p + c) for c in range(8)]
            left, right = X, U
            if q == p + 1:
                for c in range(8):
                    for a in range(c):
                        column[c] = column[c] - m[c][a] * column[a]
                column = [column[c] * rd[c] for c in range(8)]
                left, right = R, Z
            t, v = jnp.where(block, 0.0, T[q]), V[q]
            for c in range(8):
                t = t - column[c] * left[c]
                v = v - column[c] * right[c]
            T[q], V[q] = t, v
        if p + 1 == edge and edge < tiles:
            rows = finished[edge - span : edge]
            upper = jnp.concatenate([low for low, _ in rows], 0)
            keep = [
                jnp.where((lane < 8 * (edge - span + i + 1)) | (lane >= 8 * edge), low, 0.0)
                for i, (low, _) in enumerate(rows)
            ]
            side_rows = jnp.concatenate([side for _, side in rows], 0)
            taken = products(upper, jnp.concatenate([jnp.concatenate(keep, 0), side_rows], 1))
            inside = (lane >= 8 * (edge - span)) & (lane < 8 * edge)
            for q in range(edge, tiles):
                at = slice(8 * q, 8 * q + 8)
                T[q] = jnp.where(inside, 0.0, T[q]) - taken[at, :128]
                V[q] = V[q] - taken[at, 128:]
    return jnp.concatenate(inverse, 0), jnp.concatenate(solved, 0)


def products(a, b):
    ah, am, al = split3(a)
    bh, bm, bl = split3(b)
    return narrow(
        jnp.concatenate([al, am, ah, am, ah, ah], 0),
        jnp.concatenate([bh, bm, bl, bh, bm, bh], 0),
        0,
        0,
    )


def coefficients(observed, value, error):
    members, nobs = observed.shape
    mean = jnp.sum(observed, axis=0, keepdims=True) / members
    anomaly = observed - mean
    row = lax.broadcasted_iota(jnp.int32, (nobs, nobs), 0)
    col = lax.broadcasted_iota(jnp.int32, (nobs, nobs), 1)
    cov = products(anomaly, anomaly) / (members - 1) + jnp.where(row == col, error, 0.0)
    sides = jnp.concatenate(
        [anomaly, value - mean, jnp.zeros((nobs - members - 1, nobs), f32)], 0
    ).T
    inverse, solved = factored(cov, sides, error, members)
    back = products(solved, inverse)
    return anomaly, back[members : members + 1] - back[:members]


def chain_kernel(part, batches, nobs, pieces):
    def kernel(*refs):
        y_refs, refs = refs[:pieces], refs[pieces:]
        value_ref, error_ref, taper_ref, anomaly_ref, coeff_ref, *later_ref = refs
        blocks = [ref[...] for ref in y_refs]
        step = 1
        while step < pieces:
            odd = jnp.full(blocks[0].shape, lax.axis_index("mem") & step, jnp.int32) != 0
            blocks = [jnp.where(odd, blocks[k ^ step], blocks[k]) for k in range(pieces)]
            step *= 2
        observed = jnp.concatenate(blocks, 0) if pieces > 1 else blocks[0]
        members = observed.shape[0]
        first = batches - observed.shape[1] // nobs
        Y = {b: observed[:, nobs * (b - first) : nobs * (b - first + 1)] for b in range(first, batches)}
        for b in part:
            anomaly, coeff = coefficients(Y[b], value_ref[b : b + 1, :], error_ref[b : b + 1, :])
            anomaly_ref[b - first] = anomaly
            coeff_ref[b - first] = coeff
            after = range(b + 1, batches)
            if after:
                slot = b * batches - b * (b + 1) // 2
                later = jnp.concatenate([Y[e] for e in after], 1)
                spread = later - jnp.sum(later, axis=0, keepdims=True) / members
                taper = jnp.concatenate([taper_ref[slot + i] for i in range(len(after))], 1)
                hi, lo = split2(anomaly)
                fill = -3 * members % 128
                left = jnp.concatenate([hi, lo, hi, jnp.zeros((fill, nobs), bf16)], 0)
                hi, lo = split2(spread)
                blank = jnp.zeros((fill, later.shape[1]), bf16)
                gain = narrow(left, jnp.concatenate([hi, hi, lo, blank], 0), 0, 0)
                gain = gain / (members - 1) * taper
                coeff_hi, coeff_lo = split2(coeff)
                hi, lo = split2(gain)
                left = jnp.concatenate([coeff_hi, coeff_hi, coeff_lo], 1)
                later = later + narrow(left, jnp.concatenate([hi, lo, hi], 0), 1, 0)
                for i, e in enumerate(after):
                    Y[e] = later[:, nobs * i : nobs * (i + 1)]
        for e in range(part[-1] + 1, batches):
            at = e - part[-1] - 1
            later_ref[0][:, nobs * at : nobs * (at + 1)] = Y[e]

    return kernel


def update_kernel(width, comps, batches, members, cols_dev, count, blocks, bands, group):
    def kernel(
        *refs,
    ):
        own_refs, halos, refs = refs[:blocks], refs[blocks : blocks + 4], refs[blocks + 4 :]
        near_refs, far_refs = (
            [ref.at[i] for ref in halos[at : at + 2] for i in range(ref.shape[0])] for at in (0, 2)
        )
        cx_ref, cy_ref, d_ref, taper_ref, *pair_refs, out_ref, grid_ref = refs
        pairs = [
            (pair_refs[i][k], pair_refs[i + 1][k])
            for i in range(0, len(pair_refs), 2)
            for k in range(pair_refs[i].shape[0])
        ]
        start = pl.multiple_of(lax.axis_index("mem") * cols_dev, cols_dev)
        cx = cx_ref[:, pl.ds(start, cols_dev)]
        cy = cy_ref[:, pl.ds(start, cols_dev)]
        d = d_ref[:, pl.ds(start, cols_dev)]
        lane = lax.broadcasted_iota(jnp.int32, (1, cols_dev), 1)
        band = jnp.full((1, cols_dev), lax.axis_index("sub"), jnp.int32)
        even = band & 1 == 0
        outermost = (band == 0) | (band == bands - 1)
        from_south, from_north = jnp.maximum(cy, 0.0), -jnp.minimum(cy, 0.0)
        from_near = jnp.where(even, from_north, from_south)
        from_far = jnp.where(even, from_south, from_north)
        from_west, from_east = jnp.maximum(cx, 0.0), -jnp.minimum(cx, 0.0)
        for s, (own_ref, near_ref, far_ref) in enumerate(zip(own_refs, near_refs, far_refs)):
            base = pl.multiple_of((lax.axis_index("mem") ^ s) * count, 8)
            outer = to_columns(own_ref[count:, :])
            for j in range(-(-count // 128)):
                size = min(128, count - 128 * j)
                at = slice(128 * j, 128 * j + size)
                q, near = own_ref[at, :], near_ref[at, :]
                far = jnp.where(outermost, 0.0, far_ref[at, :])
                west = jnp.where(lane == 0, outer[:size, 2 * j : 2 * j + 1], pltpu.roll(q, 1, 1))
                east = jnp.where(
                    lane == cols_dev - 1,
                    outer[:size, 2 * j + 1 : 2 * j + 2],
                    pltpu.roll(q, cols_dev - 1, 1),
                )
                x = q - from_west * (q - west) - from_east * (q - east)
                x = x - from_near * (q - near) - from_far * (q - far)
                x = x + d * (east + west + near + far - 4.0 * q)
                grid_ref[pl.ds(base + 128 * j, size), :] = x
        left, right, tapers = [], [], []
        nobs = taper_ref.shape[1]
        fill = -3 * members % 128
        blank = jnp.zeros((fill, group * cols_dev), bf16)
        for b in range(batches):
            hi, lo = split2(pairs[b][0])
            left.append(jnp.concatenate([hi, lo, hi, jnp.zeros((fill, nobs), bf16)], 0))
            hi, lo = split2(pairs[b][1])
            right.append(jnp.concatenate([hi, hi, lo], 1))
            tapers.append(jnp.tile(taper_ref[b] / (members - 1), (1, group)))
        for first in range(0, comps, group):
            x = jnp.concatenate(
                [grid_ref[pl.ds(first + i, members, comps), :] for i in range(group)], 1
            )
            for b in range(batches):
                spread = x - jnp.sum(x, axis=0, keepdims=True) / members
                hi, lo = split2(spread)
                gain = narrow(left[b], jnp.concatenate([hi, hi, lo, blank], 0), 0, 0) * tapers[b]
                hi, lo = split2(gain)
                x = x + narrow(right[b], jnp.concatenate([hi, lo, hi], 0), 1, 0)
            for i in range(group):
                out_ref[pl.ds(first + i, members, comps), :] = x[:, i * cols_dev : (i + 1) * cols_dev]

    return kernel


def shards(
    prior_sample_array,
    courant_x,
    courant_y,
    diffusion,
    obs_cell,
    obs_value,
    obs_error,
    obs_weight,
    taper_radius,
):
    local, rows_dev, comps, width = prior_sample_array.shape
    blocks = lax.axis_size("mem")
    bands = lax.axis_size("sub")
    cols_dev = width // blocks
    members = local * blocks
    batches, nobs = obs_cell.shape
    count = local * comps
    edge_rows = -(-(2 * -(-count // 128)) // 8) * 8
    assert bands & (bands - 1) == 0 and bands > 2 and blocks & (blocks - 1) == 0 and rows_dev == 1 and batches == 4 and cols_dev == 128 and nobs == 128

    share_rows = -(-(local + 2) // 8) * 8
    prior = prior_sample_array.reshape(count, width)
    sends = call(
        send_kernel(width, blocks, edge_rows),
        [(count + edge_rows, cols_dev)] * blocks,
        "send",
        (prior,),
    )
    grid = [sends[0]] + [
        lax.ppermute(sends[k], "mem", [(i, i ^ k) for i in range(blocks)]) for k in range(1, blocks)
    ]
    held_x, *sends = lax.optimization_barrier((courant_x, *sends))
    sources = (prior, held_x, courant_y, diffusion, obs_cell, obs_weight.transpose(0, 2, 1))
    (share,) = call(
        share_kernel(width, comps, batches, nobs, local),
        [(share_rows, batches * nobs)],
        "share",
        sources,
        [pltpu.VMEM(x.shape, x.dtype) for x in sources] + [pltpu.SemaphoreType.DMA((6,))],
        pl.ANY,
    )
    obs_taper, cell_taper = call(
        taper_kernel(width, batches, nobs, cols_dev),
        [(batches * (batches - 1) // 2, nobs, nobs), (batches, nobs, cols_dev)],
        "tapers",
        (obs_cell, taper_radius),
    )
    swap = [(i, i ^ 1) for i in range(bands)]
    onward = [(i, i + 2) for i in range(0, bands - 2, 2)] + [(i, i - 2) for i in range(3, bands, 2)]
    around = onward + [(bands - 2, 0), (1, bands - 1)]
    across = onward + [(1, 0), (bands - 2, bands - 1)]
    middle = blocks // 2
    parts = (slice(0, middle), slice(middle, blocks))
    near, far = [], []
    step = 1
    while step < bands:
        other = lax.ppermute(share, "sub", [(i, i ^ step) for i in range(bands)])
        if step == 1:
            other, obs_taper, cell_taper = lax.optimization_barrier((other, obs_taper, cell_taper))
        last = 2 * step == bands
        (share,) = call(
            join_kernel(local, step == 1, last),
            [(local if last else share_rows, batches * nobs)],
            "join",
            (share, other),
        )
        if step in (1, 2):
            part = parts[step // 2]
            share, *grid[part] = lax.optimization_barrier((share, *grid[part]))
            near.append(lax.ppermute(jnp.stack(grid[part]), "sub", swap))
        step *= 2
    share, near[0] = lax.optimization_barrier((share, near[0]))
    far.append(lax.ppermute(near[0], "sub", around))
    observed = {0: share}
    step = blocks // 2
    while step:
        to = [(i, i ^ step) for i in range(blocks)]
        observed.update({k ^ step: lax.ppermute(x, "mem", to) for k, x in observed.items()})
        step //= 2
    observed = [observed[k] for k in range(blocks)]
    pairs = []
    for b in range(batches):
        part = range(b, b + 1)
        if b == 0:
            *observed, near[1] = lax.optimization_barrier((*observed, near[1]))
            far.append(lax.ppermute(near[1], "sub", across))
        if b == 2:
            *observed, far[0] = lax.optimization_barrier((*observed, far[0]))
        outs = call(
            chain_kernel(part, batches, nobs, len(observed)),
            [(len(part), members, nobs)] * 2
            + [(members, (batches - part[-1] - 1) * nobs)] * (part[-1] + 1 < batches),
            "chain",
            (*observed, obs_value, obs_error, obs_taper),
        )
        pairs += outs[:2]
        observed = outs[2:]
    (out,) = call(
        update_kernel(width, comps, batches, members, cols_dev, count, blocks, bands, comps),
        [(members * comps, cols_dev)],
        "update",
        (*grid, *near, *far, courant_x, courant_y, diffusion, cell_taper, *pairs),
        (pltpu.VMEM((members * comps, cols_dev), f32),),
    )
    return out.reshape(members, rows_dev, comps, cols_dev)


def solution(mesh):
    return jax.shard_map(
        shards,
        mesh=mesh,
        in_specs=(
            P("mem", "sub", None, None),
            P("sub", None),
            P("sub", None),
            P("sub", None),
            P(),
            P(),
            P(),
            P(),
            P(),
        ),
        out_specs=P(None, "sub", None, "mem"),
        check_vma=False,
    )
```

```python
import jax
import jax.numpy as jnp
from jax import lax
from jax.experimental import pallas as pl
from jax.experimental.pallas import tpu as pltpu
from jax.sharding import PartitionSpec as P

highest = lax.Precision.HIGHEST
f32 = jnp.float32
bf16 = jnp.bfloat16
TILE = (8, 128)


def dot(a, b, ca, cb, precision=highest):
    return lax.dot_general(
        a, b, (((ca,), (cb,)), ((), ())), precision=precision, preferred_element_type=f32
    )


def narrow(a, b, ca, cb):
    return dot(a, b, ca, cb, None)


def split2(x):
    hi = x.astype(bf16)
    return hi, (x - hi.astype(f32)).astype(bf16)


def split3(x):
    hi = x.astype(bf16)
    rest = x - hi.astype(f32)
    mid = rest.astype(bf16)
    return hi, mid, (rest - mid.astype(f32)).astype(bf16)


def call(kernel, out_shapes, name, operands, scratch=(), space=pltpu.VMEM):
    specs = [pl.BlockSpec(memory_space=space) for _ in operands]
    return pl.pallas_call(
        kernel,
        in_specs=specs,
        out_specs=[pl.BlockSpec(memory_space=pltpu.VMEM) for _ in out_shapes],
        out_shape=[jax.ShapeDtypeStruct(s, f32) for s in out_shapes],
        scratch_shapes=list(scratch),
        compiler_params=pltpu.CompilerParams(vmem_limit_bytes=48 * 2**20),
        name=name,
    )(*operands)


def rows_cols(cells, width):
    if width & (width - 1) == 0:
        shift = width.bit_length() - 1
        return cells >> shift, cells & (width - 1)
    return cells // width, cells % width


def to_columns(rows):
    n = rows.shape[0]
    return jnp.concatenate([rows, jnp.zeros((128 - n, 128), f32)], 0).T


def gaspari(delta_row, delta_col, cutoff_radius, width):
    half = width // 2
    folded = jnp.where(delta_col >= half, delta_col - width, delta_col)
    folded = jnp.where(delta_col < -half, delta_col + width, folded)
    ratio = jnp.sqrt(delta_row * delta_row + folded * folded) / cutoff_radius
    inner = (((-0.25 * ratio + 0.5) * ratio + 0.625) * ratio - 5.0 / 3.0) * ratio * ratio + 1.0
    bounded = jnp.maximum(ratio, 1.0)
    outer = (
        ((((ratio / 12.0 - 0.5) * ratio + 0.625) * ratio + 5.0 / 3.0) * ratio - 5.0) * ratio
        + 4.0
        - 2.0 / (3.0 * bounded)
    )
    return jnp.where(ratio <= 1.0, inner, jnp.where(ratio < 2.0, outer, 0.0))


def taper_kernel(width, batches, nobs, cols_dev):
    def kernel(cell_ref, radius_ref, obs_taper_ref, cell_taper_ref):
        row_here = lax.axis_index("sub").astype(f32)
        col_here = lax.axis_index("mem") * cols_dev
        row_i, col_i = rows_cols(cell_ref[...], width)
        rows = row_i.astype(f32)
        cols = col_i.astype(f32)
        table = to_columns(jnp.concatenate([rows, cols, radius_ref[...]], 0))
        lane = lax.broadcasted_iota(jnp.int32, (1, cols_dev), 1)
        cell_cols = (lane + col_here).astype(f32)
        slot = 0
        for b in range(batches):
            row_j = table[:, b : b + 1]
            col_j = table[:, batches + b : batches + b + 1]
            radius = table[:, 2 * batches + b : 2 * batches + b + 1]
            cell_taper_ref[b] = gaspari(row_here - row_j, cell_cols - col_j, radius, width)
            for e in range(b + 1, batches):
                obs_taper_ref[slot] = gaspari(
                    rows[e : e + 1, :] - row_j, cols[e : e + 1, :] - col_j, radius, width
                )
                slot += 1

    return kernel


def share_kernel(width, comps, batches, nobs, local):
    def kernel(*refs):
        sources, (share_ref, *fetched, arrived) = refs[:6], refs[6:]
        q_ref, cx_ref, cy_ref, d_ref, cell_ref, weight_ref = fetched
        copies = [
            pltpu.make_async_copy(source, target, arrived.at[i])
            for i, (source, target) in enumerate(zip(sources, fetched))
        ]
        for copy in copies:
            copy.start()
        here = lax.axis_index("sub")
        for copy in copies[1:]:
            copy.wait()
        cx, cy, d = cx_ref[...], cy_ref[...], d_ref[...]
        from_south, from_north = jnp.maximum(cy, 0.0) + d, d - jnp.minimum(cy, 0.0)
        even = jnp.full((1, width), here & 1, jnp.int32) == 0
        near = jnp.where(even, from_north, from_south)
        far = jnp.where(even, from_south, from_north)
        scales = [part.astype(f32) for part in split3(jnp.concatenate([near, far], 0))]
        scales = jnp.concatenate(scales + [jnp.zeros((10, width), f32)], 0).astype(bf16)
        row, col = rows_cols(cell_ref[...], width)
        row = jnp.concatenate([row[b : b + 1] for b in range(batches)], 1)
        col = jnp.concatenate([col[b : b + 1] for b in range(batches)], 1)
        away = row - here
        owned, beside = away == 0, (away == 1) | (away == -1)
        place = lax.broadcasted_iota(jnp.int32, (width, batches * nobs), 0)
        own_pick = (place == jnp.where(owned, col, -1)).astype(f32).astype(bf16)
        raw_pick = (place == jnp.where(beside, col, -1)).astype(f32).astype(bf16)
        copies[0].wait()
        q = q_ref[...]
        west = pltpu.roll(q, 1, 1)
        east = pltpu.roll(q, width - 1, 1)
        mine = q - jnp.maximum(cx, 0.0) * (q - west) - jnp.minimum(cx, 0.0) * (east - q)
        mine = mine - jnp.maximum(cy, 0.0) * q + jnp.minimum(cy, 0.0) * q
        mine = mine + d * (east + west - 4.0 * q)
        value = narrow(
            jnp.concatenate(split2(mine) + split2(q), 1),
            jnp.concatenate([own_pick, own_pick, raw_pick, raw_pick], 0),
            1,
            0,
        )
        weight = jnp.concatenate([weight_ref[b] for b in range(batches)], 1)
        value = jnp.sum(value.reshape(-1, comps, batches * nobs) * weight[None], axis=1)
        scale = narrow(scales, own_pick, 1, 0)
        scale = scale[0:2] + scale[2:4] + scale[4:6]
        share = [value, jnp.where(owned, scale, 1.0)]
        fill = share_ref.shape[0] - local - 2
        if fill:
            share.append(jnp.zeros((fill, batches * nobs), f32))
        share_ref[...] = jnp.concatenate(share, 0)

    return kernel


def send_kernel(width, blocks, edge_rows):
    def kernel(q_ref, *send_refs):
        here = lax.axis_index("mem")
        q = q_ref[...]
        count = q.shape[0]
        q_parts = split3(q)
        cols_dev = width // blocks
        lanes = -(-2 * blocks // 128) * 128
        which = lax.broadcasted_iota(jnp.int32, (width, lanes), 1)
        spot = lax.broadcasted_iota(jnp.int32, (width, lanes), 0)
        start = ((which >> 1) ^ here) * cols_dev
        wanted = jnp.where(which & 1 == 0, start - 1, start + cols_dev)
        wanted = jnp.where(wanted < 0, wanted + width, wanted)
        wanted = jnp.where(wanted == width, 0, wanted)
        pick = (spot == wanted).astype(f32).astype(bf16)
        edges = narrow(
            jnp.concatenate(q_parts, 1), jnp.concatenate([pick, pick, pick], 0), 1, 0
        )
        room = -count % 128
        if room:
            edges = jnp.concatenate([edges, jnp.zeros((room, lanes), f32)], 0)
        edges = edges.T
        chunks = -(-count // 128)
        for i, send_ref in enumerate(send_refs):
            first = pl.multiple_of((here ^ i) * cols_dev, cols_dev)
            send_ref[:count, :] = q_ref[:, pl.ds(first, cols_dev)]
            rows = [edges[2 * i : 2 * i + 2, j * 128 : (j + 1) * 128] for j in range(chunks)]
            if edge_rows > 2 * chunks:
                rows.append(jnp.zeros((edge_rows - 2 * chunks, 128), f32))
            send_ref[count:, :] = jnp.concatenate(rows, 0)

    return kernel


def join_kernel(local, first, last):
    def kernel(mine_ref, other_ref, out_ref):
        mine, other = mine_ref[...], other_ref[...]
        at = local
        value = mine[:local] * other[at : at + 1] + other[:local] * mine[at : at + 1]
        if last:
            out_ref[...] = value
        else:
            at = local + 1 if first else local
            scale = mine[at : at + 1] * other[at : at + 1]
            blank = jnp.zeros((out_ref.shape[0] - local - 1, value.shape[1]), f32)
            out_ref[...] = jnp.concatenate([value, scale, blank], 0)

    return kernel


def lane_spread(x, j):
    return jnp.take_along_axis(x, jnp.full(x.shape, j, jnp.int32), axis=1)


def row_spread(x, i):
    return jnp.broadcast_to(x[i : i + 1, :], x.shape)


def factored(cov, sides, error, members, span=4):
    tiles = cov.shape[0] // 8
    lane = lax.broadcasted_iota(jnp.int32, TILE, 1)
    sub = lax.broadcasted_iota(jnp.int32, TILE, 0)
    T = [cov[8 * q : 8 * q + 8, :] for q in range(tiles)]
    V = [sides[8 * q : 8 * q + 8, :] for q in range(tiles)]
    deviation = jnp.broadcast_to(jnp.sqrt(error), TILE)
    is_member = lane < members
    inverse, solved, finished = [], [], []
    for p in range(tiles):
        block = (lane >= 8 * p) & (lane < 8 * p + 8)
        columns = [lane_spread(T[p], 8 * p + c) for c in range(8)]
        s = [[row_spread(columns[c], a) if a >= c else None for c in range(8)] for a in range(8)]
        joined = jnp.where(block, (lane - 8 * p == sub).astype(f32), T[p])
        R = [row_spread(joined, c) for c in range(8)]
        Z = [row_spread(V[p], c) for c in range(8)]
        rd, rs = [None] * 8, [None] * 8
        m = [[None] * 8 for _ in range(8)]
        for c in range(8):
            rd[c] = 1.0 / s[c][c]
            rs[c] = lax.rsqrt(s[c][c])
            root = s[c][c] * rs[c]
            spread = lane_spread(deviation, 8 * p + c)
            Z[c] = Z[c] * jnp.where(is_member, root / (root + spread), 1.0)
            for a in range(c + 1, 8):
                m[a][c] = s[a][c] * rd[c]
            for a in range(c + 1, 8):
                for e in range(c + 1, a + 1):
                    s[a][e] = s[a][e] - (s[a][c] * s[e][c]) * rd[c]
                R[a] = R[a] - m[a][c] * R[c]
                Z[a] = Z[a] - m[a][c] * Z[c]
        X, U = [None] * 8, [None] * 8
        for a in range(7, -1, -1):
            x, u = rd[a] * R[a], rd[a] * Z[a]
            for c in range(a + 1, 8):
                x = x - m[c][a] * X[c]
                u = u - m[c][a] * U[c]
            X[a], U[a] = x, u
        low, side = R[0] * rs[0], Z[0] * rs[0]
        for c in range(1, 8):
            low = jnp.where(sub == c, R[c] * rs[c], low)
            side = jnp.where(sub == c, Z[c] * rs[c], side)
        inverse.append(jnp.where(lane < 8 * p + 8, low, 0.0))
        solved.append(side)
        finished.append((low, side))
        edge = (p // span + 1) * span
        for q in range(p + 1, edge):
            column = [lane_spread(T[q], 8 * p + c) for c in range(8)]
            left, right = X, U
            if q == p + 1:
                for c in range(8):
                    for a in range(c):
                        column[c] = column[c] - m[c][a] * column[a]
                column = [column[c] * rd[c] for c in range(8)]
                left, right = R, Z
            t, v = jnp.where(block, 0.0, T[q]), V[q]
            for c in range(8):
                t = t - column[c] * left[c]
                v = v - column[c] * right[c]
            T[q], V[q] = t, v
        if p + 1 == edge and edge < tiles:
            rows = finished[edge - span : edge]
            upper = jnp.concatenate([low for low, _ in rows], 0)
            keep = [
                jnp.where((lane < 8 * (edge - span + i + 1)) | (lane >= 8 * edge), low, 0.0)
                for i, (low, _) in enumerate(rows)
            ]
            side_rows = jnp.concatenate([side for _, side in rows], 0)
            taken = products(upper, jnp.concatenate([jnp.concatenate(keep, 0), side_rows], 1))
            inside = (lane >= 8 * (edge - span)) & (lane < 8 * edge)
            for q in range(edge, tiles):
                at = slice(8 * q, 8 * q + 8)
                T[q] = jnp.where(inside, 0.0, T[q]) - taken[at, :128]
                V[q] = V[q] - taken[at, 128:]
    return jnp.concatenate(inverse, 0), jnp.concatenate(solved, 0)


def products(a, b):
    ah, am, al = split3(a)
    bh, bm, bl = split3(b)
    return narrow(
        jnp.concatenate([al, am, ah, am, ah, ah], 0),
        jnp.concatenate([bh, bm, bl, bh, bm, bh], 0),
        0,
        0,
    )


def coefficients(observed, value, error):
    members, nobs = observed.shape
    mean = jnp.sum(observed, axis=0, keepdims=True) / members
    anomaly = observed - mean
    row = lax.broadcasted_iota(jnp.int32, (nobs, nobs), 0)
    col = lax.broadcasted_iota(jnp.int32, (nobs, nobs), 1)
    cov = products(anomaly, anomaly) / (members - 1) + jnp.where(row == col, error, 0.0)
    sides = jnp.concatenate(
        [anomaly, value - mean, jnp.zeros((nobs - members - 1, nobs), f32)], 0
    ).T
    inverse, solved = factored(cov, sides, error, members)
    back = products(solved, inverse)
    return anomaly, back[members : members + 1] - back[:members]


def chain_kernel(part, batches, nobs, pieces):
    def kernel(*refs):
        y_refs, refs = refs[:pieces], refs[pieces:]
        value_ref, error_ref, taper_ref, anomaly_ref, coeff_ref, *later_ref = refs
        blocks = [ref[...] for ref in y_refs]
        step = 1
        while step < pieces:
            odd = jnp.full(blocks[0].shape, lax.axis_index("mem") & step, jnp.int32) != 0
            blocks = [jnp.where(odd, blocks[k ^ step], blocks[k]) for k in range(pieces)]
            step *= 2
        observed = jnp.concatenate(blocks, 0) if pieces > 1 else blocks[0]
        members = observed.shape[0]
        first = batches - observed.shape[1] // nobs
        Y = {b: observed[:, nobs * (b - first) : nobs * (b - first + 1)] for b in range(first, batches)}
        for b in part:
            anomaly, coeff = coefficients(Y[b], value_ref[b : b + 1, :], error_ref[b : b + 1, :])
            anomaly_ref[b - first] = anomaly
            coeff_ref[b - first] = coeff
            after = range(b + 1, batches)
            if after:
                slot = b * batches - b * (b + 1) // 2
                later = jnp.concatenate([Y[e] for e in after], 1)
                spread = later - jnp.sum(later, axis=0, keepdims=True) / members
                taper = jnp.concatenate([taper_ref[slot + i] for i in range(len(after))], 1)
                hi, lo = split2(anomaly)
                fill = -3 * members % 128
                left = jnp.concatenate([hi, lo, hi, jnp.zeros((fill, nobs), bf16)], 0)
                hi, lo = split2(spread)
                blank = jnp.zeros((fill, later.shape[1]), bf16)
                gain = narrow(left, jnp.concatenate([hi, hi, lo, blank], 0), 0, 0)
                gain = gain / (members - 1) * taper
                coeff_hi, coeff_lo = split2(coeff)
                hi, lo = split2(gain)
                left = jnp.concatenate([coeff_hi, coeff_hi, coeff_lo], 1)
                later = later + narrow(left, jnp.concatenate([hi, lo, hi], 0), 1, 0)
                for i, e in enumerate(after):
                    Y[e] = later[:, nobs * i : nobs * (i + 1)]
        for e in range(part[-1] + 1, batches):
            at = e - part[-1] - 1
            later_ref[0][:, nobs * at : nobs * (at + 1)] = Y[e]

    return kernel


def update_kernel(width, comps, batches, members, cols_dev, count, blocks, bands, group):
    def kernel(
        *refs,
    ):
        own_refs, halos, refs = refs[:blocks], refs[blocks : blocks + 4], refs[blocks + 4 :]
        near_refs, far_refs = (
            [ref.at[i] for ref in halos[at : at + 2] for i in range(ref.shape[0])] for at in (0, 2)
        )
        cx_ref, cy_ref, d_ref, taper_ref, *pair_refs, out_ref, grid_ref = refs
        pairs = [
            (pair_refs[i][k], pair_refs[i + 1][k])
            for i in range(0, len(pair_refs), 2)
            for k in range(pair_refs[i].shape[0])
        ]
        start = pl.multiple_of(lax.axis_index("mem") * cols_dev, cols_dev)
        cx = cx_ref[:, pl.ds(start, cols_dev)]
        cy = cy_ref[:, pl.ds(start, cols_dev)]
        d = d_ref[:, pl.ds(start, cols_dev)]
        lane = lax.broadcasted_iota(jnp.int32, (1, cols_dev), 1)
        band = jnp.full((1, cols_dev), lax.axis_index("sub"), jnp.int32)
        even = band & 1 == 0
        outermost = (band == 0) | (band == bands - 1)
        from_south, from_north = jnp.maximum(cy, 0.0), -jnp.minimum(cy, 0.0)
        from_near = jnp.where(even, from_north, from_south)
        from_far = jnp.where(even, from_south, from_north)
        from_west, from_east = jnp.maximum(cx, 0.0), -jnp.minimum(cx, 0.0)
        for s, (own_ref, near_ref, far_ref) in enumerate(zip(own_refs, near_refs, far_refs)):
            base = pl.multiple_of((lax.axis_index("mem") ^ s) * count, 8)
            outer = to_columns(own_ref[count:, :])
            for j in range(-(-count // 128)):
                size = min(128, count - 128 * j)
                at = slice(128 * j, 128 * j + size)
                q, near = own_ref[at, :], near_ref[at, :]
                far = jnp.where(outermost, 0.0, far_ref[at, :])
                west = jnp.where(lane == 0, outer[:size, 2 * j : 2 * j + 1], pltpu.roll(q, 1, 1))
                east = jnp.where(
                    lane == cols_dev - 1,
                    outer[:size, 2 * j + 1 : 2 * j + 2],
                    pltpu.roll(q, cols_dev - 1, 1),
                )
                x = q - from_west * (q - west) - from_east * (q - east)
                x = x - from_near * (q - near) - from_far * (q - far)
                x = x + d * (east + west + near + far - 4.0 * q)
                grid_ref[pl.ds(base + 128 * j, size), :] = x
        left, right, tapers = [], [], []
        nobs = taper_ref.shape[1]
        fill = -3 * members % 128
        blank = jnp.zeros((fill, group * cols_dev), bf16)
        for b in range(batches):
            hi, lo = split2(pairs[b][0])
            left.append(jnp.concatenate([hi, lo, hi, jnp.zeros((fill, nobs), bf16)], 0))
            hi, lo = split2(pairs[b][1])
            right.append(jnp.concatenate([hi, hi, lo], 1))
            tapers.append(jnp.tile(taper_ref[b] / (members - 1), (1, group)))
        for first in range(0, comps, group):
            x = jnp.concatenate(
                [grid_ref[pl.ds(first + i, members, comps), :] for i in range(group)], 1
            )
            for b in range(batches):
                spread = x - jnp.sum(x, axis=0, keepdims=True) / members
                hi, lo = split2(spread)
                gain = narrow(left[b], jnp.concatenate([hi, hi, lo, blank], 0), 0, 0) * tapers[b]
                hi, lo = split2(gain)
                x = x + narrow(right[b], jnp.concatenate([hi, lo, hi], 0), 1, 0)
            for i in range(group):
                out_ref[pl.ds(first + i, members, comps), :] = x[:, i * cols_dev : (i + 1) * cols_dev]

    return kernel


def shards(
    prior_sample_array,
    courant_x,
    courant_y,
    diffusion,
    obs_cell,
    obs_value,
    obs_error,
    obs_weight,
    taper_radius,
):
    local, rows_dev, comps, width = prior_sample_array.shape
    blocks = lax.axis_size("mem")
    bands = lax.axis_size("sub")
    cols_dev = width // blocks
    members = local * blocks
    batches, nobs = obs_cell.shape
    count = local * comps
    edge_rows = -(-(2 * -(-count // 128)) // 8) * 8
    assert bands & (bands - 1) == 0 and bands > 2 and blocks & (blocks - 1) == 0 and rows_dev == 1 and batches == 4 and cols_dev == 128 and nobs == 128

    share_rows = -(-(local + 2) // 8) * 8
    prior = prior_sample_array.reshape(count, width)
    sends = call(
        send_kernel(width, blocks, edge_rows),
        [(count + edge_rows, cols_dev)] * blocks,
        "send",
        (prior,),
    )
    grid = [sends[0]] + [
        lax.ppermute(sends[k], "mem", [(i, i ^ k) for i in range(blocks)]) for k in range(1, blocks)
    ]
    held_x, *sends = lax.optimization_barrier((courant_x, *sends))
    sources = (prior, held_x, courant_y, diffusion, obs_cell, obs_weight.transpose(0, 2, 1))
    (share,) = call(
        share_kernel(width, comps, batches, nobs, local),
        [(share_rows, batches * nobs)],
        "share",
        sources,
        [pltpu.VMEM(x.shape, x.dtype) for x in sources] + [pltpu.SemaphoreType.DMA((6,))],
        pl.ANY,
    )
    obs_taper, cell_taper = call(
        taper_kernel(width, batches, nobs, cols_dev),
        [(batches * (batches - 1) // 2, nobs, nobs), (batches, nobs, cols_dev)],
        "tapers",
        (obs_cell, taper_radius),
    )
    swap = [(i, i ^ 1) for i in range(bands)]
    onward = [(i, i + 2) for i in range(0, bands - 2, 2)] + [(i, i - 2) for i in range(3, bands, 2)]
    around = onward + [(bands - 2, 0), (1, bands - 1)]
    across = onward + [(1, 0), (bands - 2, bands - 1)]
    middle = blocks // 2
    parts = (slice(0, middle), slice(middle, blocks))
    near, far = [], []
    step = 1
    while step < bands:
        other = lax.ppermute(share, "sub", [(i, i ^ step) for i in range(bands)])
        if step == 1:
            other, obs_taper, cell_taper = lax.optimization_barrier((other, obs_taper, cell_taper))
        last = 2 * step == bands
        (share,) = call(
            join_kernel(local, step == 1, last),
            [(local if last else share_rows, batches * nobs)],
            "join",
            (share, other),
        )
        if step in (1, 2):
            part = parts[step // 2]
            share, *grid[part] = lax.optimization_barrier((share, *grid[part]))
            near.append(lax.ppermute(jnp.stack(grid[part]), "sub", swap))
        step *= 2
    observed = {0: share}
    step = blocks // 2
    while step:
        to = [(i, i ^ step) for i in range(blocks)]
        observed.update({k ^ step: lax.ppermute(x, "mem", to) for k, x in observed.items()})
        step //= 2
    observed = [observed[k] for k in range(blocks)]
    pairs = []
    for b in range(batches):
        part = range(b, b + 1)
        if b < 2:
            *observed, near[b] = lax.optimization_barrier((*observed, near[b]))
            far.append(lax.ppermute(near[b], "sub", (around, across)[b]))
        if b == 3:
            *observed, far[0] = lax.optimization_barrier((*observed, far[0]))
        outs = call(
            chain_kernel(part, batches, nobs, len(observed)),
            [(len(part), members, nobs)] * 2
            + [(members, (batches - part[-1] - 1) * nobs)] * (part[-1] + 1 < batches),
            "chain",
            (*observed, obs_value, obs_error, obs_taper),
        )
        pairs += outs[:2]
        observed = outs[2:]
    (out,) = call(
        update_kernel(width, comps, batches, members, cols_dev, count, blocks, bands, comps),
        [(members * comps, cols_dev)],
        "update",
        (*grid, *near, *far, courant_x, courant_y, diffusion, cell_taper, *pairs),
        (pltpu.VMEM((members * comps, cols_dev), f32),),
    )
    return out.reshape(members, rows_dev, comps, cols_dev)


def solution(mesh):
    return jax.shard_map(
        shards,
        mesh=mesh,
        in_specs=(
            P("mem", "sub", None, None),
            P("sub", None),
            P("sub", None),
            P("sub", None),
            P(),
            P(),
            P(),
            P(),
            P(),
        ),
        out_specs=P(None, "sub", None, "mem"),
        check_vma=False,
    )
```

```python
import jax
import jax.numpy as jnp
from jax import lax
from jax.experimental import pallas as pl
from jax.experimental.pallas import tpu as pltpu
from jax.sharding import PartitionSpec as P

highest = lax.Precision.HIGHEST
f32 = jnp.float32
bf16 = jnp.bfloat16
TILE = (8, 128)


def dot(a, b, ca, cb, precision=highest):
    return lax.dot_general(
        a, b, (((ca,), (cb,)), ((), ())), precision=precision, preferred_element_type=f32
    )


def narrow(a, b, ca, cb):
    return dot(a, b, ca, cb, None)


def split2(x):
    hi = x.astype(bf16)
    return hi, (x - hi.astype(f32)).astype(bf16)


def split3(x):
    hi = x.astype(bf16)
    rest = x - hi.astype(f32)
    mid = rest.astype(bf16)
    return hi, mid, (rest - mid.astype(f32)).astype(bf16)


def call(kernel, out_shapes, name, operands, scratch=(), space=pltpu.VMEM):
    specs = [pl.BlockSpec(memory_space=space) for _ in operands]
    return pl.pallas_call(
        kernel,
        in_specs=specs,
        out_specs=[pl.BlockSpec(memory_space=pltpu.VMEM) for _ in out_shapes],
        out_shape=[jax.ShapeDtypeStruct(s, f32) for s in out_shapes],
        scratch_shapes=list(scratch),
        compiler_params=pltpu.CompilerParams(vmem_limit_bytes=48 * 2**20),
        name=name,
    )(*operands)


def rows_cols(cells, width):
    if width & (width - 1) == 0:
        shift = width.bit_length() - 1
        return cells >> shift, cells & (width - 1)
    return cells // width, cells % width


def to_columns(rows):
    n = rows.shape[0]
    return jnp.concatenate([rows, jnp.zeros((128 - n, 128), f32)], 0).T


def gaspari(delta_row, delta_col, cutoff_radius, width):
    half = width // 2
    folded = jnp.where(delta_col >= half, delta_col - width, delta_col)
    folded = jnp.where(delta_col < -half, delta_col + width, folded)
    ratio = jnp.sqrt(delta_row * delta_row + folded * folded) / cutoff_radius
    inner = (((-0.25 * ratio + 0.5) * ratio + 0.625) * ratio - 5.0 / 3.0) * ratio * ratio + 1.0
    bounded = jnp.maximum(ratio, 1.0)
    outer = (
        ((((ratio / 12.0 - 0.5) * ratio + 0.625) * ratio + 5.0 / 3.0) * ratio - 5.0) * ratio
        + 4.0
        - 2.0 / (3.0 * bounded)
    )
    return jnp.where(ratio <= 1.0, inner, jnp.where(ratio < 2.0, outer, 0.0))


def taper_kernel(width, batches, nobs, cols_dev):
    def kernel(cell_ref, radius_ref, obs_taper_ref, cell_taper_ref):
        row_here = lax.axis_index("sub").astype(f32)
        col_here = lax.axis_index("mem") * cols_dev
        row_i, col_i = rows_cols(cell_ref[...], width)
        rows = row_i.astype(f32)
        cols = col_i.astype(f32)
        table = to_columns(jnp.concatenate([rows, cols, radius_ref[...]], 0))
        lane = lax.broadcasted_iota(jnp.int32, (1, cols_dev), 1)
        cell_cols = (lane + col_here).astype(f32)
        slot = 0
        for b in range(batches):
            row_j = table[:, b : b + 1]
            col_j = table[:, batches + b : batches + b + 1]
            radius = table[:, 2 * batches + b : 2 * batches + b + 1]
            cell_taper_ref[b] = gaspari(row_here - row_j, cell_cols - col_j, radius, width)
            for e in range(b + 1, batches):
                obs_taper_ref[slot] = gaspari(
                    rows[e : e + 1, :] - row_j, cols[e : e + 1, :] - col_j, radius, width
                )
                slot += 1

    return kernel


def share_kernel(width, comps, batches, nobs, local):
    def kernel(*refs):
        sources, (share_ref, *fetched, arrived) = refs[:6], refs[6:]
        q_ref, cx_ref, cy_ref, d_ref, cell_ref, weight_ref = fetched
        copies = [
            pltpu.make_async_copy(source, target, arrived.at[i])
            for i, (source, target) in enumerate(zip(sources, fetched))
        ]
        for copy in copies:
            copy.start()
        here = lax.axis_index("sub")
        for copy in copies[1:]:
            copy.wait()
        cx, cy, d = cx_ref[...], cy_ref[...], d_ref[...]
        from_south, from_north = jnp.maximum(cy, 0.0) + d, d - jnp.minimum(cy, 0.0)
        even = jnp.full((1, width), here & 1, jnp.int32) == 0
        near = jnp.where(even, from_north, from_south)
        far = jnp.where(even, from_south, from_north)
        scales = [part.astype(f32) for part in split3(jnp.concatenate([near, far], 0))]
        scales = jnp.concatenate(scales + [jnp.zeros((10, width), f32)], 0).astype(bf16)
        row, col = rows_cols(cell_ref[...], width)
        row = jnp.concatenate([row[b : b + 1] for b in range(batches)], 1)
        col = jnp.concatenate([col[b : b + 1] for b in range(batches)], 1)
        away = row - here
        owned, beside = away == 0, (away == 1) | (away == -1)
        place = lax.broadcasted_iota(jnp.int32, (width, batches * nobs), 0)
        own_pick = (place == jnp.where(owned, col, -1)).astype(f32).astype(bf16)
        raw_pick = (place == jnp.where(beside, col, -1)).astype(f32).astype(bf16)
        copies[0].wait()
        q = q_ref[...]
        west = pltpu.roll(q, 1, 1)
        east = pltpu.roll(q, width - 1, 1)
        mine = q - jnp.maximum(cx, 0.0) * (q - west) - jnp.minimum(cx, 0.0) * (east - q)
        mine = mine - jnp.maximum(cy, 0.0) * q + jnp.minimum(cy, 0.0) * q
        mine = mine + d * (east + west - 4.0 * q)
        value = narrow(
            jnp.concatenate(split2(mine) + split2(q), 1),
            jnp.concatenate([own_pick, own_pick, raw_pick, raw_pick], 0),
            1,
            0,
        )
        weight = jnp.concatenate([weight_ref[b] for b in range(batches)], 1)
        value = jnp.sum(value.reshape(-1, comps, batches * nobs) * weight[None], axis=1)
        scale = narrow(scales, own_pick, 1, 0)
        scale = scale[0:2] + scale[2:4] + scale[4:6]
        share = [value, jnp.where(owned, scale, 1.0)]
        fill = share_ref.shape[0] - local - 2
        if fill:
            share.append(jnp.zeros((fill, batches * nobs), f32))
        share_ref[...] = jnp.concatenate(share, 0)

    return kernel


def send_kernel(width, blocks, edge_rows):
    def kernel(q_ref, *send_refs):
        here = lax.axis_index("mem")
        q = q_ref[...]
        count = q.shape[0]
        q_parts = split3(q)
        cols_dev = width // blocks
        lanes = -(-2 * blocks // 128) * 128
        which = lax.broadcasted_iota(jnp.int32, (width, lanes), 1)
        spot = lax.broadcasted_iota(jnp.int32, (width, lanes), 0)
        start = ((which >> 1) ^ here) * cols_dev
        wanted = jnp.where(which & 1 == 0, start - 1, start + cols_dev)
        wanted = jnp.where(wanted < 0, wanted + width, wanted)
        wanted = jnp.where(wanted == width, 0, wanted)
        pick = (spot == wanted).astype(f32).astype(bf16)
        edges = narrow(
            jnp.concatenate(q_parts, 1), jnp.concatenate([pick, pick, pick], 0), 1, 0
        )
        room = -count % 128
        if room:
            edges = jnp.concatenate([edges, jnp.zeros((room, lanes), f32)], 0)
        edges = edges.T
        chunks = -(-count // 128)
        for i, send_ref in enumerate(send_refs):
            first = pl.multiple_of((here ^ i) * cols_dev, cols_dev)
            send_ref[:count, :] = q_ref[:, pl.ds(first, cols_dev)]
            rows = [edges[2 * i : 2 * i + 2, j * 128 : (j + 1) * 128] for j in range(chunks)]
            if edge_rows > 2 * chunks:
                rows.append(jnp.zeros((edge_rows - 2 * chunks, 128), f32))
            send_ref[count:, :] = jnp.concatenate(rows, 0)

    return kernel


def join_kernel(local, first, last):
    def kernel(mine_ref, other_ref, out_ref):
        mine, other = mine_ref[...], other_ref[...]
        at = local
        value = mine[:local] * other[at : at + 1] + other[:local] * mine[at : at + 1]
        if last:
            out_ref[...] = value
        else:
            at = local + 1 if first else local
            scale = mine[at : at + 1] * other[at : at + 1]
            blank = jnp.zeros((out_ref.shape[0] - local - 1, value.shape[1]), f32)
            out_ref[...] = jnp.concatenate([value, scale, blank], 0)

    return kernel


def lane_spread(x, j):
    return jnp.take_along_axis(x, jnp.full(x.shape, j, jnp.int32), axis=1)


def row_spread(x, i):
    return jnp.broadcast_to(x[i : i + 1, :], x.shape)


def factored(cov, sides, error, members, span=4):
    tiles = cov.shape[0] // 8
    lane = lax.broadcasted_iota(jnp.int32, TILE, 1)
    sub = lax.broadcasted_iota(jnp.int32, TILE, 0)
    T = [cov[8 * q : 8 * q + 8, :] for q in range(tiles)]
    V = [sides[8 * q : 8 * q + 8, :] for q in range(tiles)]
    deviation = jnp.broadcast_to(jnp.sqrt(error), TILE)
    is_member = lane < members
    inverse, solved, finished = [], [], []
    for p in range(tiles):
        block = (lane >= 8 * p) & (lane < 8 * p + 8)
        columns = [lane_spread(T[p], 8 * p + c) for c in range(8)]
        s = [[row_spread(columns[c], a) if a >= c else None for c in range(8)] for a in range(8)]
        joined = jnp.where(block, (lane - 8 * p == sub).astype(f32), T[p])
        R = [row_spread(joined, c) for c in range(8)]
        Z = [row_spread(V[p], c) for c in range(8)]
        rd, rs = [None] * 8, [None] * 8
        m = [[None] * 8 for _ in range(8)]
        for c in range(8):
            rd[c] = 1.0 / s[c][c]
            rs[c] = lax.rsqrt(s[c][c])
            root = s[c][c] * rs[c]
            spread = lane_spread(deviation, 8 * p + c)
            Z[c] = Z[c] * jnp.where(is_member, root / (root + spread), 1.0)
            for a in range(c + 1, 8):
                m[a][c] = s[a][c] * rd[c]
            for a in range(c + 1, 8):
                for e in range(c + 1, a + 1):
                    s[a][e] = s[a][e] - (s[a][c] * s[e][c]) * rd[c]
                R[a] = R[a] - m[a][c] * R[c]
                Z[a] = Z[a] - m[a][c] * Z[c]
        X, U = [None] * 8, [None] * 8
        for a in range(7, -1, -1):
            x, u = rd[a] * R[a], rd[a] * Z[a]
            for c in range(a + 1, 8):
                x = x - m[c][a] * X[c]
                u = u - m[c][a] * U[c]
            X[a], U[a] = x, u
        low, side = R[0] * rs[0], Z[0] * rs[0]
        for c in range(1, 8):
            low = jnp.where(sub == c, R[c] * rs[c], low)
            side = jnp.where(sub == c, Z[c] * rs[c], side)
        inverse.append(jnp.where(lane < 8 * p + 8, low, 0.0))
        solved.append(side)
        finished.append((low, side))
        edge = (p // span + 1) * span
        for q in range(p + 1, edge):
            column = [lane_spread(T[q], 8 * p + c) for c in range(8)]
            left, right = X, U
            if q == p + 1:
                for c in range(8):
                    for a in range(c):
                        column[c] = column[c] - m[c][a] * column[a]
                column = [column[c] * rd[c] for c in range(8)]
                left, right = R, Z
            t, v = jnp.where(block, 0.0, T[q]), V[q]
            for c in range(8):
                t = t - column[c] * left[c]
                v = v - column[c] * right[c]
            T[q], V[q] = t, v
        if p + 1 == edge and edge < tiles:
            rows = finished[edge - span : edge]
            upper = jnp.concatenate([low for low, _ in rows], 0)
            keep = [
                jnp.where((lane < 8 * (edge - span + i + 1)) | (lane >= 8 * edge), low, 0.0)
                for i, (low, _) in enumerate(rows)
            ]
            side_rows = jnp.concatenate([side for _, side in rows], 0)
            taken = products(upper, jnp.concatenate([jnp.concatenate(keep, 0), side_rows], 1))
            inside = (lane >= 8 * (edge - span)) & (lane < 8 * edge)
            for q in range(edge, tiles):
                at = slice(8 * q, 8 * q + 8)
                T[q] = jnp.where(inside, 0.0, T[q]) - taken[at, :128]
                V[q] = V[q] - taken[at, 128:]
    return jnp.concatenate(inverse, 0), jnp.concatenate(solved, 0)


def products(a, b):
    ah, am, al = split3(a)
    bh, bm, bl = split3(b)
    return narrow(
        jnp.concatenate([al, am, ah, am, ah, ah], 0),
        jnp.concatenate([bh, bm, bl, bh, bm, bh], 0),
        0,
        0,
    )


def coefficients(observed, value, error):
    members, nobs = observed.shape
    mean = jnp.sum(observed, axis=0, keepdims=True) / members
    anomaly = observed - mean
    row = lax.broadcasted_iota(jnp.int32, (nobs, nobs), 0)
    col = lax.broadcasted_iota(jnp.int32, (nobs, nobs), 1)
    cov = products(anomaly, anomaly) / (members - 1) + jnp.where(row == col, error, 0.0)
    sides = jnp.concatenate(
        [anomaly, value - mean, jnp.zeros((nobs - members - 1, nobs), f32)], 0
    ).T
    inverse, solved = factored(cov, sides, error, members)
    back = products(solved, inverse)
    return anomaly, back[members : members + 1] - back[:members]


def chain_kernel(part, batches, nobs, pieces):
    def kernel(*refs):
        y_refs, refs = refs[:pieces], refs[pieces:]
        value_ref, error_ref, taper_ref, anomaly_ref, coeff_ref, *later_ref = refs
        blocks = [ref[...] for ref in y_refs]
        step = 1
        while step < pieces:
            odd = jnp.full(blocks[0].shape, lax.axis_index("mem") & step, jnp.int32) != 0
            blocks = [jnp.where(odd, blocks[k ^ step], blocks[k]) for k in range(pieces)]
            step *= 2
        observed = jnp.concatenate(blocks, 0) if pieces > 1 else blocks[0]
        members = observed.shape[0]
        first = batches - observed.shape[1] // nobs
        Y = {b: observed[:, nobs * (b - first) : nobs * (b - first + 1)] for b in range(first, batches)}
        for b in part:
            anomaly, coeff = coefficients(Y[b], value_ref[b : b + 1, :], error_ref[b : b + 1, :])
            anomaly_ref[b - first] = anomaly
            coeff_ref[b - first] = coeff
            after = range(b + 1, batches)
            if after:
                slot = b * batches - b * (b + 1) // 2
                later = jnp.concatenate([Y[e] for e in after], 1)
                spread = later - jnp.sum(later, axis=0, keepdims=True) / members
                taper = jnp.concatenate([taper_ref[slot + i] for i in range(len(after))], 1)
                hi, lo = split2(anomaly)
                fill = -3 * members % 128
                left = jnp.concatenate([hi, lo, hi, jnp.zeros((fill, nobs), bf16)], 0)
                hi, lo = split2(spread)
                blank = jnp.zeros((fill, later.shape[1]), bf16)
                gain = narrow(left, jnp.concatenate([hi, hi, lo, blank], 0), 0, 0)
                gain = gain / (members - 1) * taper
                coeff_hi, coeff_lo = split2(coeff)
                hi, lo = split2(gain)
                left = jnp.concatenate([coeff_hi, coeff_hi, coeff_lo], 1)
                later = later + narrow(left, jnp.concatenate([hi, lo, hi], 0), 1, 0)
                for i, e in enumerate(after):
                    Y[e] = later[:, nobs * i : nobs * (i + 1)]
        for e in range(part[-1] + 1, batches):
            at = e - part[-1] - 1
            later_ref[0][:, nobs * at : nobs * (at + 1)] = Y[e]

    return kernel


def halo_scales(cy, bands):
    band = jnp.full(cy.shape, lax.axis_index("sub"), jnp.int32)
    even = band & 1 == 0
    from_south, from_north = jnp.maximum(cy, 0.0), -jnp.minimum(cy, 0.0)
    from_near = jnp.where(even, from_north, from_south)
    from_far = jnp.where(even, from_south, from_north)
    return from_near, from_far, (band == 0) | (band == bands - 1)


def forecast_kernel(cols_dev, count, blocks, bands):
    def kernel(*refs):
        own_refs, halos, refs = refs[:blocks], refs[blocks : blocks + 3], refs[blocks + 3 :]
        near_refs = [ref.at[i] for ref in halos[:2] for i in range(ref.shape[0])]
        far_refs = [halos[2].at[i] for i in range(halos[2].shape[0])]
        cx_ref, cy_ref, d_ref, grid_ref = refs
        start = pl.multiple_of(lax.axis_index("mem") * cols_dev, cols_dev)
        cx = cx_ref[:, pl.ds(start, cols_dev)]
        cy = cy_ref[:, pl.ds(start, cols_dev)]
        d = d_ref[:, pl.ds(start, cols_dev)]
        lane = lax.broadcasted_iota(jnp.int32, (1, cols_dev), 1)
        from_near, from_far, outermost = halo_scales(cy, bands)
        from_west, from_east = jnp.maximum(cx, 0.0), -jnp.minimum(cx, 0.0)
        for s, (own_ref, near_ref) in enumerate(zip(own_refs, near_refs)):
            base = pl.multiple_of((lax.axis_index("mem") ^ s) * count, 8)
            outer = to_columns(own_ref[count:, :])
            for j in range(-(-count // 128)):
                size = min(128, count - 128 * j)
                at = slice(128 * j, 128 * j + size)
                q, near = own_ref[at, :], near_ref[at, :]
                west = jnp.where(lane == 0, outer[:size, 2 * j : 2 * j + 1], pltpu.roll(q, 1, 1))
                east = jnp.where(
                    lane == cols_dev - 1,
                    outer[:size, 2 * j + 1 : 2 * j + 2],
                    pltpu.roll(q, cols_dev - 1, 1),
                )
                x = q - from_west * (q - west) - from_east * (q - east)
                if s < len(far_refs):
                    far = jnp.where(outermost, 0.0, far_refs[s][at, :])
                    x = x - from_near * (q - near) - from_far * (q - far)
                    x = x + d * (east + west + near + far - 4.0 * q)
                else:
                    x = x - from_near * (q - near) - from_far * q
                    x = x + d * (east + west + near - 4.0 * q)
                grid_ref[pl.ds(base + 128 * j, size), :] = x

    return kernel


def update_kernel(comps, batches, members, cols_dev, count, bands, group):
    def kernel(cells_ref, far_ref, cy_ref, d_ref, taper_ref, *refs):
        *pair_refs, out_ref, grid_ref = refs
        pairs = [
            (pair_refs[i][k], pair_refs[i + 1][k])
            for i in range(0, len(pair_refs), 2)
            for k in range(pair_refs[i].shape[0])
        ]
        start = pl.multiple_of(lax.axis_index("mem") * cols_dev, cols_dev)
        _, from_far, outermost = halo_scales(cy_ref[:, pl.ds(start, cols_dev)], bands)
        scale = jnp.where(outermost, 0.0, from_far + d_ref[:, pl.ds(start, cols_dev)])
        late = far_ref.shape[0]
        for s in range(2 * late):
            at = pl.ds(pl.multiple_of((lax.axis_index("mem") ^ s) * count, 8), count)
            cells = cells_ref[at, :]
            grid_ref[at, :] = cells if s < late else cells + scale * far_ref[s - late, :count, :]
        left, right, tapers = [], [], []
        nobs = taper_ref.shape[1]
        fill = -3 * members % 128
        blank = jnp.zeros((fill, group * cols_dev), bf16)
        for b in range(batches):
            hi, lo = split2(pairs[b][0])
            left.append(jnp.concatenate([hi, lo, hi, jnp.zeros((fill, nobs), bf16)], 0))
            hi, lo = split2(pairs[b][1])
            right.append(jnp.concatenate([hi, hi, lo], 1))
            tapers.append(jnp.tile(taper_ref[b] / (members - 1), (1, group)))
        for first in range(0, comps, group):
            x = jnp.concatenate(
                [grid_ref[pl.ds(first + i, members, comps), :] for i in range(group)], 1
            )
            for b in range(batches):
                spread = x - jnp.sum(x, axis=0, keepdims=True) / members
                hi, lo = split2(spread)
                gain = narrow(left[b], jnp.concatenate([hi, hi, lo, blank], 0), 0, 0) * tapers[b]
                hi, lo = split2(gain)
                x = x + narrow(right[b], jnp.concatenate([hi, lo, hi], 0), 1, 0)
            for i in range(group):
                out_ref[pl.ds(first + i, members, comps), :] = x[:, i * cols_dev : (i + 1) * cols_dev]

    return kernel


def shards(
    prior_sample_array,
    courant_x,
    courant_y,
    diffusion,
    obs_cell,
    obs_value,
    obs_error,
    obs_weight,
    taper_radius,
):
    local, rows_dev, comps, width = prior_sample_array.shape
    blocks = lax.axis_size("mem")
    bands = lax.axis_size("sub")
    cols_dev = width // blocks
    members = local * blocks
    batches, nobs = obs_cell.shape
    count = local * comps
    edge_rows = -(-(2 * -(-count // 128)) // 8) * 8
    assert bands & (bands - 1) == 0 and bands > 2 and blocks & (blocks - 1) == 0 and rows_dev == 1 and batches == 4 and cols_dev == 128 and nobs == 128

    share_rows = -(-(local + 2) // 8) * 8
    prior = prior_sample_array.reshape(count, width)
    sends = call(
        send_kernel(width, blocks, edge_rows),
        [(count + edge_rows, cols_dev)] * blocks,
        "send",
        (prior,),
    )
    grid = [sends[0]] + [
        lax.ppermute(sends[k], "mem", [(i, i ^ k) for i in range(blocks)]) for k in range(1, blocks)
    ]
    held_x, *sends = lax.optimization_barrier((courant_x, *sends))
    sources = (prior, held_x, courant_y, diffusion, obs_cell, obs_weight.transpose(0, 2, 1))
    (share,) = call(
        share_kernel(width, comps, batches, nobs, local),
        [(share_rows, batches * nobs)],
        "share",
        sources,
        [pltpu.VMEM(x.shape, x.dtype) for x in sources] + [pltpu.SemaphoreType.DMA((6,))],
        pl.ANY,
    )
    obs_taper, cell_taper = call(
        taper_kernel(width, batches, nobs, cols_dev),
        [(batches * (batches - 1) // 2, nobs, nobs), (batches, nobs, cols_dev)],
        "tapers",
        (obs_cell, taper_radius),
    )
    swap = [(i, i ^ 1) for i in range(bands)]
    onward = [(i, i + 2) for i in range(0, bands - 2, 2)] + [(i, i - 2) for i in range(3, bands, 2)]
    around = onward + [(bands - 2, 0), (1, bands - 1)]
    across = onward + [(1, 0), (bands - 2, bands - 1)]
    middle = blocks // 2
    parts = (slice(0, middle), slice(middle, blocks))
    near, far = [], []
    step = 1
    while step < bands:
        other = lax.ppermute(share, "sub", [(i, i ^ step) for i in range(bands)])
        if step == 1:
            other, obs_taper, cell_taper = lax.optimization_barrier((other, obs_taper, cell_taper))
        last = 2 * step == bands
        (share,) = call(
            join_kernel(local, step == 1, last),
            [(local if last else share_rows, batches * nobs)],
            "join",
            (share, other),
        )
        if step in (1, 2):
            part = parts[step // 2]
            share, *grid[part] = lax.optimization_barrier((share, *grid[part]))
            near.append(lax.ppermute(jnp.stack(grid[part]), "sub", swap))
        step *= 2
    observed = {0: share}
    step = blocks // 2
    while step:
        to = [(i, i ^ step) for i in range(blocks)]
        observed.update({k ^ step: lax.ppermute(x, "mem", to) for k, x in observed.items()})
        step //= 2
    observed = [observed[k] for k in range(blocks)]
    pairs = []
    for b in range(batches):
        part = range(b, b + 1)
        if b < 2:
            *observed, near[b] = lax.optimization_barrier((*observed, near[b]))
            far.append(lax.ppermute(near[b], "sub", (around, across)[b]))
        if b == 3:
            *observed, far[0] = lax.optimization_barrier((*observed, far[0]))
        outs = call(
            chain_kernel(part, batches, nobs, len(observed)),
            [(len(part), members, nobs)] * 2
            + [(members, (batches - part[-1] - 1) * nobs)] * (part[-1] + 1 < batches),
            "chain",
            (*observed, obs_value, obs_error, obs_taper),
        )
        pairs += outs[:2]
        observed = outs[2:]
    (cells,) = call(
        forecast_kernel(cols_dev, count, blocks, bands),
        [(members * comps, cols_dev)],
        "forecast",
        (*grid, *near, far[0], courant_x, courant_y, diffusion),
    )
    (out,) = call(
        update_kernel(comps, batches, members, cols_dev, count, bands, comps),
        [(members * comps, cols_dev)],
        "update",
        (cells, far[1], courant_y, diffusion, cell_taper, *pairs),
        (pltpu.VMEM((members * comps, cols_dev), f32),),
    )
    return out.reshape(members, rows_dev, comps, cols_dev)


def solution(mesh):
    return jax.shard_map(
        shards,
        mesh=mesh,
        in_specs=(
            P("mem", "sub", None, None),
            P("sub", None),
            P("sub", None),
            P("sub", None),
            P(),
            P(),
            P(),
            P(),
            P(),
        ),
        out_specs=P(None, "sub", None, "mem"),
        check_vma=False,
    )
```

```python
import jax
import jax.numpy as jnp
from jax import lax
from jax.experimental import pallas as pl
from jax.experimental.pallas import tpu as pltpu
from jax.sharding import PartitionSpec as P

highest = lax.Precision.HIGHEST
f32 = jnp.float32
bf16 = jnp.bfloat16
TILE = (8, 128)


def dot(a, b, ca, cb, precision=highest):
    return lax.dot_general(
        a, b, (((ca,), (cb,)), ((), ())), precision=precision, preferred_element_type=f32
    )


def narrow(a, b, ca, cb):
    return dot(a, b, ca, cb, None)


def split2(x):
    hi = x.astype(bf16)
    return hi, (x - hi.astype(f32)).astype(bf16)


def split3(x):
    hi = x.astype(bf16)
    rest = x - hi.astype(f32)
    mid = rest.astype(bf16)
    return hi, mid, (rest - mid.astype(f32)).astype(bf16)


def call(kernel, out_shapes, name, operands, scratch=(), space=pltpu.VMEM):
    specs = [pl.BlockSpec(memory_space=space) for _ in operands]
    return pl.pallas_call(
        kernel,
        in_specs=specs,
        out_specs=[pl.BlockSpec(memory_space=pltpu.VMEM) for _ in out_shapes],
        out_shape=[jax.ShapeDtypeStruct(s, f32) for s in out_shapes],
        scratch_shapes=list(scratch),
        compiler_params=pltpu.CompilerParams(vmem_limit_bytes=48 * 2**20),
        name=name,
    )(*operands)


def rows_cols(cells, width):
    if width & (width - 1) == 0:
        shift = width.bit_length() - 1
        return cells >> shift, cells & (width - 1)
    return cells // width, cells % width


def to_columns(rows):
    n = rows.shape[0]
    return jnp.concatenate([rows, jnp.zeros((128 - n, 128), f32)], 0).T


def gaspari(delta_row, delta_col, cutoff_radius, width):
    half = width // 2
    folded = jnp.where(delta_col >= half, delta_col - width, delta_col)
    folded = jnp.where(delta_col < -half, delta_col + width, folded)
    ratio = jnp.sqrt(delta_row * delta_row + folded * folded) / cutoff_radius
    inner = (((-0.25 * ratio + 0.5) * ratio + 0.625) * ratio - 5.0 / 3.0) * ratio * ratio + 1.0
    bounded = jnp.maximum(ratio, 1.0)
    outer = (
        ((((ratio / 12.0 - 0.5) * ratio + 0.625) * ratio + 5.0 / 3.0) * ratio - 5.0) * ratio
        + 4.0
        - 2.0 / (3.0 * bounded)
    )
    return jnp.where(ratio <= 1.0, inner, jnp.where(ratio < 2.0, outer, 0.0))


def taper_kernel(width, batches, nobs, cols_dev):
    def kernel(cell_ref, radius_ref, obs_taper_ref, cell_taper_ref):
        row_here = lax.axis_index("sub").astype(f32)
        col_here = lax.axis_index("mem") * cols_dev
        row_i, col_i = rows_cols(cell_ref[...], width)
        rows = row_i.astype(f32)
        cols = col_i.astype(f32)
        table = to_columns(jnp.concatenate([rows, cols, radius_ref[...]], 0))
        lane = lax.broadcasted_iota(jnp.int32, (1, cols_dev), 1)
        cell_cols = (lane + col_here).astype(f32)
        slot = 0
        for b in range(batches):
            row_j = table[:, b : b + 1]
            col_j = table[:, batches + b : batches + b + 1]
            radius = table[:, 2 * batches + b : 2 * batches + b + 1]
            cell_taper_ref[b] = gaspari(row_here - row_j, cell_cols - col_j, radius, width)
            for e in range(b + 1, batches):
                obs_taper_ref[slot] = gaspari(
                    rows[e : e + 1, :] - row_j, cols[e : e + 1, :] - col_j, radius, width
                )
                slot += 1

    return kernel


def share_kernel(width, comps, batches, nobs, local):
    def kernel(*refs):
        sources, (share_ref, *fetched, arrived) = refs[:6], refs[6:]
        q_ref, cx_ref, cy_ref, d_ref, cell_ref, weight_ref = fetched
        copies = [
            pltpu.make_async_copy(source, target, arrived.at[i])
            for i, (source, target) in enumerate(zip(sources, fetched))
        ]
        for copy in copies:
            copy.start()
        here = lax.axis_index("sub")
        for copy in copies[1:]:
            copy.wait()
        cx, cy, d = cx_ref[...], cy_ref[...], d_ref[...]
        from_south, from_north = jnp.maximum(cy, 0.0) + d, d - jnp.minimum(cy, 0.0)
        even = jnp.full((1, width), here & 1, jnp.int32) == 0
        near = jnp.where(even, from_north, from_south)
        far = jnp.where(even, from_south, from_north)
        scales = [part.astype(f32) for part in split3(jnp.concatenate([near, far], 0))]
        scales = jnp.concatenate(scales + [jnp.zeros((10, width), f32)], 0).astype(bf16)
        row, col = rows_cols(cell_ref[...], width)
        row = jnp.concatenate([row[b : b + 1] for b in range(batches)], 1)
        col = jnp.concatenate([col[b : b + 1] for b in range(batches)], 1)
        away = row - here
        owned, beside = away == 0, (away == 1) | (away == -1)
        place = lax.broadcasted_iota(jnp.int32, (width, batches * nobs), 0)
        own_pick = (place == jnp.where(owned, col, -1)).astype(f32).astype(bf16)
        raw_pick = (place == jnp.where(beside, col, -1)).astype(f32).astype(bf16)
        copies[0].wait()
        q = q_ref[...]
        west = pltpu.roll(q, 1, 1)
        east = pltpu.roll(q, width - 1, 1)
        mine = q - jnp.maximum(cx, 0.0) * (q - west) - jnp.minimum(cx, 0.0) * (east - q)
        mine = mine - jnp.maximum(cy, 0.0) * q + jnp.minimum(cy, 0.0) * q
        mine = mine + d * (east + west - 4.0 * q)
        value = narrow(
            jnp.concatenate(split2(mine) + split2(q), 1),
            jnp.concatenate([own_pick, own_pick, raw_pick, raw_pick], 0),
            1,
            0,
        )
        weight = jnp.concatenate([weight_ref[b] for b in range(batches)], 1)
        value = jnp.sum(value.reshape(-1, comps, batches * nobs) * weight[None], axis=1)
        scale = narrow(scales, own_pick, 1, 0)
        scale = scale[0:2] + scale[2:4] + scale[4:6]
        share = [value, jnp.where(owned, scale, 1.0)]
        fill = share_ref.shape[0] - local - 2
        if fill:
            share.append(jnp.zeros((fill, batches * nobs), f32))
        share_ref[...] = jnp.concatenate(share, 0)

    return kernel


def send_kernel(width, blocks, edge_rows):
    def kernel(q_ref, *send_refs):
        here = lax.axis_index("mem")
        q = q_ref[...]
        count = q.shape[0]
        q_parts = split3(q)
        cols_dev = width // blocks
        lanes = -(-2 * blocks // 128) * 128
        which = lax.broadcasted_iota(jnp.int32, (width, lanes), 1)
        spot = lax.broadcasted_iota(jnp.int32, (width, lanes), 0)
        start = ((which >> 1) ^ here) * cols_dev
        wanted = jnp.where(which & 1 == 0, start - 1, start + cols_dev)
        wanted = jnp.where(wanted < 0, wanted + width, wanted)
        wanted = jnp.where(wanted == width, 0, wanted)
        pick = (spot == wanted).astype(f32).astype(bf16)
        edges = narrow(
            jnp.concatenate(q_parts, 1), jnp.concatenate([pick, pick, pick], 0), 1, 0
        )
        room = -count % 128
        if room:
            edges = jnp.concatenate([edges, jnp.zeros((room, lanes), f32)], 0)
        edges = edges.T
        chunks = -(-count // 128)
        for i, send_ref in enumerate(send_refs):
            first = pl.multiple_of((here ^ i) * cols_dev, cols_dev)
            send_ref[:count, :] = q_ref[:, pl.ds(first, cols_dev)]
            rows = [edges[2 * i : 2 * i + 2, j * 128 : (j + 1) * 128] for j in range(chunks)]
            if edge_rows > 2 * chunks:
                rows.append(jnp.zeros((edge_rows - 2 * chunks, 128), f32))
            send_ref[count:, :] = jnp.concatenate(rows, 0)

    return kernel


def join_kernel(local, first, last):
    def kernel(mine_ref, other_ref, out_ref):
        mine, other = mine_ref[...], other_ref[...]
        at = local
        value = mine[:local] * other[at : at + 1] + other[:local] * mine[at : at + 1]
        if last:
            out_ref[...] = value
        else:
            at = local + 1 if first else local
            scale = mine[at : at + 1] * other[at : at + 1]
            blank = jnp.zeros((out_ref.shape[0] - local - 1, value.shape[1]), f32)
            out_ref[...] = jnp.concatenate([value, scale, blank], 0)

    return kernel


def lane_spread(x, j):
    return jnp.take_along_axis(x, jnp.full(x.shape, j, jnp.int32), axis=1)


def row_spread(x, i):
    return jnp.broadcast_to(x[i : i + 1, :], x.shape)


def factored(cov, sides, error, members, span=4):
    tiles = cov.shape[0] // 8
    lane = lax.broadcasted_iota(jnp.int32, TILE, 1)
    sub = lax.broadcasted_iota(jnp.int32, TILE, 0)
    T = [cov[8 * q : 8 * q + 8, :] for q in range(tiles)]
    V = [sides[8 * q : 8 * q + 8, :] for q in range(tiles)]
    deviation = jnp.broadcast_to(jnp.sqrt(error), TILE)
    is_member = lane < members
    inverse, solved, finished = [], [], []
    for p in range(tiles):
        block = (lane >= 8 * p) & (lane < 8 * p + 8)
        columns = [lane_spread(T[p], 8 * p + c) for c in range(8)]
        s = [[row_spread(columns[c], a) if a >= c else None for c in range(8)] for a in range(8)]
        joined = jnp.where(block, (lane - 8 * p == sub).astype(f32), T[p])
        R = [row_spread(joined, c) for c in range(8)]
        Z = [row_spread(V[p], c) for c in range(8)]
        rd, rs = [None] * 8, [None] * 8
        m = [[None] * 8 for _ in range(8)]
        for c in range(8):
            rd[c] = 1.0 / s[c][c]
            rs[c] = lax.rsqrt(s[c][c])
            root = s[c][c] * rs[c]
            spread = lane_spread(deviation, 8 * p + c)
            Z[c] = Z[c] * jnp.where(is_member, root / (root + spread), 1.0)
            for a in range(c + 1, 8):
                m[a][c] = s[a][c] * rd[c]
            for a in range(c + 1, 8):
                for e in range(c + 1, a + 1):
                    s[a][e] = s[a][e] - (s[a][c] * s[e][c]) * rd[c]
                R[a] = R[a] - m[a][c] * R[c]
                Z[a] = Z[a] - m[a][c] * Z[c]
        X, U = [None] * 8, [None] * 8
        for a in range(7, -1, -1):
            x, u = rd[a] * R[a], rd[a] * Z[a]
            for c in range(a + 1, 8):
                x = x - m[c][a] * X[c]
                u = u - m[c][a] * U[c]
            X[a], U[a] = x, u
        low, side = R[0] * rs[0], Z[0] * rs[0]
        for c in range(1, 8):
            low = jnp.where(sub == c, R[c] * rs[c], low)
            side = jnp.where(sub == c, Z[c] * rs[c], side)
        inverse.append(jnp.where(lane < 8 * p + 8, low, 0.0))
        solved.append(side)
        finished.append((low, side))
        edge = (p // span + 1) * span
        for q in range(p + 1, edge):
            column = [lane_spread(T[q], 8 * p + c) for c in range(8)]
            left, right = X, U
            if q == p + 1:
                for c in range(8):
                    for a in range(c):
                        column[c] = column[c] - m[c][a] * column[a]
                column = [column[c] * rd[c] for c in range(8)]
                left, right = R, Z
            t, v = jnp.where(block, 0.0, T[q]), V[q]
            for c in range(8):
                t = t - column[c] * left[c]
                v = v - column[c] * right[c]
            T[q], V[q] = t, v
        if p + 1 == edge and edge < tiles:
            rows = finished[edge - span : edge]
            upper = jnp.concatenate([low for low, _ in rows], 0)
            keep = [
                jnp.where((lane < 8 * (edge - span + i + 1)) | (lane >= 8 * edge), low, 0.0)
                for i, (low, _) in enumerate(rows)
            ]
            side_rows = jnp.concatenate([side for _, side in rows], 0)
            taken = products(upper, jnp.concatenate([jnp.concatenate(keep, 0), side_rows], 1))
            inside = (lane >= 8 * (edge - span)) & (lane < 8 * edge)
            for q in range(edge, tiles):
                at = slice(8 * q, 8 * q + 8)
                T[q] = jnp.where(inside, 0.0, T[q]) - taken[at, :128]
                V[q] = V[q] - taken[at, 128:]
    return jnp.concatenate(inverse, 0), jnp.concatenate(solved, 0)


def products(a, b):
    ah, am, al = split3(a)
    bh, bm, bl = split3(b)
    return narrow(
        jnp.concatenate([al, am, ah, am, ah, ah], 0),
        jnp.concatenate([bh, bm, bl, bh, bm, bh], 0),
        0,
        0,
    )


def coefficients(observed, value, error):
    members, nobs = observed.shape
    mean = jnp.sum(observed, axis=0, keepdims=True) / members
    anomaly = observed - mean
    row = lax.broadcasted_iota(jnp.int32, (nobs, nobs), 0)
    col = lax.broadcasted_iota(jnp.int32, (nobs, nobs), 1)
    cov = products(anomaly, anomaly) / (members - 1) + jnp.where(row == col, error, 0.0)
    sides = jnp.concatenate(
        [anomaly, value - mean, jnp.zeros((nobs - members - 1, nobs), f32)], 0
    ).T
    inverse, solved = factored(cov, sides, error, members)
    back = products(solved, inverse)
    return anomaly, back[members : members + 1] - back[:members]


def chain_kernel(part, batches, nobs, pieces):
    def kernel(*refs):
        y_refs, refs = refs[:pieces], refs[pieces:]
        value_ref, error_ref, taper_ref, anomaly_ref, coeff_ref, *later_ref = refs
        blocks = [ref[...] for ref in y_refs]
        step = 1
        while step < pieces:
            odd = jnp.full(blocks[0].shape, lax.axis_index("mem") & step, jnp.int32) != 0
            blocks = [jnp.where(odd, blocks[k ^ step], blocks[k]) for k in range(pieces)]
            step *= 2
        observed = jnp.concatenate(blocks, 0) if pieces > 1 else blocks[0]
        members = observed.shape[0]
        first = batches - observed.shape[1] // nobs
        Y = {b: observed[:, nobs * (b - first) : nobs * (b - first + 1)] for b in range(first, batches)}
        for b in part:
            anomaly, coeff = coefficients(Y[b], value_ref[b : b + 1, :], error_ref[b : b + 1, :])
            anomaly_ref[b - first] = anomaly
            coeff_ref[b - first] = coeff
            after = range(b + 1, batches)
            if after:
                slot = b * batches - b * (b + 1) // 2
                later = jnp.concatenate([Y[e] for e in after], 1)
                spread = later - jnp.sum(later, axis=0, keepdims=True) / members
                taper = jnp.concatenate([taper_ref[slot + i] for i in range(len(after))], 1)
                hi, lo = split2(anomaly)
                fill = -3 * members % 128
                left = jnp.concatenate([hi, lo, hi, jnp.zeros((fill, nobs), bf16)], 0)
                hi, lo = split2(spread)
                blank = jnp.zeros((fill, later.shape[1]), bf16)
                gain = narrow(left, jnp.concatenate([hi, hi, lo, blank], 0), 0, 0)
                gain = gain / (members - 1) * taper
                coeff_hi, coeff_lo = split2(coeff)
                hi, lo = split2(gain)
                left = jnp.concatenate([coeff_hi, coeff_hi, coeff_lo], 1)
                later = later + narrow(left, jnp.concatenate([hi, lo, hi], 0), 1, 0)
                for i, e in enumerate(after):
                    Y[e] = later[:, nobs * i : nobs * (i + 1)]
        for e in range(part[-1] + 1, batches):
            at = e - part[-1] - 1
            later_ref[0][:, nobs * at : nobs * (at + 1)] = Y[e]

    return kernel


def halo_scales(cy, bands):
    band = jnp.full(cy.shape, lax.axis_index("sub"), jnp.int32)
    even = band & 1 == 0
    from_south, from_north = jnp.maximum(cy, 0.0), -jnp.minimum(cy, 0.0)
    from_near = jnp.where(even, from_north, from_south)
    from_far = jnp.where(even, from_south, from_north)
    return from_near, from_far, (band == 0) | (band == bands - 1)


def forecast_kernel(cols_dev, count, blocks, bands):
    def kernel(*refs):
        own_refs, halos, refs = refs[:blocks], refs[blocks : blocks + 3], refs[blocks + 3 :]
        near_refs = [ref.at[i] for ref in halos[:2] for i in range(ref.shape[0])]
        far_refs = [halos[2].at[i] for i in range(halos[2].shape[0])]
        cx_ref, cy_ref, d_ref, grid_ref = refs
        start = pl.multiple_of(lax.axis_index("mem") * cols_dev, cols_dev)
        cx = cx_ref[:, pl.ds(start, cols_dev)]
        cy = cy_ref[:, pl.ds(start, cols_dev)]
        d = d_ref[:, pl.ds(start, cols_dev)]
        lane = lax.broadcasted_iota(jnp.int32, (1, cols_dev), 1)
        from_near, from_far, outermost = halo_scales(cy, bands)
        from_west, from_east = jnp.maximum(cx, 0.0), -jnp.minimum(cx, 0.0)
        for s, (own_ref, near_ref) in enumerate(zip(own_refs, near_refs)):
            base = pl.multiple_of((lax.axis_index("mem") ^ s) * count, 8)
            outer = to_columns(own_ref[count:, :])
            for j in range(-(-count // 128)):
                size = min(128, count - 128 * j)
                at = slice(128 * j, 128 * j + size)
                q, near = own_ref[at, :], near_ref[at, :]
                west = jnp.where(lane == 0, outer[:size, 2 * j : 2 * j + 1], pltpu.roll(q, 1, 1))
                east = jnp.where(
                    lane == cols_dev - 1,
                    outer[:size, 2 * j + 1 : 2 * j + 2],
                    pltpu.roll(q, cols_dev - 1, 1),
                )
                x = q - from_west * (q - west) - from_east * (q - east)
                if s < len(far_refs):
                    far = jnp.where(outermost, 0.0, far_refs[s][at, :])
                    x = x - from_near * (q - near) - from_far * (q - far)
                    x = x + d * (east + west + near + far - 4.0 * q)
                else:
                    x = x - from_near * (q - near) - from_far * q
                    x = x + d * (east + west + near - 4.0 * q)
                grid_ref[pl.ds(base + 128 * j, size), :] = x

    return kernel


def update_kernel(comps, batches, members, cols_dev, count, bands, group):
    def kernel(cells_ref, far_ref, cy_ref, d_ref, taper_ref, *refs):
        *pair_refs, out_ref, grid_ref = refs
        pairs = [
            (pair_refs[i][k], pair_refs[i + 1][k])
            for i in range(0, len(pair_refs), 2)
            for k in range(pair_refs[i].shape[0])
        ]
        start = pl.multiple_of(lax.axis_index("mem") * cols_dev, cols_dev)
        _, from_far, outermost = halo_scales(cy_ref[:, pl.ds(start, cols_dev)], bands)
        scale = jnp.where(outermost, 0.0, from_far + d_ref[:, pl.ds(start, cols_dev)])
        late = far_ref.shape[0]
        for s in range(2 * late):
            at = pl.ds(pl.multiple_of((lax.axis_index("mem") ^ s) * count, 8), count)
            cells = cells_ref[at, :]
            grid_ref[at, :] = cells if s < late else cells + scale * far_ref[s - late, :count, :]
        left, right, tapers = [], [], []
        nobs = taper_ref.shape[1]
        fill = -3 * members % 128
        blank = jnp.zeros((fill, group * cols_dev), bf16)
        for b in range(batches):
            hi, lo = split2(pairs[b][0])
            left.append(jnp.concatenate([hi, lo, hi, jnp.zeros((fill, nobs), bf16)], 0))
            hi, lo = split2(pairs[b][1])
            right.append(jnp.concatenate([hi, hi, lo], 1))
            tapers.append(jnp.tile(taper_ref[b] / (members - 1), (1, group)))
        for first in range(0, comps, group):
            x = jnp.concatenate(
                [grid_ref[pl.ds(first + i, members, comps), :] for i in range(group)], 1
            )
            for b in range(batches):
                spread = x - jnp.sum(x, axis=0, keepdims=True) / members
                hi, lo = split2(spread)
                gain = narrow(left[b], jnp.concatenate([hi, hi, lo, blank], 0), 0, 0) * tapers[b]
                hi, lo = split2(gain)
                x = x + narrow(right[b], jnp.concatenate([hi, lo, hi], 0), 1, 0)
            for i in range(group):
                out_ref[pl.ds(first + i, members, comps), :] = x[:, i * cols_dev : (i + 1) * cols_dev]

    return kernel


def shards(
    prior_sample_array,
    courant_x,
    courant_y,
    diffusion,
    obs_cell,
    obs_value,
    obs_error,
    obs_weight,
    taper_radius,
):
    local, rows_dev, comps, width = prior_sample_array.shape
    blocks = lax.axis_size("mem")
    bands = lax.axis_size("sub")
    cols_dev = width // blocks
    members = local * blocks
    batches, nobs = obs_cell.shape
    count = local * comps
    edge_rows = -(-(2 * -(-count // 128)) // 8) * 8
    assert bands & (bands - 1) == 0 and bands > 2 and blocks & (blocks - 1) == 0 and rows_dev == 1 and batches == 4 and cols_dev == 128 and nobs == 128

    share_rows = -(-(local + 2) // 8) * 8
    prior = prior_sample_array.reshape(count, width)
    sends = call(
        send_kernel(width, blocks, edge_rows),
        [(count + edge_rows, cols_dev)] * blocks,
        "send",
        (prior,),
    )
    grid = [sends[0]] + [
        lax.ppermute(sends[k], "mem", [(i, i ^ k) for i in range(blocks)]) for k in range(1, blocks)
    ]
    held_x, *sends = lax.optimization_barrier((courant_x, *sends))
    sources = (prior, held_x, courant_y, diffusion, obs_cell, obs_weight.transpose(0, 2, 1))
    (share,) = call(
        share_kernel(width, comps, batches, nobs, local),
        [(share_rows, batches * nobs)],
        "share",
        sources,
        [pltpu.VMEM(x.shape, x.dtype) for x in sources] + [pltpu.SemaphoreType.DMA((6,))],
        pl.ANY,
    )
    obs_taper, cell_taper = call(
        taper_kernel(width, batches, nobs, cols_dev),
        [(batches * (batches - 1) // 2, nobs, nobs), (batches, nobs, cols_dev)],
        "tapers",
        (obs_cell, taper_radius),
    )
    swap = [(i, i ^ 1) for i in range(bands)]
    onward = [(i, i + 2) for i in range(0, bands - 2, 2)] + [(i, i - 2) for i in range(3, bands, 2)]
    across = onward + [(1, 0), (bands - 2, bands - 1)]
    middle = blocks // 2
    parts = (slice(0, middle), slice(middle, blocks))
    near, far = [], []
    step = 1
    while step < bands:
        other = lax.ppermute(share, "sub", [(i, i ^ step) for i in range(bands)])
        if step == 1:
            other, obs_taper, cell_taper = lax.optimization_barrier((other, obs_taper, cell_taper))
        last = 2 * step == bands
        (share,) = call(
            join_kernel(local, step == 1, last),
            [(local if last else share_rows, batches * nobs)],
            "join",
            (share, other),
        )
        if step in (1, 2):
            part = parts[step // 2]
            share, *grid[part] = lax.optimization_barrier((share, *grid[part]))
            near.append(lax.ppermute(jnp.stack(grid[part]), "sub", swap))
        step *= 2
    observed = {0: share}
    step = blocks // 2
    while step:
        to = [(i, i ^ step) for i in range(blocks)]
        observed.update({k ^ step: lax.ppermute(x, "mem", to) for k, x in observed.items()})
        step //= 2
    observed = [observed[k] for k in range(blocks)]
    pairs = []
    for b in range(batches):
        part = range(b, b + 1)
        if b < 2:
            *observed, near[b] = lax.optimization_barrier((*observed, near[b]))
            far.append(lax.ppermute(near[b], "sub", (onward, across)[b]))
        if b == 3:
            *observed, far[0] = lax.optimization_barrier((*observed, far[0]))
        outs = call(
            chain_kernel(part, batches, nobs, len(observed)),
            [(len(part), members, nobs)] * 2
            + [(members, (batches - part[-1] - 1) * nobs)] * (part[-1] + 1 < batches),
            "chain",
            (*observed, obs_value, obs_error, obs_taper),
        )
        pairs += outs[:2]
        observed = outs[2:]
    (cells,) = call(
        forecast_kernel(cols_dev, count, blocks, bands),
        [(members * comps, cols_dev)],
        "forecast",
        (*grid, *near, far[0], courant_x, courant_y, diffusion),
    )
    (out,) = call(
        update_kernel(comps, batches, members, cols_dev, count, bands, comps),
        [(members * comps, cols_dev)],
        "update",
        (cells, far[1], courant_y, diffusion, cell_taper, *pairs),
        (pltpu.VMEM((members * comps, cols_dev), f32),),
    )
    return out.reshape(members, rows_dev, comps, cols_dev)


def solution(mesh):
    return jax.shard_map(
        shards,
        mesh=mesh,
        in_specs=(
            P("mem", "sub", None, None),
            P("sub", None),
            P("sub", None),
            P("sub", None),
            P(),
            P(),
            P(),
            P(),
            P(),
        ),
        out_specs=P(None, "sub", None, "mem"),
        check_vma=False,
    )
```

```python
import jax
import jax.numpy as jnp
from jax import lax
from jax.experimental import pallas as pl
from jax.experimental.pallas import tpu as pltpu
from jax.sharding import PartitionSpec as P

highest = lax.Precision.HIGHEST
f32 = jnp.float32
bf16 = jnp.bfloat16
TILE = (8, 128)


def dot(a, b, ca, cb, precision=highest):
    return lax.dot_general(
        a, b, (((ca,), (cb,)), ((), ())), precision=precision, preferred_element_type=f32
    )


def narrow(a, b, ca, cb):
    return dot(a, b, ca, cb, None)


def split2(x):
    hi = x.astype(bf16)
    return hi, (x - hi.astype(f32)).astype(bf16)


def split3(x):
    hi = x.astype(bf16)
    rest = x - hi.astype(f32)
    mid = rest.astype(bf16)
    return hi, mid, (rest - mid.astype(f32)).astype(bf16)


def call(kernel, out_shapes, name, operands, scratch=(), space=pltpu.VMEM):
    specs = [pl.BlockSpec(memory_space=space) for _ in operands]
    return pl.pallas_call(
        kernel,
        in_specs=specs,
        out_specs=[pl.BlockSpec(memory_space=pltpu.VMEM) for _ in out_shapes],
        out_shape=[jax.ShapeDtypeStruct(s, f32) for s in out_shapes],
        scratch_shapes=list(scratch),
        compiler_params=pltpu.CompilerParams(vmem_limit_bytes=48 * 2**20),
        name=name,
    )(*operands)


def rows_cols(cells, width):
    if width & (width - 1) == 0:
        shift = width.bit_length() - 1
        return cells >> shift, cells & (width - 1)
    return cells // width, cells % width


def to_columns(rows):
    n = rows.shape[0]
    return jnp.concatenate([rows, jnp.zeros((128 - n, 128), f32)], 0).T


def gaspari(delta_row, delta_col, cutoff_radius, width):
    half = width // 2
    folded = jnp.where(delta_col >= half, delta_col - width, delta_col)
    folded = jnp.where(delta_col < -half, delta_col + width, folded)
    ratio = jnp.sqrt(delta_row * delta_row + folded * folded) / cutoff_radius
    inner = (((-0.25 * ratio + 0.5) * ratio + 0.625) * ratio - 5.0 / 3.0) * ratio * ratio + 1.0
    bounded = jnp.maximum(ratio, 1.0)
    outer = (
        ((((ratio / 12.0 - 0.5) * ratio + 0.625) * ratio + 5.0 / 3.0) * ratio - 5.0) * ratio
        + 4.0
        - 2.0 / (3.0 * bounded)
    )
    return jnp.where(ratio <= 1.0, inner, jnp.where(ratio < 2.0, outer, 0.0))


def taper_kernel(width, batches, nobs, cols_dev):
    def kernel(cell_ref, radius_ref, obs_taper_ref, cell_taper_ref):
        row_here = lax.axis_index("sub").astype(f32)
        col_here = lax.axis_index("mem") * cols_dev
        row_i, col_i = rows_cols(cell_ref[...], width)
        rows = row_i.astype(f32)
        cols = col_i.astype(f32)
        table = to_columns(jnp.concatenate([rows, cols, radius_ref[...]], 0))
        lane = lax.broadcasted_iota(jnp.int32, (1, cols_dev), 1)
        cell_cols = (lane + col_here).astype(f32)
        slot = 0
        for b in range(batches):
            row_j = table[:, b : b + 1]
            col_j = table[:, batches + b : batches + b + 1]
            radius = table[:, 2 * batches + b : 2 * batches + b + 1]
            cell_taper_ref[b] = gaspari(row_here - row_j, cell_cols - col_j, radius, width)
            for e in range(b + 1, batches):
                obs_taper_ref[slot] = gaspari(
                    rows[e : e + 1, :] - row_j, cols[e : e + 1, :] - col_j, radius, width
                )
                slot += 1

    return kernel


def share_kernel(width, comps, batches, nobs, local):
    def kernel(*refs):
        sources, (share_ref, *fetched, arrived) = refs[:6], refs[6:]
        q_ref, cx_ref, cy_ref, d_ref, cell_ref, weight_ref = fetched
        copies = [
            pltpu.make_async_copy(source, target, arrived.at[i])
            for i, (source, target) in enumerate(zip(sources, fetched))
        ]
        for copy in copies:
            copy.start()
        here = lax.axis_index("sub")
        for copy in copies[1:]:
            copy.wait()
        cx, cy, d = cx_ref[...], cy_ref[...], d_ref[...]
        from_south, from_north = jnp.maximum(cy, 0.0) + d, d - jnp.minimum(cy, 0.0)
        even = jnp.full((1, width), here & 1, jnp.int32) == 0
        near = jnp.where(even, from_north, from_south)
        far = jnp.where(even, from_south, from_north)
        scales = [part.astype(f32) for part in split3(jnp.concatenate([near, far], 0))]
        scales = jnp.concatenate(scales + [jnp.zeros((10, width), f32)], 0).astype(bf16)
        row, col = rows_cols(cell_ref[...], width)
        row = jnp.concatenate([row[b : b + 1] for b in range(batches)], 1)
        col = jnp.concatenate([col[b : b + 1] for b in range(batches)], 1)
        away = row - here
        owned, beside = away == 0, (away == 1) | (away == -1)
        place = lax.broadcasted_iota(jnp.int32, (width, batches * nobs), 0)
        own_pick = (place == jnp.where(owned, col, -1)).astype(f32).astype(bf16)
        raw_pick = (place == jnp.where(beside, col, -1)).astype(f32).astype(bf16)
        copies[0].wait()
        q = q_ref[...]
        west = pltpu.roll(q, 1, 1)
        east = pltpu.roll(q, width - 1, 1)
        mine = q - jnp.maximum(cx, 0.0) * (q - west) - jnp.minimum(cx, 0.0) * (east - q)
        mine = mine - jnp.maximum(cy, 0.0) * q + jnp.minimum(cy, 0.0) * q
        mine = mine + d * (east + west - 4.0 * q)
        value = narrow(
            jnp.concatenate(split2(mine) + split2(q), 1),
            jnp.concatenate([own_pick, own_pick, raw_pick, raw_pick], 0),
            1,
            0,
        )
        weight = jnp.concatenate([weight_ref[b] for b in range(batches)], 1)
        value = jnp.sum(value.reshape(-1, comps, batches * nobs) * weight[None], axis=1)
        scale = narrow(scales, own_pick, 1, 0)
        scale = scale[0:2] + scale[2:4] + scale[4:6]
        share = [value, jnp.where(owned, scale, 1.0)]
        fill = share_ref.shape[0] - local - 2
        if fill:
            share.append(jnp.zeros((fill, batches * nobs), f32))
        share_ref[...] = jnp.concatenate(share, 0)

    return kernel


def send_kernel(width, blocks, edge_rows):
    def kernel(q_ref, *send_refs):
        here = lax.axis_index("mem")
        q = q_ref[...]
        count = q.shape[0]
        q_parts = split3(q)
        cols_dev = width // blocks
        lanes = -(-2 * blocks // 128) * 128
        which = lax.broadcasted_iota(jnp.int32, (width, lanes), 1)
        spot = lax.broadcasted_iota(jnp.int32, (width, lanes), 0)
        start = ((which >> 1) ^ here) * cols_dev
        wanted = jnp.where(which & 1 == 0, start - 1, start + cols_dev)
        wanted = jnp.where(wanted < 0, wanted + width, wanted)
        wanted = jnp.where(wanted == width, 0, wanted)
        pick = (spot == wanted).astype(f32).astype(bf16)
        edges = narrow(
            jnp.concatenate(q_parts, 1), jnp.concatenate([pick, pick, pick], 0), 1, 0
        )
        room = -count % 128
        if room:
            edges = jnp.concatenate([edges, jnp.zeros((room, lanes), f32)], 0)
        edges = edges.T
        chunks = -(-count // 128)
        for i, send_ref in enumerate(send_refs):
            first = pl.multiple_of((here ^ i) * cols_dev, cols_dev)
            send_ref[:count, :] = q_ref[:, pl.ds(first, cols_dev)]
            rows = [edges[2 * i : 2 * i + 2, j * 128 : (j + 1) * 128] for j in range(chunks)]
            if edge_rows > 2 * chunks:
                rows.append(jnp.zeros((edge_rows - 2 * chunks, 128), f32))
            send_ref[count:, :] = jnp.concatenate(rows, 0)

    return kernel


def join_kernel(local, first, last):
    def kernel(mine_ref, other_ref, out_ref):
        mine, other = mine_ref[...], other_ref[...]
        at = local
        value = mine[:local] * other[at : at + 1] + other[:local] * mine[at : at + 1]
        if last:
            out_ref[...] = value
        else:
            at = local + 1 if first else local
            scale = mine[at : at + 1] * other[at : at + 1]
            blank = jnp.zeros((out_ref.shape[0] - local - 1, value.shape[1]), f32)
            out_ref[...] = jnp.concatenate([value, scale, blank], 0)

    return kernel


def lane_spread(x, j):
    return jnp.take_along_axis(x, jnp.full(x.shape, j, jnp.int32), axis=1)


def row_spread(x, i):
    return jnp.broadcast_to(x[i : i + 1, :], x.shape)


def factored(cov, sides, error, members, span=4):
    tiles = cov.shape[0] // 8
    lane = lax.broadcasted_iota(jnp.int32, TILE, 1)
    sub = lax.broadcasted_iota(jnp.int32, TILE, 0)
    T = [cov[8 * q : 8 * q + 8, :] for q in range(tiles)]
    V = [sides[8 * q : 8 * q + 8, :] for q in range(tiles)]
    deviation = jnp.broadcast_to(jnp.sqrt(error), TILE)
    is_member = lane < members
    inverse, solved, finished = [], [], []
    for p in range(tiles):
        block = (lane >= 8 * p) & (lane < 8 * p + 8)
        columns = [lane_spread(T[p], 8 * p + c) for c in range(8)]
        s = [[row_spread(columns[c], a) if a >= c else None for c in range(8)] for a in range(8)]
        joined = jnp.where(block, (lane - 8 * p == sub).astype(f32), T[p])
        R = [row_spread(joined, c) for c in range(8)]
        Z = [row_spread(V[p], c) for c in range(8)]
        rd, rs = [None] * 8, [None] * 8
        m = [[None] * 8 for _ in range(8)]
        for c in range(8):
            rd[c] = 1.0 / s[c][c]
            rs[c] = lax.rsqrt(s[c][c])
            root = s[c][c] * rs[c]
            spread = lane_spread(deviation, 8 * p + c)
            Z[c] = Z[c] * jnp.where(is_member, root / (root + spread), 1.0)
            for a in range(c + 1, 8):
                m[a][c] = s[a][c] * rd[c]
            for a in range(c + 1, 8):
                for e in range(c + 1, a + 1):
                    s[a][e] = s[a][e] - (s[a][c] * s[e][c]) * rd[c]
                R[a] = R[a] - m[a][c] * R[c]
                Z[a] = Z[a] - m[a][c] * Z[c]
        X, U = [None] * 8, [None] * 8
        for a in range(7, -1, -1):
            x, u = rd[a] * R[a], rd[a] * Z[a]
            for c in range(a + 1, 8):
                x = x - m[c][a] * X[c]
                u = u - m[c][a] * U[c]
            X[a], U[a] = x, u
        low, side = R[0] * rs[0], Z[0] * rs[0]
        for c in range(1, 8):
            low = jnp.where(sub == c, R[c] * rs[c], low)
            side = jnp.where(sub == c, Z[c] * rs[c], side)
        inverse.append(jnp.where(lane < 8 * p + 8, low, 0.0))
        solved.append(side)
        finished.append((low, side))
        edge = (p // span + 1) * span
        for q in range(p + 1, edge):
            column = [lane_spread(T[q], 8 * p + c) for c in range(8)]
            left, right = X, U
            if q == p + 1:
                for c in range(8):
                    for a in range(c):
                        column[c] = column[c] - m[c][a] * column[a]
                column = [column[c] * rd[c] for c in range(8)]
                left, right = R, Z
            t, v = jnp.where(block, 0.0, T[q]), V[q]
            for c in range(8):
                t = t - column[c] * left[c]
                v = v - column[c] * right[c]
            T[q], V[q] = t, v
        if p + 1 == edge and edge < tiles:
            rows = finished[edge - span : edge]
            upper = jnp.concatenate([low for low, _ in rows], 0)
            keep = [
                jnp.where((lane < 8 * (edge - span + i + 1)) | (lane >= 8 * edge), low, 0.0)
                for i, (low, _) in enumerate(rows)
            ]
            side_rows = jnp.concatenate([side for _, side in rows], 0)
            taken = products(upper, jnp.concatenate([jnp.concatenate(keep, 0), side_rows], 1))
            inside = (lane >= 8 * (edge - span)) & (lane < 8 * edge)
            for q in range(edge, tiles):
                at = slice(8 * q, 8 * q + 8)
                T[q] = jnp.where(inside, 0.0, T[q]) - taken[at, :128]
                V[q] = V[q] - taken[at, 128:]
    return jnp.concatenate(inverse, 0), jnp.concatenate(solved, 0)


def products(a, b):
    ah, am, al = split3(a)
    bh, bm, bl = split3(b)
    return narrow(
        jnp.concatenate([al, am, ah, am, ah, ah], 0),
        jnp.concatenate([bh, bm, bl, bh, bm, bh], 0),
        0,
        0,
    )


def coefficients(observed, value, error):
    members, nobs = observed.shape
    mean = jnp.sum(observed, axis=0, keepdims=True) / members
    anomaly = observed - mean
    row = lax.broadcasted_iota(jnp.int32, (nobs, nobs), 0)
    col = lax.broadcasted_iota(jnp.int32, (nobs, nobs), 1)
    cov = products(anomaly, anomaly) / (members - 1) + jnp.where(row == col, error, 0.0)
    sides = jnp.concatenate(
        [anomaly, value - mean, jnp.zeros((nobs - members - 1, nobs), f32)], 0
    ).T
    inverse, solved = factored(cov, sides, error, members)
    back = products(solved, inverse)
    return anomaly, back[members : members + 1] - back[:members]


def chain_kernel(part, batches, nobs, pieces):
    def kernel(*refs):
        y_refs, refs = refs[:pieces], refs[pieces:]
        value_ref, error_ref, taper_ref, anomaly_ref, coeff_ref, *later_ref = refs
        blocks = [ref[...] for ref in y_refs]
        step = 1
        while step < pieces:
            odd = jnp.full(blocks[0].shape, lax.axis_index("mem") & step, jnp.int32) != 0
            blocks = [jnp.where(odd, blocks[k ^ step], blocks[k]) for k in range(pieces)]
            step *= 2
        observed = jnp.concatenate(blocks, 0) if pieces > 1 else blocks[0]
        members = observed.shape[0]
        first = batches - observed.shape[1] // nobs
        Y = {b: observed[:, nobs * (b - first) : nobs * (b - first + 1)] for b in range(first, batches)}
        for b in part:
            anomaly, coeff = coefficients(Y[b], value_ref[b : b + 1, :], error_ref[b : b + 1, :])
            anomaly_ref[b - first] = anomaly
            coeff_ref[b - first] = coeff
            after = range(b + 1, batches)
            if after:
                slot = b * batches - b * (b + 1) // 2
                later = jnp.concatenate([Y[e] for e in after], 1)
                spread = later - jnp.sum(later, axis=0, keepdims=True) / members
                taper = jnp.concatenate([taper_ref[slot + i] for i in range(len(after))], 1)
                hi, lo = split2(anomaly)
                fill = -3 * members % 128
                left = jnp.concatenate([hi, lo, hi, jnp.zeros((fill, nobs), bf16)], 0)
                hi, lo = split2(spread)
                blank = jnp.zeros((fill, later.shape[1]), bf16)
                gain = narrow(left, jnp.concatenate([hi, hi, lo, blank], 0), 0, 0)
                gain = gain / (members - 1) * taper
                coeff_hi, coeff_lo = split2(coeff)
                hi, lo = split2(gain)
                left = jnp.concatenate([coeff_hi, coeff_hi, coeff_lo], 1)
                later = later + narrow(left, jnp.concatenate([hi, lo, hi], 0), 1, 0)
                for i, e in enumerate(after):
                    Y[e] = later[:, nobs * i : nobs * (i + 1)]
        for e in range(part[-1] + 1, batches):
            at = e - part[-1] - 1
            later_ref[0][:, nobs * at : nobs * (at + 1)] = Y[e]

    return kernel


def halo_scales(cy, bands):
    band = jnp.full(cy.shape, lax.axis_index("sub"), jnp.int32)
    even = band & 1 == 0
    from_south, from_north = jnp.maximum(cy, 0.0), -jnp.minimum(cy, 0.0)
    from_near = jnp.where(even, from_north, from_south)
    from_far = jnp.where(even, from_south, from_north)
    return from_near, from_far, (band == 0) | (band == bands - 1)


def forecast_kernel(cols_dev, count, blocks, bands):
    def kernel(*refs):
        own_refs, halos, refs = refs[:blocks], refs[blocks : blocks + 3], refs[blocks + 3 :]
        near_refs = [ref.at[i] for ref in halos[:2] for i in range(ref.shape[0])]
        far_refs = [halos[2].at[i] for i in range(halos[2].shape[0])]
        cx_ref, cy_ref, d_ref, grid_ref = refs
        start = pl.multiple_of(lax.axis_index("mem") * cols_dev, cols_dev)
        cx = cx_ref[:, pl.ds(start, cols_dev)]
        cy = cy_ref[:, pl.ds(start, cols_dev)]
        d = d_ref[:, pl.ds(start, cols_dev)]
        lane = lax.broadcasted_iota(jnp.int32, (1, cols_dev), 1)
        from_near, from_far, outermost = halo_scales(cy, bands)
        from_west, from_east = jnp.maximum(cx, 0.0), -jnp.minimum(cx, 0.0)
        for s, (own_ref, near_ref) in enumerate(zip(own_refs, near_refs)):
            base = pl.multiple_of((lax.axis_index("mem") ^ s) * count, 8)
            outer = to_columns(own_ref[count:, :])
            for j in range(-(-count // 128)):
                size = min(128, count - 128 * j)
                at = slice(128 * j, 128 * j + size)
                q, near = own_ref[at, :], near_ref[at, :]
                west = jnp.where(lane == 0, outer[:size, 2 * j : 2 * j + 1], pltpu.roll(q, 1, 1))
                east = jnp.where(
                    lane == cols_dev - 1,
                    outer[:size, 2 * j + 1 : 2 * j + 2],
                    pltpu.roll(q, cols_dev - 1, 1),
                )
                x = q - from_west * (q - west) - from_east * (q - east)
                if s < len(far_refs):
                    far = jnp.where(outermost, 0.0, far_refs[s][at, :])
                    x = x - from_near * (q - near) - from_far * (q - far)
                    x = x + d * (east + west + near + far - 4.0 * q)
                else:
                    x = x - from_near * (q - near) - from_far * q
                    x = x + d * (east + west + near - 4.0 * q)
                grid_ref[pl.ds(base + 128 * j, size), :] = x

    return kernel


def update_kernel(comps, batches, members, cols_dev, count, bands, group):
    def kernel(cells_ref, far_ref, cy_ref, d_ref, taper_ref, *refs):
        *pair_refs, out_ref, grid_ref = refs
        pairs = [
            (pair_refs[i][k], pair_refs[i + 1][k])
            for i in range(0, len(pair_refs), 2)
            for k in range(pair_refs[i].shape[0])
        ]
        start = pl.multiple_of(lax.axis_index("mem") * cols_dev, cols_dev)
        _, from_far, outermost = halo_scales(cy_ref[:, pl.ds(start, cols_dev)], bands)
        scale = jnp.where(outermost, 0.0, from_far + d_ref[:, pl.ds(start, cols_dev)])
        late = far_ref.shape[0]
        for s in range(2 * late):
            at = pl.ds(pl.multiple_of((lax.axis_index("mem") ^ s) * count, 8), count)
            cells = cells_ref[at, :]
            grid_ref[at, :] = cells if s < late else cells + scale * far_ref[s - late, :count, :]
        left, right, tapers = [], [], []
        nobs = taper_ref.shape[1]
        fill = -3 * members % 128
        blank = jnp.zeros((fill, group * cols_dev), bf16)
        for b in range(batches):
            hi, lo = split2(pairs[b][0])
            left.append(jnp.concatenate([hi, lo, hi, jnp.zeros((fill, nobs), bf16)], 0))
            hi, lo = split2(pairs[b][1])
            right.append(jnp.concatenate([hi, hi, lo], 1))
            tapers.append(jnp.tile(taper_ref[b] / (members - 1), (1, group)))
        for first in range(0, comps, group):
            x = jnp.concatenate(
                [grid_ref[pl.ds(first + i, members, comps), :] for i in range(group)], 1
            )
            for b in range(batches):
                spread = x - jnp.sum(x, axis=0, keepdims=True) / members
                hi, lo = split2(spread)
                gain = narrow(left[b], jnp.concatenate([hi, hi, lo, blank], 0), 0, 0) * tapers[b]
                hi, lo = split2(gain)
                x = x + narrow(right[b], jnp.concatenate([hi, lo, hi], 0), 1, 0)
            for i in range(group):
                out_ref[pl.ds(first + i, members, comps), :] = x[:, i * cols_dev : (i + 1) * cols_dev]

    return kernel


def shards(
    prior_sample_array,
    courant_x,
    courant_y,
    diffusion,
    obs_cell,
    obs_value,
    obs_error,
    obs_weight,
    taper_radius,
):
    local, rows_dev, comps, width = prior_sample_array.shape
    blocks = lax.axis_size("mem")
    bands = lax.axis_size("sub")
    cols_dev = width // blocks
    members = local * blocks
    batches, nobs = obs_cell.shape
    count = local * comps
    edge_rows = -(-(2 * -(-count // 128)) // 8) * 8
    assert bands & (bands - 1) == 0 and bands > 2 and blocks & (blocks - 1) == 0 and rows_dev == 1 and batches == 4 and cols_dev == 128 and nobs == 128

    share_rows = -(-(local + 2) // 8) * 8
    prior = prior_sample_array.reshape(count, width)
    sends = call(
        send_kernel(width, blocks, edge_rows),
        [(count + edge_rows, cols_dev)] * blocks,
        "send",
        (prior,),
    )
    grid = [sends[0]] + [
        lax.ppermute(sends[k], "mem", [(i, i ^ k) for i in range(blocks)]) for k in range(1, blocks)
    ]
    weight, *sends = lax.optimization_barrier((obs_weight, *sends))
    sources = (prior, courant_x, courant_y, diffusion, obs_cell, weight.transpose(0, 2, 1))
    (share,) = call(
        share_kernel(width, comps, batches, nobs, local),
        [(share_rows, batches * nobs)],
        "share",
        sources,
        [pltpu.VMEM(x.shape, x.dtype) for x in sources] + [pltpu.SemaphoreType.DMA((6,))],
        pl.ANY,
    )
    obs_taper, cell_taper = call(
        taper_kernel(width, batches, nobs, cols_dev),
        [(batches * (batches - 1) // 2, nobs, nobs), (batches, nobs, cols_dev)],
        "tapers",
        (obs_cell, taper_radius),
    )
    swap = [(i, i ^ 1) for i in range(bands)]
    onward = [(i, i + 2) for i in range(0, bands - 2, 2)] + [(i, i - 2) for i in range(3, bands, 2)]
    around = onward + [(bands - 2, 0), (1, bands - 1)]
    across = onward + [(1, 0), (bands - 2, bands - 1)]
    middle = blocks // 2
    parts = (slice(0, middle), slice(middle, blocks))
    near, far = [], []
    step = 1
    while step < bands:
        other = lax.ppermute(share, "sub", [(i, i ^ step) for i in range(bands)])
        if step == 1:
            other, obs_taper, cell_taper = lax.optimization_barrier((other, obs_taper, cell_taper))
        last = 2 * step == bands
        (share,) = call(
            join_kernel(local, step == 1, last),
            [(local if last else share_rows, batches * nobs)],
            "join",
            (share, other),
        )
        if step in (1, 2):
            part = parts[step // 2]
            share, *grid[part] = lax.optimization_barrier((share, *grid[part]))
            near.append(lax.ppermute(jnp.stack(grid[part]), "sub", swap))
        step *= 2
    observed = {0: share}
    step = blocks // 2
    while step:
        to = [(i, i ^ step) for i in range(blocks)]
        observed.update({k ^ step: lax.ppermute(x, "mem", to) for k, x in observed.items()})
        step //= 2
    observed = [observed[k] for k in range(blocks)]
    pairs = []
    for b in range(batches):
        part = range(b, b + 1)
        if b < 2:
            *observed, near[b] = lax.optimization_barrier((*observed, near[b]))
            far.append(lax.ppermute(near[b], "sub", (around, across)[b]))
        if b == 3:
            *observed, far[0] = lax.optimization_barrier((*observed, far[0]))
        outs = call(
            chain_kernel(part, batches, nobs, len(observed)),
            [(len(part), members, nobs)] * 2
            + [(members, (batches - part[-1] - 1) * nobs)] * (part[-1] + 1 < batches),
            "chain",
            (*observed, obs_value, obs_error, obs_taper),
        )
        pairs += outs[:2]
        observed = outs[2:]
    (cells,) = call(
        forecast_kernel(cols_dev, count, blocks, bands),
        [(members * comps, cols_dev)],
        "forecast",
        (*grid, *near, far[0], courant_x, courant_y, diffusion),
    )
    (out,) = call(
        update_kernel(comps, batches, members, cols_dev, count, bands, comps),
        [(members * comps, cols_dev)],
        "update",
        (cells, far[1], courant_y, diffusion, cell_taper, *pairs),
        (pltpu.VMEM((members * comps, cols_dev), f32),),
    )
    return out.reshape(members, rows_dev, comps, cols_dev)


def solution(mesh):
    return jax.shard_map(
        shards,
        mesh=mesh,
        in_specs=(
            P("mem", "sub", None, None),
            P("sub", None),
            P("sub", None),
            P("sub", None),
            P(),
            P(),
            P(),
            P(),
            P(),
        ),
        out_specs=P(None, "sub", None, "mem"),
        check_vma=False,
    )
```
